256 devices in a mesh: item: 32 (over x, z), store: 8 (over y, core).
Axes of the slice: x: 4, y: 4, z: 8, core: 2. Of those that a mesh axis runs over, the one named last changes fastest.
Arguments:
- predicted_units: bfloat16 [4096, 8, 4096], P('item', None, 'store'), may hold values from 0.049804688 to 5
- product_group: int32 [4096], P('item'), may hold values from 0 to 63, as said below
- product_goal: float32 [4096], P('item'), may hold values from 9830 to 98304
- group_outlet_goal: float32 [64, 4096], P(None, 'store'), may hold values from 153 to 1536
- outlet_date_goal: float32 [8, 4096], P(None, 'store'), may hold values from 1228 to 12288
Outputs:
- product_factor: float32 [4096], P('item')
- group_outlet_factor: float32 [64, 4096], P(None, 'store')
- outlet_date_factor: float32 [8, 4096], P(None, 'store')
- adjusted_tensor: bfloat16 [4096, 8, 4096], P('item', None, 'store')
The draws below stay inside these ranges and needn't reach their ends.
Inputs may be any that keep to these rules, and one draw needn't show every extreme that they name: `product_group`: category ids never fall along the items, and every category holds at least 32 items; some category holds exactly that many.
All inputs are finite; a program needn't handle non-finite values.
Results may differ from the reference program's by a relative error of at most 0.001.
Values sent between devices are 32-bit elements; how exact they have to be, the bound alone decides.
No kernel may reach another device: no remote copies, remote signals or barrier semaphores. Data moves between devices by JAX's collectives and lax.ppermute only.
A program may use at most 64 MiB of HBM per device.

```python
import math
import jax
import jax.numpy as jnp
from jax import lax

PRODUCTS_EACH = 128
GROUP_KINDS = 64
HORIZON_LENGTH = 8
ROUNDS = 4
INNER = 3
PRODUCT_TALLY = 4096
OUTLET_TALLY = 4096
N_ITEM = 32


def draw_product_group(key, part):
    least = PRODUCT_TALLY // (2 * GROUP_KINDS)
    spare = PRODUCT_TALLY - GROUP_KINDS * least
    first_key, second_key = jax.random.split(jax.random.fold_in(key, 17))
    raw = jax.random.randint(first_key, (GROUP_KINDS,), 0, 4).astype(jnp.int32)
    chosen = jax.random.randint(second_key, (), 0, GROUP_KINDS).astype(jnp.int32)
    labels = jnp.arange(GROUP_KINDS, dtype=jnp.int32)
    raw = jnp.where(labels == chosen, 0, raw)
    raw = raw + (labels == (chosen + 1) % GROUP_KINDS).astype(jnp.int32)
    current_tensor = jnp.cumsum(raw)
    bounds = (labels + 1) * least + current_tensor * spare // current_tensor[-1]
    position = jnp.arange(PRODUCT_TALLY, dtype=jnp.int32)
    return jnp.sum((position[:, None] >= bounds[None, :]).astype(jnp.int32), axis=1)


def block_levels(own_key, extent, cuts, low, high):
    factor_of = 1.0
    for axis_at, shards_of in cuts:
        steps = jax.random.uniform(jax.random.fold_in(jax.random.fold_in(own_key, 6), axis_at), (shards_of,), jnp.float32, low / len(cuts), high / len(cuts))
        factor_of = factor_of * jnp.repeat(jnp.exp(steps), extent[axis_at] // shards_of).reshape((-1,) + (1,) * (len(extent) - 1 - axis_at))
    return factor_of


def setup_inputs(seed: int = 0) -> dict:
    key_list = jax.random.split(jax.random.key(seed), 6)
    predicted_units = jnp.clip(jnp.exp(math.log(5.0) - 4.609084 * jax.random.uniform(key_list[0], (PRODUCT_TALLY, HORIZON_LENGTH, OUTLET_TALLY), jnp.float32) ** block_levels(key_list[0], (PRODUCT_TALLY, HORIZON_LENGTH, OUTLET_TALLY), ((0, 32), (2, 8)), -0.2, 0.2)), 0.049804688, 5.0).astype(jnp.bfloat16)
    product_group = draw_product_group(jax.random.fold_in(key_list[5], 71), 0)
    product_goal = jnp.clip(jnp.exp(math.log(98304.0) - 2.302626 * jax.random.uniform(key_list[2], (PRODUCT_TALLY,), jnp.float32) ** block_levels(key_list[2], (PRODUCT_TALLY,), ((0, 32),), -0.2, 0.2)), 9830.0, 98304.0)
    group_outlet_goal = jnp.clip(jnp.exp(math.log(1536.0) - 2.306499 * jax.random.uniform(key_list[3], (GROUP_KINDS, OUTLET_TALLY), jnp.float32) ** block_levels(key_list[3], (GROUP_KINDS, OUTLET_TALLY), ((1, 8),), -0.2, 0.2)), 153.0, 1536.0)
    outlet_date_goal = jnp.clip(jnp.exp(math.log(12288.0) - 2.3032363 * jax.random.uniform(key_list[4], (HORIZON_LENGTH, OUTLET_TALLY), jnp.float32) ** block_levels(key_list[4], (HORIZON_LENGTH, OUTLET_TALLY), ((1, 8),), -0.2, 0.2)), 1228.0, 12288.0)
    return {"predicted_units": predicted_units, "product_group": product_group, "product_goal": product_goal, "group_outlet_goal": group_outlet_goal, "outlet_date_goal": outlet_date_goal}


def reference(predicted_units, product_group, product_goal, group_outlet_goal, outlet_date_goal):
    prediction_tensors = predicted_units.reshape(N_ITEM, PRODUCTS_EACH, HORIZON_LENGTH, OUTLET_TALLY)
    group_labels = product_group.reshape(N_ITEM, PRODUCTS_EACH)
    goal_vector = product_goal.reshape(N_ITEM, PRODUCTS_EACH)
    group_outlet_factor = jnp.ones((GROUP_KINDS, OUTLET_TALLY), jnp.float32)
    outlet_date_factor = jnp.ones((HORIZON_LENGTH, OUTLET_TALLY), jnp.float32)
    product_factor = jnp.ones((N_ITEM, PRODUCTS_EACH), jnp.float32)
    for round_index in range(ROUNDS):
        def product_adjust(inputs):
            tensor_portion, block_ids, target = inputs
            spread_tensor = group_outlet_factor[block_ids]
            product_marginals = jnp.sum(tensor_portion.astype(jnp.float32) * spread_tensor[:, None, :] * outlet_date_factor[None], axis=(1, 2))
            return target / product_marginals

        product_factor = lax.map(product_adjust, (prediction_tensors, group_labels, goal_vector))

        def merged_portion(current_tensor, inputs):
            tensor_portion, block_ids, multiplier = inputs
            indicator_matrix = (block_ids[:, None] == jnp.arange(GROUP_KINDS, dtype=jnp.int32)[None, :]).astype(jnp.float32)
            masked_prediction = tensor_portion.astype(jnp.float32) * multiplier[:, None, None]
            return current_tensor + jnp.einsum("bv,bjz->vjz", indicator_matrix, masked_prediction, precision=lax.Precision.HIGHEST), None

        merged_matrix, unused_slot = lax.scan(merged_portion, jnp.zeros((GROUP_KINDS, HORIZON_LENGTH, OUTLET_TALLY), jnp.float32), (prediction_tensors, group_labels, product_factor))
        for pass_index in range(INNER):
            group_outlet_factor = group_outlet_goal / jnp.sum(merged_matrix * outlet_date_factor[None], axis=1)
            outlet_date_factor = outlet_date_goal / jnp.sum(merged_matrix * group_outlet_factor[:, None, :], axis=0)

    def closing_portion(inputs):
        tensor_portion, block_ids, multiplier = inputs
        values = tensor_portion.astype(jnp.float32) * multiplier[:, None, None] * group_outlet_factor[block_ids][:, None, :] * outlet_date_factor[None]
        return values.astype(jnp.bfloat16)

    adjusted_tensor = lax.map(closing_portion, (prediction_tensors, group_labels, product_factor))
    return product_factor.reshape(PRODUCT_TALLY), group_outlet_factor, outlet_date_factor, adjusted_tensor.reshape(PRODUCT_TALLY, HORIZON_LENGTH, OUTLET_TALLY)
```

```python
import functools

import jax
import jax.numpy as jnp
from jax import lax
from jax.experimental import pallas as pl
from jax.experimental.pallas import tpu as pltpu
from jax.sharding import PartitionSpec as P

ROUNDS = 4
INNER = 3
LANES = 128
SUB = 8
SLOTS = 5
BASE_ROW = 7

F32 = jnp.float32
BF16 = jnp.bfloat16


def iota(shape, dim):
    return lax.broadcasted_iota(jnp.int32, shape, dim)


def two_parts(x):
    high = x.astype(BF16)
    low = (x - high.astype(F32)).astype(BF16)
    return high, low


def swap_blocks(tiles):
    count = len(tiles)
    width = LANES // count
    group = iota(tiles[0].shape, 1) // width
    bit = 1
    while bit < count:
        low = (group & bit) == 0
        fresh = []
        for a in range(count):
            other = tiles[a ^ bit]
            if a & bit == 0:
                fresh.append(jnp.where(low, tiles[a], pltpu.roll(other, bit * width, 1)))
            else:
                fresh.append(jnp.where(low, pltpu.roll(other, LANES - bit * width, 1), tiles[a]))
        tiles = fresh
        bit *= 2
    return tiles


def eight_sum(x):
    lane = iota(x.shape, 1)
    for bit in (1, 2, 4):
        x = x + jnp.where((lane & bit) == 0, pltpu.roll(x, LANES - bit, 1), pltpu.roll(x, bit, 1))
    return x


def compacted(rows):
    row = iota((SUB, LANES), 0)
    tile = rows[0]
    for q in range(1, SUB):
        tile = jnp.where(row == q, rows[q], tile)
    tile = eight_sum(tile)
    kept = jnp.where((iota((SUB, LANES), 1) & 7) == row, tile, 0.0)
    return jnp.sum(kept, axis=0, keepdims=True)


def expanded(line):
    line = jnp.broadcast_to(line, (SUB, LANES))
    return eight_sum(jnp.where((iota((SUB, LANES), 1) & 7) == iota((SUB, LANES), 0), line, 0.0))


def first_kernel(x_ref, flat_ref, out_ref):
    items, days, stores = x_ref.shape
    flat = x_ref[...].astype(F32).reshape(items * days, stores).astype(BF16)
    flat_ref[...] = flat
    sums = lax.dot_general(
        jnp.ones((SUB, stores), BF16), flat, (((1,), (1,)), ((), ())), preferred_element_type=F32
    )
    line = compacted([sums[:, q * LANES : (q + 1) * LANES] for q in range(SUB)])
    out_ref[...] = jnp.broadcast_to(line[None], out_ref.shape)


def margin_kernel(back_ref, flat_ref, tid_ref, out_ref):
    stores = flat_ref.shape[1]
    columns = []
    for t in range(stores // LANES):
        columns.append(jnp.concatenate(swap_blocks([back_ref[t * SUB + j] for j in range(SUB)]), axis=0))
    weights = jnp.concatenate(columns, axis=1)
    parts = jnp.concatenate(two_parts(weights), axis=0)
    sums = lax.dot_general(parts, flat_ref[...], (((1,), (1,)), ((), ())), preferred_element_type=F32)
    half = weights.shape[0]
    sums = sums[:half] + sums[half:]
    which = iota((half, LANES), 0)
    rows = []
    for q in range(SUB):
        kept = jnp.where(which == tid_ref[q : q + 1, :], sums[:, q * LANES : (q + 1) * LANES], 0.0)
        rows.append(jnp.broadcast_to(jnp.sum(kept, axis=0, keepdims=True), (SUB, LANES)))
    line = compacted(rows)
    out_ref[...] = jnp.broadcast_to(line[None], out_ref.shape)


def pool_kernel(margin_ref, goal_ref, flat_ref, tid_ref, base_ref, out_ref, factor_ref):
    stores = flat_ref.shape[1]
    total = jnp.sum(margin_ref[...], axis=0)
    factor = goal_ref[...] / total
    factor_ref[...] = factor
    spread = expanded(factor)
    half = SUB * SUB
    which = iota((half, LANES), 0)
    columns = []
    for q in range(SUB):
        columns.append(jnp.where(which == tid_ref[q : q + 1, :], spread[q : q + 1, :], 0.0))
    weights = jnp.concatenate(columns, axis=1)
    parts = jnp.concatenate(two_parts(weights), axis=0)
    sums = jnp.dot(parts, flat_ref[...], preferred_element_type=F32)
    sums = sums[:half] + sums[half:]
    row = iota((SUB, LANES), 0)
    base = jnp.broadcast_to(base_ref[...], (SUB, LANES))
    for t in range(stores // LANES):
        tiles = [sums[d * SUB : (d + 1) * SUB, t * LANES : (t + 1) * LANES] for d in range(SUB)]
        for j, tile in enumerate(swap_blocks(tiles)):
            out_ref[t * SUB + j] = jnp.where(row == BASE_ROW, base, tile)


def owner_kernel(last, taken_ref, cat_goal_ref, day_goal_ref, day_ref, out_ref, *day_out):
    devices = taken_ref.shape[0]
    cats = cat_goal_ref.shape[0]
    taken = taken_ref[...]
    slot = iota(taken.shape, 1)
    base = taken[:, BASE_ROW : BASE_ROW + 1, :].astype(jnp.int32)
    place = ((base + slot == iota(taken.shape, 2)) & (slot < SLOTS)).astype(F32)
    place = place.reshape(devices * SUB, LANES).astype(BF16)
    parts = jnp.concatenate(two_parts(taken.reshape(devices * SUB, LANES)), axis=1)
    merged = lax.dot_general(place, parts, (((0,), (0,)), ((), ())), preferred_element_type=F32)
    merged = (merged[:, :LANES] + merged[:, LANES:])[:cats]
    cat_goal, day_goal = cat_goal_ref[...], day_goal_ref[...]
    width = LANES // SUB
    day = day_ref[...]
    for _ in range(INNER):
        below = merged * day
        step = LANES // 2
        while step >= width:
            below = below + pltpu.roll(below, step, 1)
            step //= 2
        cat = cat_goal / below
        day = day_goal / jnp.sum(merged * cat, axis=0, keepdims=True)
    if last:
        group = iota((SUB, LANES), 1) // width
        tile = cat[:SUB]
        for d in range(1, SUB):
            tile = jnp.where(group == d, cat[d * SUB : (d + 1) * SUB], tile)
        both = jnp.concatenate([tile, jnp.broadcast_to(day, (SUB, LANES))], axis=0)
        out_ref[...] = jnp.broadcast_to(both[None], out_ref.shape)
        return
    day_out[0][...] = day
    product = jnp.concatenate([cat * day, jnp.zeros((LANES - cats, LANES), F32)], axis=0)
    product = jnp.concatenate(two_parts(product), axis=1)
    sent = jnp.dot(place, product, preferred_element_type=F32)
    out_ref[...] = (sent[:, :LANES] + sent[:, LANES:]).reshape(devices, SUB, LANES)


def closing_kernel(group_ref, factor_ref, back_ref, x_ref, cat_ref, day_ref, out_ref, scale_ref):
    block = x_ref.shape[0]
    stores = x_ref.shape[2]
    first = group_ref[0]
    step = pl.program_id(0)

    @pl.when(step == 0)
    def _():
        row = iota((SUB, LANES), 0)
        for t in range(stores // LANES):
            here = slice(t * LANES, (t + 1) * LANES)
            tiles = swap_blocks([back_ref[t * SUB + j, :SUB] for j in range(SUB)])
            cat_ref[:, here] = jnp.concatenate(tiles, axis=0)
            tiles = swap_blocks([back_ref[t * SUB + j, SUB:] for j in range(SUB)])
            day = tiles[0]
            for d in range(1, SUB):
                day = jnp.where(row == d, tiles[d], day)
            day_ref[:, here] = day
        last = cat_ref.shape[0] - 1
        for s in range(SLOTS):
            at = jnp.minimum(first + s, last)
            scale_ref[s] = cat_ref[pl.ds(at, 1), :] * day_ref[...]

    for i in range(block):
        at = step * block + i
        value = x_ref[i].astype(F32) * factor_ref[at] * scale_ref[group_ref[at] - first]
        out_ref[i] = value.astype(BF16)


def vmem(count):
    return [pl.BlockSpec(memory_space=pltpu.VMEM)] * count


def shards(predicted_units, product_group, product_goal, group_outlet_goal, outlet_date_goal):
    items, days, stores = predicted_units.shape
    cats = group_outlet_goal.shape[0]
    owners = lax.axis_size("item")
    width = stores // owners
    beside = lax.axis_size("store")
    at = lax.axis_index("item") * width

    message = jax.ShapeDtypeStruct((owners, SUB, LANES), F32)
    margin = jax.ShapeDtypeStruct((beside, 1, LANES), F32)
    line = jax.ShapeDtypeStruct((1, LANES), F32)

    slot = product_group - product_group[0]
    tid = jnp.repeat(slot, days).reshape(SUB, LANES) + (jnp.arange(LANES, dtype=jnp.int32) % days)[None] * SUB
    base = jnp.broadcast_to(product_group[:1].astype(F32)[None], (1, LANES))
    goal = product_goal.reshape(SUB, items // SUB).T.reshape(1, LANES)
    cat_goal = jnp.tile(lax.dynamic_slice_in_dim(group_outlet_goal, at, width, 1), (1, days))
    day_goal = lax.dynamic_slice_in_dim(outlet_date_goal, at, width, 1).reshape(1, LANES)
    day = jnp.ones((1, LANES), F32)

    flat, part = pl.pallas_call(
        first_kernel,
        out_shape=(jax.ShapeDtypeStruct((items * days, stores), BF16), margin),
        in_specs=vmem(1),
        out_specs=tuple(vmem(2)),
        name="first",
    )(predicted_units)
    for round_index in range(ROUNDS):
        total = lax.all_to_all(part, "store", 0, 0, tiled=True)
        pooled, factor = pl.pallas_call(
            pool_kernel,
            out_shape=(message, line),
            in_specs=vmem(5),
            out_specs=tuple(vmem(2)),
            name="pool",
        )(total, goal, flat, tid, base)
        taken = lax.all_to_all(pooled, "item", 0, 0, tiled=True)
        if round_index == ROUNDS - 1:
            break
        back, day = pl.pallas_call(
            functools.partial(owner_kernel, False),
            out_shape=(message, line),
            in_specs=vmem(4),
            out_specs=tuple(vmem(2)),
            name="owner",
        )(taken, cat_goal, day_goal, day)
        back = lax.all_to_all(back, "item", 0, 0, tiled=True)
        part = pl.pallas_call(
            margin_kernel,
            out_shape=margin,
            in_specs=vmem(3),
            out_specs=vmem(1)[0],
            name="margin",
        )(back, flat, tid)

    back = pl.pallas_call(
        functools.partial(owner_kernel, True),
        out_shape=jax.ShapeDtypeStruct((owners, 2 * SUB, LANES), F32),
        in_specs=vmem(4),
        out_specs=vmem(1)[0],
        name="owner_last",
    )(taken, cat_goal, day_goal, day)
    back = lax.all_to_all(back, "item", 0, 0, tiled=True)
    product_factor = factor.reshape(items // SUB, SUB).T.reshape(items)
    block = 16
    smem = pl.BlockSpec(memory_space=pltpu.SMEM)
    wide = pl.BlockSpec((block, days, stores), lambda i: (i, 0, 0))
    group_outlet_factor, outlet_date_factor, adjusted_tensor = pl.pallas_call(
        closing_kernel,
        grid=(items // block,),
        out_shape=(
            jax.ShapeDtypeStruct((cats, stores), F32),
            jax.ShapeDtypeStruct((days, stores), F32),
            jax.ShapeDtypeStruct((items, days, stores), BF16),
        ),
        in_specs=[smem, smem, pl.BlockSpec((owners, 2 * SUB, LANES), lambda i: (0, 0, 0)), wide],
        out_specs=(
            pl.BlockSpec((cats, stores), lambda i: (0, 0)),
            pl.BlockSpec((days, stores), lambda i: (0, 0)),
            wide,
        ),
        scratch_shapes=[pltpu.VMEM((SUB, days, stores), F32)],
        name="closing",
    )(product_group, product_factor, back, predicted_units)
    return (product_factor, group_outlet_factor, outlet_date_factor, adjusted_tensor)


def solution(mesh):
    in_specs = (P("item", None, "store"), P("item"), P("item"), P(None, "store"), P(None, "store"))
    out_specs = (P("item"), P(None, "store"), P(None, "store"), P("item", None, "store"))
    return jax.shard_map(shards, mesh=mesh, in_specs=in_specs, out_specs=out_specs, check_vma=False)
```

```python
import functools

import jax
import jax.numpy as jnp
from jax import lax
from jax.experimental import pallas as pl
from jax.experimental.pallas import tpu as pltpu
from jax.sharding import PartitionSpec as P

ROUNDS = 4
INNER = 3
LANES = 128
SUB = 8
SLOTS = 5
BASE_ROW = 7

F32 = jnp.float32
BF16 = jnp.bfloat16


def iota(shape, dim):
    return lax.broadcasted_iota(jnp.int32, shape, dim)


def two_parts(x):
    high = x.astype(BF16)
    low = (x - high.astype(F32)).astype(BF16)
    return high, low


def swap_blocks(tiles):
    count = len(tiles)
    width = LANES // count
    group = iota(tiles[0].shape, 1) // width
    bit = 1
    while bit < count:
        low = (group & bit) == 0
        fresh = []
        for a in range(count):
            other = tiles[a ^ bit]
            if a & bit == 0:
                fresh.append(jnp.where(low, tiles[a], pltpu.roll(other, bit * width, 1)))
            else:
                fresh.append(jnp.where(low, pltpu.roll(other, LANES - bit * width, 1), tiles[a]))
        tiles = fresh
        bit *= 2
    return tiles


def eight_sum(x):
    lane = iota(x.shape, 1)
    for bit in (1, 2, 4):
        x = x + jnp.where((lane & bit) == 0, pltpu.roll(x, LANES - bit, 1), pltpu.roll(x, bit, 1))
    return x


def compacted(rows):
    row = iota((SUB, LANES), 0)
    tile = rows[0]
    for q in range(1, SUB):
        tile = jnp.where(row == q, rows[q], tile)
    tile = eight_sum(tile)
    kept = jnp.where((iota((SUB, LANES), 1) & 7) == row, tile, 0.0)
    return jnp.sum(kept, axis=0, keepdims=True)


def expanded(line):
    line = jnp.broadcast_to(line, (SUB, LANES))
    return eight_sum(jnp.where((iota((SUB, LANES), 1) & 7) == iota((SUB, LANES), 0), line, 0.0))


def first_kernel(x_ref, flat_ref, out_ref):
    items, days, stores = x_ref.shape
    flat = x_ref[...].astype(F32).reshape(items * days, stores).astype(BF16)
    flat_ref[...] = flat
    sums = lax.dot_general(
        jnp.ones((SUB, stores), BF16), flat, (((1,), (1,)), ((), ())), preferred_element_type=F32
    )
    line = compacted([sums[:, q * LANES : (q + 1) * LANES] for q in range(SUB)])
    out_ref[...] = jnp.broadcast_to(line[None], out_ref.shape)


def margin_kernel(back_ref, flat_ref, tid_ref, out_ref):
    stores = flat_ref.shape[1]
    columns = []
    for t in range(stores // LANES):
        columns.append(jnp.concatenate(swap_blocks([back_ref[t * SUB + j] for j in range(SUB)]), axis=0))
    weights = jnp.concatenate(columns, axis=1)
    parts = jnp.concatenate(two_parts(weights), axis=0)
    sums = lax.dot_general(parts, flat_ref[...], (((1,), (1,)), ((), ())), preferred_element_type=F32)
    half = weights.shape[0]
    sums = sums[:half] + sums[half:]
    which = iota((half, LANES), 0)
    rows = []
    for q in range(SUB):
        kept = jnp.where(which == tid_ref[q : q + 1, :], sums[:, q * LANES : (q + 1) * LANES], 0.0)
        rows.append(jnp.broadcast_to(jnp.sum(kept, axis=0, keepdims=True), (SUB, LANES)))
    line = compacted(rows)
    out_ref[...] = jnp.broadcast_to(line[None], out_ref.shape)


def pool_kernel(margin_ref, goal_ref, flat_ref, tid_ref, base_ref, out_ref, factor_ref):
    stores = flat_ref.shape[1]
    total = jnp.sum(margin_ref[...], axis=0)
    factor = goal_ref[...] / total
    factor_ref[...] = factor
    spread = expanded(factor)
    half = SUB * SUB
    which = iota((half, LANES), 0)
    columns = []
    for q in range(SUB):
        columns.append(jnp.where(which == tid_ref[q : q + 1, :], spread[q : q + 1, :], 0.0))
    weights = jnp.concatenate(columns, axis=1)
    parts = jnp.concatenate(two_parts(weights), axis=0)
    sums = jnp.dot(parts, flat_ref[...], preferred_element_type=F32)
    sums = sums[:half] + sums[half:]
    row = iota((SUB, LANES), 0)
    base = jnp.broadcast_to(base_ref[...], (SUB, LANES))
    for t in range(stores // LANES):
        tiles = [sums[d * SUB : (d + 1) * SUB, t * LANES : (t + 1) * LANES] for d in range(SUB)]
        for j, tile in enumerate(swap_blocks(tiles)):
            out_ref[t * SUB + j] = jnp.where(row == BASE_ROW, base, tile)


def owner_kernel(last, taken_ref, cat_goal_ref, day_goal_ref, day_ref, out_ref, *day_out):
    devices = taken_ref.shape[0]
    cats = cat_goal_ref.shape[0]
    taken = taken_ref[...]
    slot = iota(taken.shape, 1)
    base = taken[:, BASE_ROW : BASE_ROW + 1, :].astype(jnp.int32)
    place = ((base + slot == iota(taken.shape, 2)) & (slot < SLOTS)).astype(F32)
    place = place.reshape(devices * SUB, LANES).astype(BF16)
    parts = jnp.concatenate(two_parts(taken.reshape(devices * SUB, LANES)), axis=1)
    merged = lax.dot_general(place, parts, (((0,), (0,)), ((), ())), preferred_element_type=F32)
    merged = (merged[:, :LANES] + merged[:, LANES:])[:cats]
    cat_goal, day_goal = cat_goal_ref[...], day_goal_ref[...]
    width = LANES // SUB
    day = day_ref[...]
    for _ in range(INNER):
        below = merged * day
        step = LANES // 2
        while step >= width:
            below = below + pltpu.roll(below, step, 1)
            step //= 2
        cat = cat_goal / below
        day = day_goal / jnp.sum(merged * cat, axis=0, keepdims=True)
    if last:
        group = iota((SUB, LANES), 1) // width
        tile = cat[:SUB]
        for d in range(1, SUB):
            tile = jnp.where(group == d, cat[d * SUB : (d + 1) * SUB], tile)
        both = jnp.concatenate([tile, jnp.broadcast_to(day, (SUB, LANES))], axis=0)
        out_ref[...] = jnp.broadcast_to(both[None], out_ref.shape)
        return
    day_out[0][...] = day
    product = jnp.concatenate([cat * day, jnp.zeros((LANES - cats, LANES), F32)], axis=0)
    product = jnp.concatenate(two_parts(product), axis=1)
    sent = jnp.dot(place, product, preferred_element_type=F32)
    out_ref[...] = (sent[:, :LANES] + sent[:, LANES:]).reshape(devices, SUB, LANES)


def closing_kernel(group_ref, factor_ref, back_ref, x_ref, cat_ref, day_ref, out_ref, scale_ref):
    block = x_ref.shape[0]
    stores = x_ref.shape[2]
    first = group_ref[0]
    step = pl.program_id(0)

    @pl.when(step == 0)
    def _():
        row = iota((SUB, LANES), 0)
        for t in range(stores // LANES):
            here = slice(t * LANES, (t + 1) * LANES)
            tiles = swap_blocks([back_ref[t * SUB + j, :SUB] for j in range(SUB)])
            cat_ref[:, here] = jnp.concatenate(tiles, axis=0)
            tiles = swap_blocks([back_ref[t * SUB + j, SUB:] for j in range(SUB)])
            day = tiles[0]
            for d in range(1, SUB):
                day = jnp.where(row == d, tiles[d], day)
            day_ref[:, here] = day
        last = cat_ref.shape[0] - 1
        for s in range(SLOTS):
            at = jnp.minimum(first + s, last)
            scale_ref[s] = cat_ref[pl.ds(at, 1), :] * day_ref[...]

    for i in range(block):
        at = step * block + i
        value = x_ref[i].astype(F32) * factor_ref[at] * scale_ref[group_ref[at] - first]
        out_ref[i] = value.astype(BF16)


def vmem(count):
    return [pl.BlockSpec(memory_space=pltpu.VMEM)] * count


def held(x):
    return pltpu.with_memory_space_constraint(x, pltpu.VMEM)


LIMIT = pltpu.CompilerParams(vmem_limit_bytes=8 * 1024 * 1024)


def shards(predicted_units, product_group, product_goal, group_outlet_goal, outlet_date_goal):
    items, days, stores = predicted_units.shape
    cats = group_outlet_goal.shape[0]
    owners = lax.axis_size("item")
    width = stores // owners
    beside = lax.axis_size("store")
    at = lax.axis_index("item") * width

    message = pltpu.VMEM((owners, SUB, LANES), F32)
    margin = pltpu.VMEM((beside, 1, LANES), F32)
    line = pltpu.VMEM((1, LANES), F32)

    slot = product_group - product_group[0]
    tid = jnp.repeat(slot, days).reshape(SUB, LANES) + (jnp.arange(LANES, dtype=jnp.int32) % days)[None] * SUB
    base = jnp.broadcast_to(product_group[:1].astype(F32)[None], (1, LANES))
    goal = product_goal.reshape(SUB, items // SUB).T.reshape(1, LANES)
    cat_goal = jnp.tile(lax.dynamic_slice_in_dim(group_outlet_goal, at, width, 1), (1, days))
    day_goal = lax.dynamic_slice_in_dim(outlet_date_goal, at, width, 1).reshape(1, LANES)
    day = jnp.ones((1, LANES), F32)

    flat, part = pl.pallas_call(
        first_kernel,
        out_shape=(pltpu.VMEM((items * days, stores), BF16), margin),
        in_specs=vmem(1),
        out_specs=tuple(vmem(2)),
        compiler_params=LIMIT,
        name="first",
    )(predicted_units)
    for round_index in range(ROUNDS):
        total = lax.all_to_all(part, "store", 0, 0, tiled=True)
        pooled, factor = pl.pallas_call(
            pool_kernel,
            out_shape=(message, line),
            in_specs=vmem(5),
            out_specs=tuple(vmem(2)),
            compiler_params=LIMIT,
        name="pool",
        )(*map(held, (total, goal, flat, tid, base)))
        taken = lax.all_to_all(pooled, "item", 0, 0, tiled=True)
        if round_index == ROUNDS - 1:
            break
        back, day = pl.pallas_call(
            functools.partial(owner_kernel, False),
            out_shape=(message, line),
            in_specs=vmem(4),
            out_specs=tuple(vmem(2)),
            compiler_params=LIMIT,
        name="owner",
        )(*map(held, (taken, cat_goal, day_goal, day)))
        back = lax.all_to_all(back, "item", 0, 0, tiled=True)
        part = pl.pallas_call(
            margin_kernel,
            out_shape=margin,
            in_specs=vmem(3),
            out_specs=vmem(1)[0],
            compiler_params=LIMIT,
        name="margin",
        )(*map(held, (back, flat, tid)))

    back = pl.pallas_call(
        functools.partial(owner_kernel, True),
        out_shape=pltpu.VMEM((owners, 2 * SUB, LANES), F32),
        in_specs=vmem(4),
        out_specs=vmem(1)[0],
        compiler_params=LIMIT,
        name="owner_last",
    )(*map(held, (taken, cat_goal, day_goal, day)))
    back = lax.all_to_all(back, "item", 0, 0, tiled=True)
    product_factor = factor.reshape(items // SUB, SUB).T.reshape(items)
    block = 16
    smem = pl.BlockSpec(memory_space=pltpu.SMEM)
    wide = pl.BlockSpec((block, days, stores), lambda i: (i, 0, 0))
    group_outlet_factor, outlet_date_factor, adjusted_tensor = pl.pallas_call(
        closing_kernel,
        grid=(items // block,),
        out_shape=(
            jax.ShapeDtypeStruct((cats, stores), F32),
            jax.ShapeDtypeStruct((days, stores), F32),
            jax.ShapeDtypeStruct((items, days, stores), BF16),
        ),
        in_specs=[smem, smem, pl.BlockSpec((owners, 2 * SUB, LANES), lambda i: (0, 0, 0)), wide],
        out_specs=(
            pl.BlockSpec((cats, stores), lambda i: (0, 0)),
            pl.BlockSpec((days, stores), lambda i: (0, 0)),
            wide,
        ),
        scratch_shapes=[pltpu.VMEM((SUB, days, stores), F32)],
        compiler_params=LIMIT,
        name="closing",
    )(product_group, product_factor, back, predicted_units)
    return (product_factor, group_outlet_factor, outlet_date_factor, adjusted_tensor)


def solution(mesh):
    in_specs = (P("item", None, "store"), P("item"), P("item"), P(None, "store"), P(None, "store"))
    out_specs = (P("item"), P(None, "store"), P(None, "store"), P("item", None, "store"))
    return jax.shard_map(shards, mesh=mesh, in_specs=in_specs, out_specs=out_specs, check_vma=False)
```

```python
import functools

import jax
import jax.numpy as jnp
from jax import lax
from jax.experimental import pallas as pl
from jax.experimental.pallas import tpu as pltpu
from jax.sharding import PartitionSpec as P

ROUNDS = 4
INNER = 3
LANES = 128
SUB = 8
SLOTS = 5
BASE_ROW = 7

F32 = jnp.float32
BF16 = jnp.bfloat16


def iota(shape, dim):
    return lax.broadcasted_iota(jnp.int32, shape, dim)


def two_parts(x):
    high = x.astype(BF16)
    low = (x - high.astype(F32)).astype(BF16)
    return high, low


def swap_blocks(tiles):
    count = len(tiles)
    width = LANES // count
    group = iota(tiles[0].shape, 1) // width
    bit = 1
    while bit < count:
        low = (group & bit) == 0
        fresh = []
        for a in range(count):
            other = tiles[a ^ bit]
            if a & bit == 0:
                fresh.append(jnp.where(low, tiles[a], pltpu.roll(other, bit * width, 1)))
            else:
                fresh.append(jnp.where(low, pltpu.roll(other, LANES - bit * width, 1), tiles[a]))
        tiles = fresh
        bit *= 2
    return tiles


def eight_sum(x):
    lane = iota(x.shape, 1)
    for bit in (1, 2, 4):
        x = x + jnp.where((lane & bit) == 0, pltpu.roll(x, LANES - bit, 1), pltpu.roll(x, bit, 1))
    return x


def compacted(rows):
    row = iota((SUB, LANES), 0)
    tile = rows[0]
    for q in range(1, SUB):
        tile = jnp.where(row == q, rows[q], tile)
    tile = eight_sum(tile)
    kept = jnp.where((iota((SUB, LANES), 1) & 7) == row, tile, 0.0)
    return jnp.sum(kept, axis=0, keepdims=True)


def expanded(line):
    line = jnp.broadcast_to(line, (SUB, LANES))
    return eight_sum(jnp.where((iota((SUB, LANES), 1) & 7) == iota((SUB, LANES), 0), line, 0.0))


def picked(x, index):
    return jnp.take_along_axis(x, index, axis=1)


def first_kernel(
    x_hbm, group_hbm, goal_hbm, cat_all_hbm, day_all_hbm,
    flat_ref, out_ref, tid_ref, line_ref, cat_goal_ref,
    x_buf, group_ref, goal_ref, cat_all_ref, day_all_ref, sems, small_sems,
):
    items, days, stores = x_hbm.shape
    chunks = sems.shape[0]
    block = items // chunks
    small = []
    for n, (src, dst) in enumerate(
        ((group_hbm, group_ref), (goal_hbm, goal_ref), (cat_all_hbm, cat_all_ref), (day_all_hbm, day_all_ref))
    ):
        small.append(pltpu.make_async_copy(src, dst, small_sems.at[n]))
        small[n].start()
    copies = []
    for n in range(chunks):
        rows = pl.ds(n * block, block)
        copies.append(pltpu.make_async_copy(x_hbm.at[rows], x_buf.at[rows], sems.at[n]))
        copies[n].start()
    for copy in small:
        copy.wait()

    row, lane = iota((SUB, LANES), 0), iota((SUB, LANES), 1)
    group = jnp.broadcast_to(group_ref[...], (SUB, LANES))
    first = picked(group, jnp.zeros_like(lane))
    slot = picked(group, row * (items // SUB) + lane // days) - first
    tid_ref[...] = (lane % days) * SUB + slot
    goal = jnp.broadcast_to(goal_ref[...], (SUB, LANES))
    line_ref[0:1] = picked(goal, (lane % SUB) * (items // SUB) + lane // SUB)[:1]
    line_ref[1:2] = first[:1].astype(F32)
    width = LANES // days
    at = lax.axis_index("item") * width
    there = pl.ds(pl.multiple_of(at // LANES * LANES, LANES), LANES)
    index = at % LANES + lane % width
    for k in range(cat_goal_ref.shape[0] // SUB):
        rows = slice(k * SUB, (k + 1) * SUB)
        cat_goal_ref[rows] = picked(cat_all_ref[rows, there], index)
    day_goal = jnp.where(lane // width == row, picked(day_all_ref[:, there], index), 0.0)
    line_ref[2:3] = jnp.sum(day_goal, axis=0, keepdims=True)

    tiles = []
    for n in range(chunks):
        copies[n].wait()
        x = x_buf[n * block : (n + 1) * block].astype(F32)
        flat = x.reshape(block * days, stores).astype(BF16)
        flat_ref[n * block * days : (n + 1) * block * days] = flat
        sums = lax.dot_general(
            jnp.ones((SUB, stores), BF16), flat, (((1,), (1,)), ((), ())), preferred_element_type=F32
        )
        tiles += [sums[:, q * LANES : (q + 1) * LANES] for q in range(block * days // LANES)]
    out_ref[...] = jnp.broadcast_to(compacted(tiles)[None], out_ref.shape)


def margin_kernel(back_ref, flat_ref, tid_ref, out_ref):
    stores = flat_ref.shape[1]
    columns = []
    for t in range(stores // LANES):
        columns.append(jnp.concatenate(swap_blocks([back_ref[t * SUB + j] for j in range(SUB)]), axis=0))
    weights = jnp.concatenate(columns, axis=1)
    parts = jnp.concatenate(two_parts(weights), axis=0)
    sums = lax.dot_general(parts, flat_ref[...], (((1,), (1,)), ((), ())), preferred_element_type=F32)
    half = weights.shape[0]
    sums = sums[:half] + sums[half:]
    which = iota((half, LANES), 0)
    rows = []
    for q in range(SUB):
        kept = jnp.where(which == tid_ref[q : q + 1, :], sums[:, q * LANES : (q + 1) * LANES], 0.0)
        rows.append(jnp.broadcast_to(jnp.sum(kept, axis=0, keepdims=True), (SUB, LANES)))
    line = compacted(rows)
    out_ref[...] = jnp.broadcast_to(line[None], out_ref.shape)


def pool_kernel(margin_ref, line_ref, flat_ref, tid_ref, out_ref, *factor_out):
    stores = flat_ref.shape[1]
    total = jnp.sum(margin_ref[...], axis=0)
    factor = line_ref[0:1] / total
    if factor_out:
        lane = iota((SUB, LANES), 1)
        index = lane % (LANES // SUB) * SUB + lane // (LANES // SUB)
        factor_out[0][...] = picked(jnp.broadcast_to(factor, (SUB, LANES)), index)[:1]
    spread = expanded(factor)
    half = SUB * SUB
    which = iota((half, LANES), 0)
    columns = []
    for q in range(SUB):
        columns.append(jnp.where(which == tid_ref[q : q + 1, :], spread[q : q + 1, :], 0.0))
    weights = jnp.concatenate(columns, axis=1)
    parts = jnp.concatenate(two_parts(weights), axis=0)
    sums = jnp.dot(parts, flat_ref[...], preferred_element_type=F32)
    sums = sums[:half] + sums[half:]
    row = iota((SUB, LANES), 0)
    base = jnp.broadcast_to(line_ref[1:2], (SUB, LANES))
    for t in range(stores // LANES):
        tiles = [sums[d * SUB : (d + 1) * SUB, t * LANES : (t + 1) * LANES] for d in range(SUB)]
        for j, tile in enumerate(swap_blocks(tiles)):
            out_ref[t * SUB + j] = jnp.where(row == BASE_ROW, base, tile)


def fitted(merged, cat_goal, day_goal, day):
    width = LANES // SUB
    for _ in range(INNER):
        below = merged * day
        step = LANES // 2
        while step >= width:
            below = below + pltpu.roll(below, step, 1)
            step //= 2
        cat = cat_goal / below
        day = day_goal / jnp.sum(merged * cat, axis=0, keepdims=True)
    return cat, day


def taken_parts(taken_ref):
    devices = taken_ref.shape[0]
    return jnp.concatenate(two_parts(taken_ref[...].reshape(devices * SUB, LANES)), axis=1)


def answer(place, cat, day, out_ref):
    cats = cat.shape[0]
    product = jnp.concatenate([cat * day, jnp.zeros((LANES - cats, LANES), F32)], axis=0)
    product = jnp.concatenate(two_parts(product), axis=1)
    sent = jnp.dot(place, product, preferred_element_type=F32)
    out_ref[...] = (sent[:, :LANES] + sent[:, LANES:]).reshape(out_ref.shape)


def owner_first_kernel(taken_ref, cat_goal_ref, line_ref, out_ref, day_ref, place_ref, across_ref):
    devices = taken_ref.shape[0]
    cats = cat_goal_ref.shape[0]
    shape = taken_ref.shape
    slot = iota(shape, 1)
    base = taken_ref[:, BASE_ROW : BASE_ROW + 1, :].astype(jnp.int32)
    place = ((base + slot == iota(shape, 2)) & (slot < SLOTS)).astype(F32)
    place = place.reshape(devices * SUB, LANES)
    across = place.T[:cats].astype(BF16)
    place = place.astype(BF16)
    place_ref[...] = place
    across_ref[...] = across
    merged = jnp.dot(across, taken_parts(taken_ref), preferred_element_type=F32)
    merged = merged[:, :LANES] + merged[:, LANES:]
    cat, day = fitted(merged, cat_goal_ref[...], line_ref[2:3], jnp.ones((1, LANES), F32))
    day_ref[...] = day
    answer(place, cat, day, out_ref)


def owner_kernel(taken_ref, cat_goal_ref, line_ref, day_ref, place_ref, across_ref, out_ref, day_out_ref):
    merged = jnp.dot(across_ref[...], taken_parts(taken_ref), preferred_element_type=F32)
    merged = merged[:, :LANES] + merged[:, LANES:]
    cat, day = fitted(merged, cat_goal_ref[...], line_ref[2:3], day_ref[...])
    day_out_ref[...] = day
    answer(place_ref[...], cat, day, out_ref)


def owner_last_kernel(taken_ref, cat_goal_ref, line_ref, day_ref, across_ref, out_ref):
    merged = jnp.dot(across_ref[...], taken_parts(taken_ref), preferred_element_type=F32)
    merged = merged[:, :LANES] + merged[:, LANES:]
    cat, day = fitted(merged, cat_goal_ref[...], line_ref[2:3], day_ref[...])
    group = iota((SUB, LANES), 1) // (LANES // SUB)
    tile = cat[:SUB]
    for d in range(1, SUB):
        tile = jnp.where(group == d, cat[d * SUB : (d + 1) * SUB], tile)
    both = jnp.concatenate([tile, jnp.broadcast_to(day, (SUB, LANES))], axis=0)
    out_ref[...] = jnp.broadcast_to(both[None], out_ref.shape)


def closing_kernel(group_ref, factor_ref, back_ref, x_ref, cat_ref, day_ref, out_ref, scale_ref):
    block = x_ref.shape[0]
    stores = x_ref.shape[2]
    first = group_ref[0]
    step = pl.program_id(0)

    @pl.when(step == 0)
    def _():
        row = iota((SUB, LANES), 0)
        for t in range(stores // LANES):
            here = slice(t * LANES, (t + 1) * LANES)
            tiles = swap_blocks([back_ref[t * SUB + j, :SUB] for j in range(SUB)])
            cat_ref[:, here] = jnp.concatenate(tiles, axis=0)
            tiles = swap_blocks([back_ref[t * SUB + j, SUB:] for j in range(SUB)])
            day = tiles[0]
            for d in range(1, SUB):
                day = jnp.where(row == d, tiles[d], day)
            day_ref[:, here] = day
        last = cat_ref.shape[0] - 1
        for s in range(SLOTS):
            at = jnp.minimum(first + s, last)
            scale_ref[s] = cat_ref[pl.ds(at, 1), :] * day_ref[...]

    for i in range(block):
        at = step * block + i
        value = x_ref[i].astype(F32) * factor_ref[0, at] * scale_ref[group_ref[at] - first]
        out_ref[i] = value.astype(BF16)


def vmem(count):
    return [pl.BlockSpec(memory_space=pltpu.VMEM)] * count


def held(x):
    return pltpu.with_memory_space_constraint(x, pltpu.VMEM)


def far(x):
    return pltpu.with_memory_space_constraint(x, pltpu.HBM)


LIMIT = pltpu.CompilerParams(vmem_limit_bytes=8 * 1024 * 1024)


def call(kernel, out_shape, *args, **options):
    return pl.pallas_call(
        kernel,
        out_shape=out_shape,
        in_specs=vmem(len(args)),
        out_specs=tuple(vmem(len(out_shape))),
        compiler_params=LIMIT,
        **options,
    )(*map(held, args))


def shards(predicted_units, product_group, product_goal, group_outlet_goal, outlet_date_goal):
    items, days, stores = predicted_units.shape
    cats = group_outlet_goal.shape[0]
    owners = lax.axis_size("item")
    beside = lax.axis_size("store")

    message = pltpu.VMEM((owners, SUB, LANES), F32)
    margin = pltpu.VMEM((beside, 1, LANES), F32)
    line = pltpu.VMEM((1, LANES), F32)
    tile = pltpu.VMEM((SUB, LANES), jnp.int32)
    per_cat = pltpu.VMEM((cats, LANES), F32)

    flat, part, tid, lines, cat_goal = pl.pallas_call(
        first_kernel,
        out_shape=(
            pltpu.VMEM((items * days, stores), BF16),
            margin,
            tile,
            pltpu.VMEM((SUB, LANES), F32),
            per_cat,
        ),
        in_specs=[pl.BlockSpec(memory_space=pltpu.HBM)] * 5,
        out_specs=tuple(vmem(5)),
        scratch_shapes=[
            pltpu.VMEM(predicted_units.shape, BF16),
            pltpu.VMEM((1, items), jnp.int32),
            pltpu.VMEM((1, items), F32),
            pltpu.VMEM((cats, stores), F32),
            pltpu.VMEM((days, stores), F32),
            pltpu.SemaphoreType.DMA((4,)),
            pltpu.SemaphoreType.DMA((4,)),
        ],
        compiler_params=LIMIT,
        name="first",
    )(
        *map(
            far,
            (
                predicted_units,
                product_group.reshape(1, items),
                product_goal.reshape(1, items),
                group_outlet_goal,
                outlet_date_goal,
            ),
        )
    )
    for n in range(ROUNDS):
        total = lax.all_to_all(part, "store", 0, 0, tiled=True)
        shapes = (message,) if n < ROUNDS - 1 else (message, jax.ShapeDtypeStruct((1, LANES), F32))
        pooled, *factor = call(pool_kernel, shapes, total, lines, flat, tid, name="pool")
        taken = lax.all_to_all(pooled, "item", 0, 0, tiled=True)
        if n == ROUNDS - 1:
            break
        if n == 0:
            shapes = (message, line, pltpu.VMEM((owners * SUB, LANES), BF16), pltpu.VMEM((cats, owners * SUB), BF16))
            back, day, place, across = call(owner_first_kernel, shapes, taken, cat_goal, lines, name="owner_first")
        else:
            back, day = call(owner_kernel, (message, line), taken, cat_goal, lines, day, place, across, name="owner")
        back = lax.all_to_all(back, "item", 0, 0, tiled=True)
        (part,) = call(margin_kernel, (margin,), back, flat, tid, name="margin")

    (back,) = call(
        owner_last_kernel,
        (pltpu.VMEM((owners, 2 * SUB, LANES), F32),),
        taken, cat_goal, lines, day, across,
        name="owner_last",
    )
    back = lax.all_to_all(back, "item", 0, 0, tiled=True)
    block = 32
    smem = pl.BlockSpec(memory_space=pltpu.SMEM)
    wide = pl.BlockSpec((block, days, stores), lambda i: (i, 0, 0))
    group_outlet_factor, outlet_date_factor, adjusted_tensor = pl.pallas_call(
        closing_kernel,
        grid=(items // block,),
        out_shape=(
            jax.ShapeDtypeStruct((cats, stores), F32),
            jax.ShapeDtypeStruct((days, stores), F32),
            jax.ShapeDtypeStruct((items, days, stores), BF16),
        ),
        in_specs=[smem, smem, pl.BlockSpec((owners, 2 * SUB, LANES), lambda i: (0, 0, 0)), wide],
        out_specs=(
            pl.BlockSpec((cats, stores), lambda i: (0, 0)),
            pl.BlockSpec((days, stores), lambda i: (0, 0)),
            wide,
        ),
        scratch_shapes=[pltpu.VMEM((SUB, days, stores), F32)],
        compiler_params=LIMIT,
        name="closing",
    )(product_group, factor[0], back, predicted_units)
    return (factor[0].reshape(items), group_outlet_factor, outlet_date_factor, adjusted_tensor)


def solution(mesh):
    in_specs = (P("item", None, "store"), P("item"), P("item"), P(None, "store"), P(None, "store"))
    out_specs = (P("item"), P(None, "store"), P(None, "store"), P("item", None, "store"))
    return jax.shard_map(shards, mesh=mesh, in_specs=in_specs, out_specs=out_specs, check_vma=False)
```

```python
import functools

import jax
import jax.numpy as jnp
from jax import lax
from jax.experimental import pallas as pl
from jax.experimental.pallas import tpu as pltpu
from jax.sharding import PartitionSpec as P

ROUNDS = 4
INNER = 3
LANES = 128
SUB = 8
SLOTS = 5
BASE_ROW = 7

F32 = jnp.float32
BF16 = jnp.bfloat16


def iota(shape, dim):
    return lax.broadcasted_iota(jnp.int32, shape, dim)


def two_parts(x):
    high = x.astype(BF16)
    low = (x - high.astype(F32)).astype(BF16)
    return high, low


def swap_blocks(tiles):
    count = len(tiles)
    width = LANES // count
    group = iota(tiles[0].shape, 1) // width
    bit = 1
    while bit < count:
        low = (group & bit) == 0
        fresh = []
        for a in range(count):
            other = tiles[a ^ bit]
            if a & bit == 0:
                fresh.append(jnp.where(low, tiles[a], pltpu.roll(other, bit * width, 1)))
            else:
                fresh.append(jnp.where(low, pltpu.roll(other, LANES - bit * width, 1), tiles[a]))
        tiles = fresh
        bit *= 2
    return tiles


def swap_within(x):
    width = LANES // SUB
    row, group = iota(x.shape, 0), iota(x.shape, 1) // width
    for bit in (1, 2, 4):
        low, same = (row & bit) == 0, (row & bit) == (group & bit)
        above = pltpu.roll(pltpu.roll(x, SUB - bit, 0), bit * width, 1)
        if 2 * bit == SUB:
            x = jnp.where(same, x, above)
        else:
            below = pltpu.roll(pltpu.roll(x, bit, 0), LANES - bit * width, 1)
            x = jnp.where(same, x, jnp.where(low, above, below))
    return x


def eight_sum(x):
    lane = iota(x.shape, 1)
    for bit in (1, 2, 4):
        x = x + jnp.where((lane & bit) == 0, pltpu.roll(x, LANES - bit, 1), pltpu.roll(x, bit, 1))
    return x


def compacted(rows):
    row = iota((SUB, LANES), 0)
    tile = rows[0]
    for q in range(1, SUB):
        tile = jnp.where(row == q, rows[q], tile)
    tile = eight_sum(tile)
    kept = jnp.where((iota((SUB, LANES), 1) & 7) == row, tile, 0.0)
    return jnp.sum(kept, axis=0, keepdims=True)


def expanded(line):
    line = jnp.broadcast_to(line, (SUB, LANES))
    return eight_sum(jnp.where((iota((SUB, LANES), 1) & 7) == iota((SUB, LANES), 0), line, 0.0))


def picked(x, index):
    return jnp.take_along_axis(x, index, axis=1)


def first_kernel(
    x_hbm, group_hbm, goal_hbm, cat_all_hbm, day_all_hbm,
    flat_ref, out_ref, tid_ref, line_ref, cat_goal_ref,
    x_buf, group_ref, goal_ref, cat_all_ref, day_all_ref, sems, small_sems,
):
    items, days, stores = x_hbm.shape
    chunks = sems.shape[0]
    block = items // chunks
    small = []
    for n, (src, dst) in enumerate(
        ((group_hbm, group_ref), (goal_hbm, goal_ref), (cat_all_hbm, cat_all_ref), (day_all_hbm, day_all_ref))
    ):
        small.append(pltpu.make_async_copy(src, dst, small_sems.at[n]))
        small[n].start()
    copies = []
    for n in range(chunks):
        rows = pl.ds(n * block, block)
        copies.append(pltpu.make_async_copy(x_hbm.at[rows], x_buf.at[rows], sems.at[n]))
        copies[n].start()
    for copy in small:
        copy.wait()

    row, lane = iota((SUB, LANES), 0), iota((SUB, LANES), 1)
    group = jnp.broadcast_to(group_ref[...], (SUB, LANES))
    first = picked(group, jnp.zeros_like(lane))
    slot = picked(group, row * (items // SUB) + lane // days) - first
    tid_ref[...] = (lane % days) * SUB + slot
    goal = jnp.broadcast_to(goal_ref[...], (SUB, LANES))
    line_ref[0:1] = picked(goal, (lane % SUB) * (items // SUB) + lane // SUB)[:1]
    line_ref[1:2] = first[:1].astype(F32)
    width = LANES // days
    at = lax.axis_index("item") * width
    there = pl.ds(pl.multiple_of(at // LANES * LANES, LANES), LANES)
    index = at % LANES + lane % width
    for k in range(cat_goal_ref.shape[0] // SUB):
        rows = slice(k * SUB, (k + 1) * SUB)
        cat_goal_ref[rows] = picked(cat_all_ref[rows, there], index)
    day_goal = jnp.where(lane // width == row, picked(day_all_ref[:, there], index), 0.0)
    line_ref[2:3] = jnp.sum(day_goal, axis=0, keepdims=True)

    tiles = []
    for n in range(chunks):
        copies[n].wait()
        x = x_buf[n * block : (n + 1) * block].astype(F32)
        flat = x.reshape(block * days, stores).astype(BF16)
        flat_ref[n * block * days : (n + 1) * block * days] = flat
        sums = lax.dot_general(
            jnp.ones((SUB, stores), BF16), flat, (((1,), (1,)), ((), ())), preferred_element_type=F32
        )
        tiles += [sums[:, q * LANES : (q + 1) * LANES] for q in range(block * days // LANES)]
    out_ref[...] = jnp.broadcast_to(compacted(tiles)[None], out_ref.shape)


def margin_kernel(back_ref, flat_ref, tid_ref, out_ref):
    days, stores = SUB, flat_ref.shape[1]
    pairs = []
    for t in range(stores // LANES):
        at = t * 2 * SUB
        day = swap_within(back_ref[pl.ds(at, SUB, stride=2), :])
        cat = swap_within(back_ref[pl.ds(at + 1, SUB, stride=2), :])
        pairs.append((day, cat))
    weights = jnp.concatenate(
        [jnp.concatenate([cat * day[d : d + 1] for day, cat in pairs], axis=1) for d in range(days)], axis=0
    )
    parts = jnp.concatenate(two_parts(weights), axis=0)
    sums = lax.dot_general(parts, flat_ref[...], (((1,), (1,)), ((), ())), preferred_element_type=F32)
    half = weights.shape[0]
    sums = sums[:half] + sums[half:]
    which = iota((half, LANES), 0)
    rows = []
    for q in range(SUB):
        kept = jnp.where(which == tid_ref[q : q + 1, :], sums[:, q * LANES : (q + 1) * LANES], 0.0)
        rows.append(jnp.broadcast_to(jnp.sum(kept, axis=0, keepdims=True), (SUB, LANES)))
    line = compacted(rows)
    out_ref[...] = jnp.broadcast_to(line[None], out_ref.shape)


def pool_kernel(margin_ref, line_ref, flat_ref, tid_ref, out_ref, *factor_out):
    stores = flat_ref.shape[1]
    total = jnp.sum(margin_ref[...], axis=0)
    factor = line_ref[0:1] / total
    if factor_out:
        lane = iota((SUB, LANES), 1)
        index = lane % (LANES // SUB) * SUB + lane // (LANES // SUB)
        factor_out[0][...] = picked(jnp.broadcast_to(factor, (SUB, LANES)), index)[:1]
    spread = expanded(factor)
    half = SUB * SUB
    which = iota((half, LANES), 0)
    columns = []
    for q in range(SUB):
        columns.append(jnp.where(which == tid_ref[q : q + 1, :], spread[q : q + 1, :], 0.0))
    weights = jnp.concatenate(columns, axis=1)
    parts = jnp.concatenate(two_parts(weights), axis=0)
    sums = jnp.dot(parts, flat_ref[...], preferred_element_type=F32)
    sums = sums[:half] + sums[half:]
    row = iota((SUB, LANES), 0)
    base = jnp.broadcast_to(line_ref[1:2], (SUB, LANES))
    count = stores // (LANES // SUB)
    each = out_ref.shape[0] // count
    for t in range(stores // LANES):
        tiles = [sums[d * SUB : (d + 1) * SUB, t * LANES : (t + 1) * LANES] for d in range(SUB)]
        for j, tile in enumerate(swap_blocks(tiles)):
            if each > SLOTS:
                tile = jnp.where(row == BASE_ROW, base, tile)
            at = (t * SUB + j) * each
            out_ref[at : at + each] = tile[:each]


def fitted(merged, cat_goal, day_goal, day):
    width = LANES // SUB
    for _ in range(INNER):
        below = merged * day
        step = LANES // 2
        while step >= width:
            below = below + pltpu.roll(below, step, 1)
            step //= 2
        cat = cat_goal / below
        day = day_goal / jnp.sum(merged * cat, axis=0, keepdims=True)
    return cat, day


def summed(across, taken):
    merged = jnp.dot(across, jnp.concatenate(two_parts(taken), axis=1), preferred_element_type=F32)
    return merged[:, :LANES] + merged[:, LANES:]


def answer(choice, cat, day, out_ref):
    cats = cat.shape[0]
    group = iota(cat.shape, 1) // (LANES // SUB)
    blocks = [jnp.where(group == s, cat, 0.0) for s in range(choice.shape[1] // cats)]
    parts = jnp.concatenate(two_parts(jnp.concatenate(blocks, axis=0)), axis=1)
    rows = jnp.dot(choice, parts, preferred_element_type=F32)
    devices = choice.shape[0]
    out_ref[pl.ds(0, devices, stride=2), :] = jnp.broadcast_to(day, (devices, LANES))
    out_ref[pl.ds(1, devices, stride=2), :] = rows[:, :LANES] + rows[:, LANES:]


def owner_first_kernel(taken_ref, cat_goal_ref, line_ref, out_ref, day_ref, choice_ref, across_ref):
    cats = cat_goal_ref.shape[0]
    devices = choice_ref.shape[0]
    base = taken_ref[pl.ds(BASE_ROW, devices, stride=SUB), :]

    def placed(each, slots):
        rows = devices * each
        at = iota((rows, devices), 0) - iota((rows, devices), 1) * each
        spread = jnp.dot(
            ((at >= 0) & (at < each)).astype(F32).astype(BF16), base.astype(BF16), preferred_element_type=F32
        ).astype(jnp.int32)
        slot = jnp.sum(jnp.where((at >= 0) & (at < each), at, 0), axis=1, keepdims=True)
        hit = (spread + slot == iota((rows, LANES), 1)) & (slot < slots)
        return hit.astype(F32).T[:cats].astype(BF16)

    across_ref[...] = placed(SLOTS, SLOTS)
    per = LANES // cats
    lane = iota((devices, LANES), 1)
    number = base.astype(jnp.int32)
    for n in range(choice_ref.shape[1] // LANES):
        slot = n * per + lane // cats
        hit = (number + slot == lane % cats) & (slot < SLOTS)
        choice_ref[:, n * LANES : (n + 1) * LANES] = hit.astype(F32).astype(BF16)
    merged = summed(placed(SUB, SLOTS), taken_ref[...])
    cat, day = fitted(merged, cat_goal_ref[...], line_ref[2:3], jnp.ones((1, LANES), F32))
    day_ref[...] = day
    answer(choice_ref[...], cat, day, out_ref)


def owner_kernel(taken_ref, cat_goal_ref, line_ref, day_ref, choice_ref, across_ref, out_ref, day_out_ref):
    merged = summed(across_ref[...], taken_ref[...])
    cat, day = fitted(merged, cat_goal_ref[...], line_ref[2:3], day_ref[...])
    day_out_ref[...] = day
    answer(choice_ref[...], cat, day, out_ref)


def owner_last_kernel(taken_ref, cat_goal_ref, line_ref, day_ref, across_ref, out_ref):
    merged = summed(across_ref[...], taken_ref[...])
    cat, day = fitted(merged, cat_goal_ref[...], line_ref[2:3], day_ref[...])
    group = iota((SUB, LANES), 1) // (LANES // SUB)
    tile = cat[:SUB]
    for d in range(1, SUB):
        tile = jnp.where(group == d, cat[d * SUB : (d + 1) * SUB], tile)
    both = jnp.concatenate([tile, day], axis=0)
    each = both.shape[0]
    for j in range(out_ref.shape[0] // each):
        out_ref[j * each : (j + 1) * each] = both


def closing_kernel(
    group_hbm, factor_hbm, back_ref, x_ref, cat_hbm, day_hbm, out_hbm,
    group_ref, factor_ref, cat_ref, day_ref, scale_ref, buf_ref, sems, out_sems,
):
    items, _, stores = x_ref.shape
    loads = [
        pltpu.make_async_copy(group_hbm, group_ref, sems.at[0]),
        pltpu.make_async_copy(factor_hbm, factor_ref, sems.at[1]),
    ]
    for copy in loads:
        copy.start()
    each = SUB + 1
    for t in range(stores // LANES):
        here = slice(t * LANES, (t + 1) * LANES)
        tiles = swap_blocks([back_ref[(t * SUB + j) * each : (t * SUB + j) * each + SUB] for j in range(SUB)])
        cat_ref[:, here] = jnp.concatenate(tiles, axis=0)
        day_ref[:, here] = swap_within(back_ref[pl.ds(t * SUB * each + SUB, SUB, stride=each), :])
    stores_out = [
        pltpu.make_async_copy(cat_ref, cat_hbm, sems.at[2]),
        pltpu.make_async_copy(day_ref, day_hbm, sems.at[3]),
    ]
    for copy in stores_out:
        copy.start()
    for copy in loads:
        copy.wait()
    first = group_ref[0, 0]
    last = cat_ref.shape[0] - 1
    for s in range(SLOTS):
        scale_ref[s] = cat_ref[pl.ds(jnp.minimum(first + s, last), 1), :] * day_ref[...]
    chunks = out_sems.shape[0]
    block = items // chunks
    for n in range(chunks):
        for i in range(n * block, (n + 1) * block):
            value = x_ref[i].astype(F32) * factor_ref[0, i] * scale_ref[group_ref[0, i] - first]
            buf_ref[i] = value.astype(BF16)
        rows = pl.ds(n * block, block)
        copy = pltpu.make_async_copy(buf_ref.at[rows], out_hbm.at[rows], out_sems.at[n])
        copy.start()
        stores_out.append(copy)
    for copy in stores_out:
        copy.wait()


def vmem(count):
    return [pl.BlockSpec(memory_space=pltpu.VMEM)] * count


def held(x):
    return pltpu.with_memory_space_constraint(x, pltpu.VMEM)


def far(x):
    return pltpu.with_memory_space_constraint(x, pltpu.HBM)


LIMIT = pltpu.CompilerParams(vmem_limit_bytes=8 * 1024 * 1024)


def call(kernel, out_shape, *args, **options):
    return pl.pallas_call(
        kernel,
        out_shape=out_shape,
        in_specs=vmem(len(args)),
        out_specs=tuple(vmem(len(out_shape))),
        compiler_params=LIMIT,
        **options,
    )(*map(held, args))


def shards(predicted_units, product_group, product_goal, group_outlet_goal, outlet_date_goal):
    items, days, stores = predicted_units.shape
    cats = group_outlet_goal.shape[0]
    owners = lax.axis_size("item")
    beside = lax.axis_size("store")

    def message(each):
        return pltpu.VMEM((owners * each, LANES), F32)

    def exchanged(x):
        sent = x.reshape(owners, 1, x.size // owners)
        return lax.all_to_all(sent, "item", 0, 0, tiled=True).reshape(x.shape)

    margin = pltpu.VMEM((beside, 1, LANES), F32)
    line = pltpu.VMEM((1, LANES), F32)
    tile = pltpu.VMEM((SUB, LANES), jnp.int32)
    per_cat = pltpu.VMEM((cats, LANES), F32)

    flat, part, tid, lines, cat_goal = pl.pallas_call(
        first_kernel,
        out_shape=(
            pltpu.VMEM((items * days, stores), BF16),
            margin,
            tile,
            pltpu.VMEM((SUB, LANES), F32),
            per_cat,
        ),
        in_specs=[pl.BlockSpec(memory_space=pltpu.HBM)] * 5,
        out_specs=tuple(vmem(5)),
        scratch_shapes=[
            pltpu.VMEM(predicted_units.shape, BF16),
            pltpu.VMEM((1, items), jnp.int32),
            pltpu.VMEM((1, items), F32),
            pltpu.VMEM((cats, stores), F32),
            pltpu.VMEM((days, stores), F32),
            pltpu.SemaphoreType.DMA((4,)),
            pltpu.SemaphoreType.DMA((4,)),
        ],
        compiler_params=LIMIT,
        name="first",
    )(
        *map(
            far,
            (
                predicted_units,
                product_group.reshape(1, items),
                product_goal.reshape(1, items),
                group_outlet_goal,
                outlet_date_goal,
            ),
        )
    )
    for n in range(ROUNDS):
        total = lax.all_to_all(part, "store", 0, 0, tiled=True)
        shapes = (message(SLOTS if n else SUB),)
        if n == ROUNDS - 1:
            shapes += (jax.ShapeDtypeStruct((1, LANES), F32),)
        pooled, *factor = call(pool_kernel, shapes, total, lines, flat, tid, name="pool")
        taken = exchanged(pooled)
        if n == ROUNDS - 1:
            break
        if n == 0:
            blocks = -(-SLOTS * cats // LANES)
            shapes = (
                message(2),
                line,
                pltpu.VMEM((owners, blocks * LANES), BF16),
                pltpu.VMEM((cats, owners * SLOTS), BF16),
            )
            back, day, choice, across = call(owner_first_kernel, shapes, taken, cat_goal, lines, name="owner_first")
        else:
            back, day = call(owner_kernel, (message(2), line), taken, cat_goal, lines, day, choice, across, name="owner")
        (part,) = call(margin_kernel, (margin,), exchanged(back), flat, tid, name="margin")

    (back,) = call(
        owner_last_kernel, (message(SUB + 1),), taken, cat_goal, lines, day, across, name="owner_last"
    )
    far_spec = pl.BlockSpec(memory_space=pltpu.HBM)
    group_outlet_factor, outlet_date_factor, adjusted_tensor = pl.pallas_call(
        closing_kernel,
        out_shape=(
            jax.ShapeDtypeStruct((cats, stores), F32),
            jax.ShapeDtypeStruct((days, stores), F32),
            jax.ShapeDtypeStruct((items, days, stores), BF16),
        ),
        in_specs=[far_spec] * 2 + vmem(2),
        out_specs=(far_spec,) * 3,
        scratch_shapes=[
            pltpu.SMEM((1, items), jnp.int32),
            pltpu.SMEM((1, items), F32),
            pltpu.VMEM((cats, stores), F32),
            pltpu.VMEM((days, stores), F32),
            pltpu.VMEM((SUB, days, stores), F32),
            pltpu.VMEM((items, days, stores), BF16),
            pltpu.SemaphoreType.DMA((4,)),
            pltpu.SemaphoreType.DMA((4,)),
        ],
        compiler_params=LIMIT,
        name="closing",
    )(far(product_group.reshape(1, items)), far(factor[0]), held(exchanged(back)), held(predicted_units))
    return (factor[0].reshape(items), group_outlet_factor, outlet_date_factor, adjusted_tensor)


def solution(mesh):
    in_specs = (P("item", None, "store"), P("item"), P("item"), P(None, "store"), P(None, "store"))
    out_specs = (P("item"), P(None, "store"), P(None, "store"), P("item", None, "store"))
    return jax.shard_map(shards, mesh=mesh, in_specs=in_specs, out_specs=out_specs, check_vma=False)
```

```python
import functools

import jax
import jax.numpy as jnp
from jax import lax
from jax.experimental import pallas as pl
from jax.experimental.pallas import tpu as pltpu
from jax.sharding import PartitionSpec as P

ROUNDS = 4
INNER = 3
LANES = 128
SUB = 8
SLOTS = 5
BASE_ROW = 7

F32 = jnp.float32
BF16 = jnp.bfloat16


def iota(shape, dim):
    return lax.broadcasted_iota(jnp.int32, shape, dim)


def two_parts(x):
    high = x.astype(BF16)
    low = (x - high.astype(F32)).astype(BF16)
    return high, low


def swap_blocks(tiles):
    count = len(tiles)
    width = LANES // count
    group = iota(tiles[0].shape, 1) // width
    bit = 1
    while bit < count:
        low = (group & bit) == 0
        fresh = []
        for a in range(count):
            other = tiles[a ^ bit]
            if a & bit == 0:
                fresh.append(jnp.where(low, tiles[a], pltpu.roll(other, bit * width, 1)))
            else:
                fresh.append(jnp.where(low, pltpu.roll(other, LANES - bit * width, 1), tiles[a]))
        tiles = fresh
        bit *= 2
    return tiles


def swap_within(x):
    width = LANES // SUB
    row, group = iota(x.shape, 0), iota(x.shape, 1) // width
    for bit in (1, 2, 4):
        low, same = (row & bit) == 0, (row & bit) == (group & bit)
        above = pltpu.roll(pltpu.roll(x, SUB - bit, 0), bit * width, 1)
        if 2 * bit == SUB:
            x = jnp.where(same, x, above)
        else:
            below = pltpu.roll(pltpu.roll(x, bit, 0), LANES - bit * width, 1)
            x = jnp.where(same, x, jnp.where(low, above, below))
    return x


def eight_sum(x):
    lane = iota(x.shape, 1)
    for bit in (1, 2, 4):
        x = x + jnp.where((lane & bit) == 0, pltpu.roll(x, LANES - bit, 1), pltpu.roll(x, bit, 1))
    return x


def compacted(rows):
    row = iota((SUB, LANES), 0)
    tile = rows[0]
    for q in range(1, SUB):
        tile = jnp.where(row == q, rows[q], tile)
    tile = eight_sum(tile)
    kept = jnp.where((iota((SUB, LANES), 1) & 7) == row, tile, 0.0)
    return jnp.sum(kept, axis=0, keepdims=True)


def picked(x, index):
    return jnp.take_along_axis(x, index, axis=1)


def first_kernel(
    x_hbm, group_hbm, goal_hbm, cat_all_hbm, day_all_hbm,
    rows_ref, out_ref, slot_ref, line_ref, cat_goal_ref,
    x_buf, group_ref, goal_ref, cat_all_ref, day_all_ref, sems, small_sems,
):
    items, days, stores = x_hbm.shape
    chunks = sems.shape[0]
    block = items // chunks
    small = []
    for n, (src, dst) in enumerate(
        ((group_hbm, group_ref), (goal_hbm, goal_ref), (cat_all_hbm, cat_all_ref), (day_all_hbm, day_all_ref))
    ):
        small.append(pltpu.make_async_copy(src, dst, small_sems.at[n]))
        small[n].start()
    copies = []
    for n in range(chunks):
        rows = pl.ds(n * block, block)
        copies.append(pltpu.make_async_copy(x_hbm.at[rows], x_buf.at[rows], sems.at[n]))
        copies[n].start()
    for copy in small:
        copy.wait()

    row, lane = iota((SUB, LANES), 0), iota((SUB, LANES), 1)
    group = jnp.broadcast_to(group_ref[...], (SUB, LANES))
    first = picked(group, jnp.zeros_like(lane))
    slot_ref[...] = group - first
    line_ref[0:1] = goal_ref[...]
    line_ref[1:2] = first[:1].astype(F32)
    width = LANES // days
    at = lax.axis_index("item") * width
    there = pl.ds(pl.multiple_of(at // LANES * LANES, LANES), LANES)
    index = at % LANES + lane % width
    for k in range(cat_goal_ref.shape[0] // SUB):
        rows = slice(k * SUB, (k + 1) * SUB)
        cat_goal_ref[rows] = picked(cat_all_ref[rows, there], index)
    day_goal = jnp.where(lane // width == row, picked(day_all_ref[:, there], index), 0.0)
    line_ref[2:3] = jnp.sum(day_goal, axis=0, keepdims=True)

    tiles = []
    for n in range(chunks):
        copies[n].wait()
        x = x_buf[n * block : (n + 1) * block].astype(F32).reshape(block * days, stores)
        for t in range(stores // LANES):
            at = (t * items + n * block) * days
            rows_ref[at : at + block * days] = x[:, t * LANES : (t + 1) * LANES]
        sums = lax.dot_general(
            jnp.ones((SUB, stores), BF16), x.astype(BF16), (((1,), (1,)), ((), ())), preferred_element_type=F32
        )
        tiles += [sums[:, q * LANES : (q + 1) * LANES] for q in range(block * days // LANES)]
    line = jnp.broadcast_to(compacted(tiles), (SUB, LANES))
    half = LANES // SUB
    line = picked(line, lane % half * SUB + lane // half)[:1]
    out_ref[...] = jnp.broadcast_to(line[None], out_ref.shape)


def spread_kernel(rows_ref, out_ref):
    tall = 2 * SUB
    items, columns = out_ref.shape

    def step(n, carry):
        into = pl.ds(pl.multiple_of(n * tall, tall), tall)
        for t in range(columns // (SUB * LANES)):
            at = (t * items + n * tall) * SUB
            tiles = [rows_ref[pl.ds(at + d, tall, stride=SUB), :] for d in range(SUB)]
            for j, tile in enumerate(swap_blocks(tiles)):
                at = (t * SUB + j) * LANES
                out_ref[into, at : at + LANES] = tile.astype(BF16)
        return carry

    lax.fori_loop(0, items // tall, step, 0)


def margin_kernel(back_ref, wide_ref, slot_ref, out_ref):
    count = wide_ref.shape[1] // LANES
    tiles = []
    for j in range(count):
        at = min(j * SLOTS, count * SLOTS - SUB)
        tile = back_ref[at : at + SUB]
        if at < j * SLOTS:
            tile = pltpu.roll(tile, SUB - (j * SLOTS - at), 0)
        tiles.append(tile)
    parts = jnp.concatenate(two_parts(jnp.concatenate(tiles, axis=1)), axis=0)
    sums = lax.dot_general(parts, wide_ref[...], (((1,), (1,)), ((), ())), preferred_element_type=F32)
    sums = sums[:SUB] + sums[SUB:]
    kept = jnp.where(iota((SUB, LANES), 0) == slot_ref[...], sums, 0.0)
    line = jnp.sum(kept, axis=0, keepdims=True)
    out_ref[...] = jnp.broadcast_to(line[None], out_ref.shape)


def pool_kernel(margin_ref, line_ref, wide_ref, slot_ref, out_ref, *factor_out):
    total = jnp.sum(margin_ref[...], axis=0)
    factor = line_ref[0:1] / total
    if factor_out:
        factor_out[0][...] = factor
    row = iota((SUB, LANES), 0)
    weights = jnp.where(row == slot_ref[...], factor, 0.0)
    parts = jnp.concatenate(two_parts(weights), axis=0)
    sums = jnp.dot(parts, wide_ref[...], preferred_element_type=F32)
    sums = sums[:SUB] + sums[SUB:]
    count = wide_ref.shape[1] // LANES
    each = out_ref.shape[0] // count
    base = jnp.broadcast_to(line_ref[1:2], (SUB, LANES))
    for j in range(count):
        tile = sums[:, j * LANES : (j + 1) * LANES]
        if each > SLOTS:
            tile = jnp.where(row == BASE_ROW, base, tile)
        out_ref[j * each : (j + 1) * each] = tile[:each]


def fitted(merged, cat_goal, day_goal, day):
    width = LANES // SUB
    for _ in range(INNER):
        below = merged * day
        step = LANES // 2
        while step >= width:
            below = below + pltpu.roll(below, step, 1)
            step //= 2
        cat = cat_goal / below
        day = day_goal / jnp.sum(merged * cat, axis=0, keepdims=True)
    return cat, day


def summed(across, taken):
    merged = jnp.dot(across, jnp.concatenate(two_parts(taken), axis=1), preferred_element_type=F32)
    return merged[:, :LANES] + merged[:, LANES:]


def answer(place, cat, day, out_ref):
    cats = cat.shape[0]
    product = jnp.concatenate([cat * day, jnp.zeros((LANES - cats, LANES), F32)], axis=0)
    parts = jnp.concatenate(two_parts(product), axis=1)
    sent = jnp.dot(place, parts, preferred_element_type=F32)
    out_ref[...] = sent[:, :LANES] + sent[:, LANES:]


def owner_first_kernel(taken_ref, cat_goal_ref, line_ref, out_ref, day_ref, place_ref, across_ref):
    cats = cat_goal_ref.shape[0]
    devices = taken_ref.shape[0] // SUB
    base = taken_ref[pl.ds(BASE_ROW, devices, stride=SUB), :]

    def placed(each):
        rows = devices * each
        at = iota((rows, devices), 0) - iota((rows, devices), 1) * each
        own = (at >= 0) & (at < each)
        spread = jnp.dot(own.astype(F32).astype(BF16), base.astype(BF16), preferred_element_type=F32)
        slot = jnp.sum(jnp.where(own, at, 0), axis=1, keepdims=True)
        hit = (spread.astype(jnp.int32) + slot == iota((rows, LANES), 1)) & (slot < SLOTS)
        return hit.astype(F32)

    place = placed(SLOTS)
    across_ref[...] = place.T[:cats].astype(BF16)
    place_ref[...] = place.astype(BF16)
    merged = summed(placed(SUB).T[:cats].astype(BF16), taken_ref[...])
    cat, day = fitted(merged, cat_goal_ref[...], line_ref[2:3], jnp.ones((1, LANES), F32))
    day_ref[...] = day
    answer(place_ref[...], cat, day, out_ref)


def owner_kernel(taken_ref, cat_goal_ref, line_ref, day_ref, place_ref, across_ref, out_ref, day_out_ref):
    merged = summed(across_ref[...], taken_ref[...])
    cat, day = fitted(merged, cat_goal_ref[...], line_ref[2:3], day_ref[...])
    day_out_ref[...] = day
    answer(place_ref[...], cat, day, out_ref)


def owner_last_kernel(taken_ref, cat_goal_ref, line_ref, day_ref, across_ref, out_ref):
    merged = summed(across_ref[...], taken_ref[...])
    cat, day = fitted(merged, cat_goal_ref[...], line_ref[2:3], day_ref[...])
    group = iota((SUB, LANES), 1) // (LANES // SUB)
    tile = cat[:SUB]
    for d in range(1, SUB):
        tile = jnp.where(group == d, cat[d * SUB : (d + 1) * SUB], tile)
    both = jnp.concatenate([tile, day], axis=0)
    each = both.shape[0]
    for j in range(out_ref.shape[0] // each):
        out_ref[j * each : (j + 1) * each] = both


def closing_kernel(
    group_hbm, factor_vmem, back_ref, x_ref, factor_hbm, cat_hbm, day_hbm, out_hbm,
    group_ref, factor_ref, cat_ref, day_ref, scale_ref, buf_ref, sems, out_sems,
):
    items, _, stores = x_ref.shape
    loads = [
        pltpu.make_async_copy(group_hbm, group_ref, sems.at[0]),
        pltpu.make_async_copy(factor_vmem, factor_ref, sems.at[1]),
    ]
    for copy in loads:
        copy.start()
    each = SUB + 1
    for t in range(stores // LANES):
        here = slice(t * LANES, (t + 1) * LANES)
        tiles = swap_blocks([back_ref[(t * SUB + j) * each : (t * SUB + j) * each + SUB] for j in range(SUB)])
        cat_ref[:, here] = jnp.concatenate(tiles, axis=0)
        day_ref[:, here] = swap_within(back_ref[pl.ds(t * SUB * each + SUB, SUB, stride=each), :])
    stores_out = [
        pltpu.make_async_copy(factor_vmem, factor_hbm, sems.at[4]),
        pltpu.make_async_copy(cat_ref, cat_hbm, sems.at[2]),
        pltpu.make_async_copy(day_ref, day_hbm, sems.at[3]),
    ]
    for copy in stores_out:
        copy.start()
    for copy in loads:
        copy.wait()
    first = group_ref[0, 0]
    last = cat_ref.shape[0] - 1
    for s in range(SLOTS):
        scale_ref[s] = cat_ref[pl.ds(jnp.minimum(first + s, last), 1), :] * day_ref[...]
    chunks = out_sems.shape[0]
    block = items // chunks
    for n in range(chunks):
        for i in range(n * block, (n + 1) * block):
            value = x_ref[i].astype(F32) * factor_ref[0, i] * scale_ref[group_ref[0, i] - first]
            buf_ref[i] = value.astype(BF16)
        rows = pl.ds(n * block, block)
        copy = pltpu.make_async_copy(buf_ref.at[rows], out_hbm.at[rows], out_sems.at[n])
        copy.start()
        stores_out.append(copy)
    for copy in stores_out:
        copy.wait()


def vmem(count):
    return [pl.BlockSpec(memory_space=pltpu.VMEM)] * count


def held(x):
    return pltpu.with_memory_space_constraint(x, pltpu.VMEM)


def far(x):
    return pltpu.with_memory_space_constraint(x, pltpu.HBM)


LIMIT = pltpu.CompilerParams(vmem_limit_bytes=8 * 1024 * 1024)


def call(kernel, out_shape, *args, **options):
    return pl.pallas_call(
        kernel,
        out_shape=out_shape,
        in_specs=vmem(len(args)),
        out_specs=tuple(vmem(len(out_shape))),
        compiler_params=LIMIT,
        **options,
    )(*map(held, args))


def shards(predicted_units, product_group, product_goal, group_outlet_goal, outlet_date_goal):
    items, days, stores = predicted_units.shape
    cats = group_outlet_goal.shape[0]
    owners = lax.axis_size("item")
    beside = lax.axis_size("store")

    def message(each):
        return pltpu.VMEM((owners * each, LANES), F32)

    def exchanged(x):
        sent = x.reshape(owners, 1, x.size // owners)
        return lax.all_to_all(sent, "item", 0, 0, tiled=True).reshape(x.shape)

    margin = pltpu.VMEM((beside, 1, LANES), F32)
    line = pltpu.VMEM((1, LANES), F32)
    tile = pltpu.VMEM((SUB, LANES), jnp.int32)
    per_cat = pltpu.VMEM((cats, LANES), F32)

    rows, part, slot, lines, cat_goal = pl.pallas_call(
        first_kernel,
        out_shape=(
            pltpu.VMEM((items * days * stores // LANES, LANES), F32),
            margin,
            tile,
            pltpu.VMEM((SUB, LANES), F32),
            per_cat,
        ),
        in_specs=[pl.BlockSpec(memory_space=pltpu.HBM)] * 5,
        out_specs=tuple(vmem(5)),
        scratch_shapes=[
            pltpu.VMEM(predicted_units.shape, BF16),
            pltpu.VMEM((1, items), jnp.int32),
            pltpu.VMEM((1, items), F32),
            pltpu.VMEM((cats, stores), F32),
            pltpu.VMEM((days, stores), F32),
            pltpu.SemaphoreType.DMA((4,)),
            pltpu.SemaphoreType.DMA((4,)),
        ],
        compiler_params=LIMIT,
        name="first",
    )(
        *map(
            far,
            (
                predicted_units,
                product_group.reshape(1, items),
                product_goal.reshape(1, items),
                group_outlet_goal,
                outlet_date_goal,
            ),
        )
    )
    (wide,) = call(spread_kernel, (pltpu.VMEM((items, days * stores), BF16),), rows, name="spread")
    for n in range(ROUNDS):
        total = lax.all_to_all(part, "store", 0, 0, tiled=True)
        shapes = (message(SLOTS if n else SUB),)
        if n == ROUNDS - 1:
            shapes += (line,)
        pooled, *factor = call(pool_kernel, shapes, total, lines, wide, slot, name="pool")
        taken = exchanged(pooled)
        if n == ROUNDS - 1:
            break
        if n == 0:
            shapes = (
                message(SLOTS),
                line,
                pltpu.VMEM((owners * SLOTS, LANES), BF16),
                pltpu.VMEM((cats, owners * SLOTS), BF16),
            )
            back, day, place, across = call(owner_first_kernel, shapes, taken, cat_goal, lines, name="owner_first")
        else:
            shapes = (message(SLOTS), line)
            back, day = call(owner_kernel, shapes, taken, cat_goal, lines, day, place, across, name="owner")
        (part,) = call(margin_kernel, (margin,), exchanged(back), wide, slot, name="margin")

    (back,) = call(
        owner_last_kernel, (message(SUB + 1),), taken, cat_goal, lines, day, across, name="owner_last"
    )
    far_spec = pl.BlockSpec(memory_space=pltpu.HBM)
    product_factor, group_outlet_factor, outlet_date_factor, adjusted_tensor = pl.pallas_call(
        closing_kernel,
        out_shape=(
            jax.ShapeDtypeStruct((1, items), F32),
            jax.ShapeDtypeStruct((cats, stores), F32),
            jax.ShapeDtypeStruct((days, stores), F32),
            jax.ShapeDtypeStruct((items, days, stores), BF16),
        ),
        in_specs=[far_spec] + vmem(3),
        out_specs=(far_spec,) * 4,
        scratch_shapes=[
            pltpu.SMEM((1, items), jnp.int32),
            pltpu.SMEM((1, items), F32),
            pltpu.VMEM((cats, stores), F32),
            pltpu.VMEM((days, stores), F32),
            pltpu.VMEM((SUB, days, stores), F32),
            pltpu.VMEM((items, days, stores), BF16),
            pltpu.SemaphoreType.DMA((5,)),
            pltpu.SemaphoreType.DMA((4,)),
        ],
        compiler_params=LIMIT,
        name="closing",
    )(far(product_group.reshape(1, items)), held(factor[0]), held(exchanged(back)), held(predicted_units))
    return (product_factor.reshape(items), group_outlet_factor, outlet_date_factor, adjusted_tensor)


def solution(mesh):
    in_specs = (P("item", None, "store"), P("item"), P("item"), P(None, "store"), P(None, "store"))
    out_specs = (P("item"), P(None, "store"), P(None, "store"), P("item", None, "store"))
    return jax.shard_map(shards, mesh=mesh, in_specs=in_specs, out_specs=out_specs, check_vma=False)
```

```python
import functools

import jax
import jax.numpy as jnp
from jax import lax
from jax.experimental import pallas as pl
from jax.experimental.pallas import tpu as pltpu
from jax.sharding import PartitionSpec as P

ROUNDS = 4
INNER = 3
LANES = 128
SUB = 8
SLOTS = 5
BASE_ROW = 7

F32 = jnp.float32
BF16 = jnp.bfloat16


def iota(shape, dim):
    return lax.broadcasted_iota(jnp.int32, shape, dim)


def two_parts(x):
    high = x.astype(BF16)
    low = (x - high.astype(F32)).astype(BF16)
    return high, low


def swap_blocks(tiles):
    count = len(tiles)
    width = LANES // count
    group = iota(tiles[0].shape, 1) // width
    bit = 1
    while bit < count:
        low = (group & bit) == 0
        fresh = []
        for a in range(count):
            other = tiles[a ^ bit]
            if a & bit == 0:
                fresh.append(jnp.where(low, tiles[a], pltpu.roll(other, bit * width, 1)))
            else:
                fresh.append(jnp.where(low, pltpu.roll(other, LANES - bit * width, 1), tiles[a]))
        tiles = fresh
        bit *= 2
    return tiles


def swap_within(x):
    width = LANES // SUB
    row, group = iota(x.shape, 0), iota(x.shape, 1) // width
    for bit in (1, 2, 4):
        low, same = (row & bit) == 0, (row & bit) == (group & bit)
        above = pltpu.roll(pltpu.roll(x, SUB - bit, 0), bit * width, 1)
        if 2 * bit == SUB:
            x = jnp.where(same, x, above)
        else:
            below = pltpu.roll(pltpu.roll(x, bit, 0), LANES - bit * width, 1)
            x = jnp.where(same, x, jnp.where(low, above, below))
    return x


def picked(x, index):
    return jnp.take_along_axis(x, index, axis=1)


def first_kernel(x_hbm, x_ref, out_ref, sems):
    items, days, stores = x_hbm.shape
    chunks = sems.shape[0]
    block = items // chunks
    copies = []
    for n in range(chunks):
        rows = pl.ds(n * block, block)
        copies.append(pltpu.make_async_copy(x_hbm.at[rows], x_ref.at[rows], sems.at[n]))
        copies[n].start()
    row, lane = iota((SUB, LANES), 0), iota((SUB, LANES), 1)
    half = items // SUB
    gather = (iota((LANES, LANES), 0) // days == iota((LANES, LANES), 1) % half).astype(F32).astype(BF16)
    tile, q = jnp.zeros((SUB, LANES), F32), 0
    for n in range(chunks):
        copies[n].wait()
        x = x_ref[n * block : (n + 1) * block].astype(F32).reshape(block * days, stores)
        sums = lax.dot_general(
            jnp.ones((SUB, stores), BF16), x.astype(BF16), (((1,), (1,)), ((), ())), preferred_element_type=F32
        )
        for at in range(0, block * days, LANES):
            tile = jnp.where(row == q, sums[:, at : at + LANES], tile)
            q += 1
    each = jnp.dot(jnp.concatenate(two_parts(tile), axis=0), gather, preferred_element_type=F32)
    kept = jnp.where(lane // half == row, each[:SUB] + each[SUB:], 0.0)
    line = jnp.sum(kept, axis=0, keepdims=True)
    out_ref[...] = jnp.broadcast_to(line[None], out_ref.shape)


def spread_kernel(
    x_ref, group_hbm, goal_hbm, cat_all_hbm, day_all_hbm,
    wide_ref, slot_ref, line_ref, cat_goal_ref,
    rows_ref, group_ref, goal_ref, cat_all_ref, day_all_ref, sems,
):
    pairs = ((group_hbm, group_ref), (goal_hbm, goal_ref), (cat_all_hbm, cat_all_ref), (day_all_hbm, day_all_ref))
    copies = [pltpu.make_async_copy(src, dst, sems.at[n]) for n, (src, dst) in enumerate(pairs)]
    for copy in copies:
        copy.start()
    items, days, stores = x_ref.shape
    tall = 2 * SUB

    def step(n, carry):
        into = pl.ds(pl.multiple_of(n * tall, tall), tall)
        x = x_ref[into].astype(F32).reshape(tall * days, stores)
        for t in range(stores // LANES):
            at = (t * items + n * tall) * days
            rows_ref[pl.ds(pl.multiple_of(at, SUB), tall * days), :] = x[:, t * LANES : (t + 1) * LANES]
            tiles = [rows_ref[pl.ds(at + d, tall, stride=days), :] for d in range(days)]
            for j, tile in enumerate(swap_blocks(tiles)):
                column = (t * SUB + j) * LANES
                wide_ref[into, column : column + LANES] = tile.astype(BF16)
        return carry

    lax.fori_loop(0, items // tall, step, 0)
    for copy in copies:
        copy.wait()
    row, lane = iota((SUB, LANES), 0), iota((SUB, LANES), 1)
    group = jnp.broadcast_to(group_ref[...], (SUB, LANES))
    first = picked(group, jnp.zeros_like(lane))
    slot_ref[...] = group - first
    line_ref[0:1] = goal_ref[...]
    line_ref[1:2] = first[:1].astype(F32)
    width = LANES // days
    at = lax.axis_index("item") * width
    there = pl.ds(pl.multiple_of(at // LANES * LANES, LANES), LANES)
    index = at % LANES + lane % width
    for k in range(cat_goal_ref.shape[0] // SUB):
        rows = slice(k * SUB, (k + 1) * SUB)
        cat_goal_ref[rows] = picked(cat_all_ref[rows, there], index)
    day_goal = jnp.where(lane // width == row, picked(day_all_ref[:, there], index), 0.0)
    line_ref[2:3] = jnp.sum(day_goal, axis=0, keepdims=True)


def margin_kernel(back_ref, wide_ref, slot_ref, out_ref):
    count = wide_ref.shape[1] // LANES
    tiles = []
    for j in range(count):
        at = min(j * SLOTS, count * SLOTS - SUB)
        tile = back_ref[at : at + SUB]
        if at < j * SLOTS:
            tile = pltpu.roll(tile, SUB - (j * SLOTS - at), 0)
        tiles.append(tile)
    parts = jnp.concatenate(two_parts(jnp.concatenate(tiles, axis=1)), axis=0)
    sums = lax.dot_general(parts, wide_ref[...], (((1,), (1,)), ((), ())), preferred_element_type=F32)
    sums = sums[:SUB] + sums[SUB:]
    kept = jnp.where(iota((SUB, LANES), 0) == slot_ref[...], sums, 0.0)
    line = jnp.sum(kept, axis=0, keepdims=True)
    out_ref[...] = jnp.broadcast_to(line[None], out_ref.shape)


def pool_kernel(margin_ref, line_ref, wide_ref, slot_ref, out_ref, *factor_out):
    total = jnp.sum(margin_ref[...], axis=0)
    factor = line_ref[0:1] / total
    if factor_out:
        factor_out[0][...] = factor
    row = iota((SUB, LANES), 0)
    weights = jnp.where(row == slot_ref[...], factor, 0.0)
    parts = jnp.concatenate(two_parts(weights), axis=0)
    sums = jnp.dot(parts, wide_ref[...], preferred_element_type=F32)
    sums = sums[:SUB] + sums[SUB:]
    count = wide_ref.shape[1] // LANES
    each = out_ref.shape[0] // count
    base = jnp.broadcast_to(line_ref[1:2], (SUB, LANES))
    for j in range(count):
        tile = sums[:, j * LANES : (j + 1) * LANES]
        if each > SLOTS:
            tile = jnp.where(row == BASE_ROW, base, tile)
        out_ref[j * each : (j + 1) * each] = tile[:each]


def fitted(merged, cat_goal, day_goal, day):
    width = LANES // SUB
    for _ in range(INNER):
        below = merged * day
        turned = [below] + [pltpu.roll(below, n * width, 1) for n in range(1, SUB)]
        while len(turned) > 1:
            turned = [turned[n] + turned[n + 1] for n in range(0, len(turned), 2)]
        cat = cat_goal / turned[0]
        day = day_goal / jnp.sum(merged * cat, axis=0, keepdims=True)
    return cat, day


def summed(across, taken):
    merged = jnp.dot(across, jnp.concatenate(two_parts(taken), axis=1), preferred_element_type=F32)
    return merged[:, :LANES] + merged[:, LANES:]


def answer(place, cat, day, out_ref):
    parts = jnp.concatenate(two_parts(cat * day), axis=0)
    out_ref[...] = jnp.dot(place, parts, preferred_element_type=F32)


def owner_first_kernel(taken_ref, cat_goal_ref, line_ref, out_ref, day_ref, place_ref, across_ref):
    cats = cat_goal_ref.shape[0]
    devices = taken_ref.shape[0] // SUB
    base = taken_ref[pl.ds(BASE_ROW, devices, stride=SUB), :]

    def placed(each):
        rows = devices * each
        at = iota((rows, devices), 0) - iota((rows, devices), 1) * each
        own = (at >= 0) & (at < each)
        spread = jnp.dot(own.astype(F32).astype(BF16), base.astype(BF16), preferred_element_type=F32)
        slot = jnp.sum(jnp.where(own, at, 0), axis=1, keepdims=True)
        lane = iota((rows, LANES), 1)
        hit = (spread.astype(jnp.int32) + slot == lane % cats) & (slot < SLOTS)
        return hit.astype(F32)

    place = placed(SLOTS)
    across_ref[...] = place.T[:cats].astype(BF16)
    place_ref[...] = place.astype(BF16)
    merged = summed(placed(SUB).T[:cats].astype(BF16), taken_ref[...])
    cat, day = fitted(merged, cat_goal_ref[...], line_ref[2:3], jnp.ones((1, LANES), F32))
    day_ref[...] = day
    answer(place_ref[...], cat, day, out_ref)


def owner_kernel(taken_ref, cat_goal_ref, line_ref, day_ref, place_ref, across_ref, out_ref, day_out_ref):
    merged = summed(across_ref[...], taken_ref[...])
    cat, day = fitted(merged, cat_goal_ref[...], line_ref[2:3], day_ref[...])
    day_out_ref[...] = day
    answer(place_ref[...], cat, day, out_ref)


def owner_last_kernel(taken_ref, cat_goal_ref, line_ref, day_ref, across_ref, out_ref):
    merged = summed(across_ref[...], taken_ref[...])
    cat, day = fitted(merged, cat_goal_ref[...], line_ref[2:3], day_ref[...])
    group = iota((SUB, LANES), 1) // (LANES // SUB)
    tile = cat[:SUB]
    for d in range(1, SUB):
        tile = jnp.where(group == d, cat[d * SUB : (d + 1) * SUB], tile)
    both = jnp.concatenate([tile, day], axis=0)
    each = both.shape[0]
    for j in range(out_ref.shape[0] // each):
        out_ref[j * each : (j + 1) * each] = both


def closing_kernel(
    group_hbm, factor_vmem, back_ref, x_ref, factor_hbm, cat_hbm, day_hbm, out_hbm,
    group_ref, factor_ref, cat_ref, day_ref, scale_ref, buf_ref, sems, out_sems,
):
    items, _, stores = x_ref.shape
    loads = [
        pltpu.make_async_copy(group_hbm, group_ref, sems.at[0]),
        pltpu.make_async_copy(factor_vmem, factor_ref, sems.at[1]),
    ]
    for copy in loads:
        copy.start()
    each = SUB + 1
    for t in range(stores // LANES):
        here = slice(t * LANES, (t + 1) * LANES)
        tiles = swap_blocks([back_ref[(t * SUB + j) * each : (t * SUB + j) * each + SUB] for j in range(SUB)])
        cat_ref[:, here] = jnp.concatenate(tiles, axis=0)
        day_ref[:, here] = swap_within(back_ref[pl.ds(t * SUB * each + SUB, SUB, stride=each), :])
    stores_out = [
        pltpu.make_async_copy(factor_vmem, factor_hbm, sems.at[4]),
        pltpu.make_async_copy(cat_ref, cat_hbm, sems.at[2]),
        pltpu.make_async_copy(day_ref, day_hbm, sems.at[3]),
    ]
    for copy in stores_out:
        copy.start()
    for copy in loads:
        copy.wait()
    first = group_ref[0, 0]
    last = cat_ref.shape[0] - 1
    for s in range(SLOTS):
        scale_ref[s] = cat_ref[pl.ds(jnp.minimum(first + s, last), 1), :] * day_ref[...]
    chunks = out_sems.shape[0]
    block = items // chunks
    for n in range(chunks):
        for i in range(n * block, (n + 1) * block):
            value = x_ref[i].astype(F32) * factor_ref[0, i] * scale_ref[group_ref[0, i] - first]
            buf_ref[i] = value.astype(BF16)
        rows = pl.ds(n * block, block)
        copy = pltpu.make_async_copy(buf_ref.at[rows], out_hbm.at[rows], out_sems.at[n])
        copy.start()
        stores_out.append(copy)
    for copy in stores_out:
        copy.wait()


def vmem(count):
    return [pl.BlockSpec(memory_space=pltpu.VMEM)] * count


def held(x):
    return pltpu.with_memory_space_constraint(x, pltpu.VMEM)


def far(x):
    return pltpu.with_memory_space_constraint(x, pltpu.HBM)


LIMIT = pltpu.CompilerParams(vmem_limit_bytes=8 * 1024 * 1024)


def call(kernel, out_shape, *args, **options):
    return pl.pallas_call(
        kernel,
        out_shape=out_shape,
        in_specs=vmem(len(args)),
        out_specs=tuple(vmem(len(out_shape))),
        compiler_params=LIMIT,
        **options,
    )(*map(held, args))


def shards(predicted_units, product_group, product_goal, group_outlet_goal, outlet_date_goal):
    items, days, stores = predicted_units.shape
    cats = group_outlet_goal.shape[0]
    owners = lax.axis_size("item")
    beside = lax.axis_size("store")

    def message(each):
        return pltpu.VMEM((owners * each, LANES), F32)

    def exchanged(x):
        sent = x.reshape(owners, 1, x.size // owners)
        return lax.all_to_all(sent, "item", 0, 0, tiled=True).reshape(x.shape)

    margin = pltpu.VMEM((beside, 1, LANES), F32)
    line = pltpu.VMEM((1, LANES), F32)
    tile = pltpu.VMEM((SUB, LANES), jnp.int32)
    per_cat = pltpu.VMEM((cats, LANES), F32)

    far_spec = pl.BlockSpec(memory_space=pltpu.HBM)
    near, part = pl.pallas_call(
        first_kernel,
        out_shape=(pltpu.VMEM(predicted_units.shape, BF16), margin),
        in_specs=[far_spec],
        out_specs=tuple(vmem(2)),
        scratch_shapes=[pltpu.SemaphoreType.DMA((8,))],
        compiler_params=LIMIT,
        name="first",
    )(far(predicted_units))
    wide, slot, lines, cat_goal = pl.pallas_call(
        spread_kernel,
        out_shape=(
            pltpu.VMEM((items, days * stores), BF16),
            tile,
            pltpu.VMEM((SUB, LANES), F32),
            per_cat,
        ),
        in_specs=vmem(1) + [far_spec] * 4,
        out_specs=tuple(vmem(4)),
        scratch_shapes=[
            pltpu.VMEM((items * days * stores // LANES, LANES), F32),
            pltpu.VMEM((1, items), jnp.int32),
            pltpu.VMEM((1, items), F32),
            pltpu.VMEM((cats, stores), F32),
            pltpu.VMEM((days, stores), F32),
            pltpu.SemaphoreType.DMA((4,)),
        ],
        compiler_params=LIMIT,
        name="spread",
    )(
        held(near),
        far(product_group.reshape(1, items)),
        far(product_goal.reshape(1, items)),
        far(group_outlet_goal),
        far(outlet_date_goal),
    )
    for n in range(ROUNDS):
        total = lax.all_to_all(part, "store", 0, 0, tiled=True)
        shapes = (message(SLOTS if n else SUB),)
        if n == ROUNDS - 1:
            shapes += (line,)
        pooled, *factor = call(pool_kernel, shapes, total, lines, wide, slot, name="pool")
        taken = exchanged(pooled)
        if n == ROUNDS - 1:
            break
        if n == 0:
            shapes = (
                message(SLOTS),
                line,
                pltpu.VMEM((owners * SLOTS, LANES), BF16),
                pltpu.VMEM((cats, owners * SLOTS), BF16),
            )
            back, day, place, across = call(owner_first_kernel, shapes, taken, cat_goal, lines, name="owner_first")
        else:
            shapes = (message(SLOTS), line)
            back, day = call(owner_kernel, shapes, taken, cat_goal, lines, day, place, across, name="owner")
        (part,) = call(margin_kernel, (margin,), exchanged(back), wide, slot, name="margin")

    (back,) = call(
        owner_last_kernel, (message(SUB + 1),), taken, cat_goal, lines, day, across, name="owner_last"
    )
    product_factor, group_outlet_factor, outlet_date_factor, adjusted_tensor = pl.pallas_call(
        closing_kernel,
        out_shape=(
            jax.ShapeDtypeStruct((1, items), F32),
            jax.ShapeDtypeStruct((cats, stores), F32),
            jax.ShapeDtypeStruct((days, stores), F32),
            jax.ShapeDtypeStruct((items, days, stores), BF16),
        ),
        in_specs=[far_spec] + vmem(3),
        out_specs=(far_spec,) * 4,
        scratch_shapes=[
            pltpu.SMEM((1, items), jnp.int32),
            pltpu.SMEM((1, items), F32),
            pltpu.VMEM((cats, stores), F32),
            pltpu.VMEM((days, stores), F32),
            pltpu.VMEM((SUB, days, stores), F32),
            pltpu.VMEM((items, days, stores), BF16),
            pltpu.SemaphoreType.DMA((5,)),
            pltpu.SemaphoreType.DMA((4,)),
        ],
        compiler_params=LIMIT,
        name="closing",
    )(far(product_group.reshape(1, items)), held(factor[0]), held(exchanged(back)), held(near))
    return (product_factor.reshape(items), group_outlet_factor, outlet_date_factor, adjusted_tensor)


def solution(mesh):
    in_specs = (P("item", None, "store"), P("item"), P("item"), P(None, "store"), P(None, "store"))
    out_specs = (P("item"), P(None, "store"), P(None, "store"), P("item", None, "store"))
    return jax.shard_map(shards, mesh=mesh, in_specs=in_specs, out_specs=out_specs, check_vma=False)
```

```python
import functools

import jax
import jax.numpy as jnp
from jax import lax
from jax.experimental import pallas as pl
from jax.experimental.pallas import tpu as pltpu
from jax.sharding import PartitionSpec as P

ROUNDS = 4
INNER = 3
LANES = 128
SUB = 8
SLOTS = 5
BASE_ROW = 7

F32 = jnp.float32
BF16 = jnp.bfloat16


def iota(shape, dim):
    return lax.broadcasted_iota(jnp.int32, shape, dim)


def two_parts(x):
    high = x.astype(BF16)
    low = (x - high.astype(F32)).astype(BF16)
    return high, low


def swap_blocks(tiles):
    count = len(tiles)
    width = LANES // count
    group = iota(tiles[0].shape, 1) // width
    bit = 1
    while bit < count:
        low = (group & bit) == 0
        fresh = []
        for a in range(count):
            other = tiles[a ^ bit]
            if a & bit == 0:
                fresh.append(jnp.where(low, tiles[a], pltpu.roll(other, bit * width, 1)))
            else:
                fresh.append(jnp.where(low, pltpu.roll(other, LANES - bit * width, 1), tiles[a]))
        tiles = fresh
        bit *= 2
    return tiles


def swap_within(x):
    width = LANES // SUB
    row, group = iota(x.shape, 0), iota(x.shape, 1) // width
    for bit in (1, 2, 4):
        low, same = (row & bit) == 0, (row & bit) == (group & bit)
        above = pltpu.roll(pltpu.roll(x, SUB - bit, 0), bit * width, 1)
        if 2 * bit == SUB:
            x = jnp.where(same, x, above)
        else:
            below = pltpu.roll(pltpu.roll(x, bit, 0), LANES - bit * width, 1)
            x = jnp.where(same, x, jnp.where(low, above, below))
    return x


def picked(x, index):
    return jnp.take_along_axis(x, index, axis=1)


def first_kernel(x_ref, out_ref):
    items, days, stores = x_ref.shape
    row, lane = iota((SUB, LANES), 0), iota((SUB, LANES), 1)
    half = items // SUB
    gather = (iota((LANES, LANES), 0) // days == iota((LANES, LANES), 1) % half).astype(F32).astype(BF16)
    x = x_ref[...].astype(F32).reshape(items * days, stores).astype(BF16)
    sums = lax.dot_general(
        jnp.ones((SUB, stores), BF16), x, (((1,), (1,)), ((), ())), preferred_element_type=F32
    )
    tile = sums[:, :LANES]
    for q in range(1, SUB):
        tile = jnp.where(row == q, sums[:, q * LANES : (q + 1) * LANES], tile)
    each = jnp.dot(jnp.concatenate(two_parts(tile), axis=0), gather, preferred_element_type=F32)
    kept = jnp.where(lane // half == row, each[:SUB] + each[SUB:], 0.0)
    line = jnp.sum(kept, axis=0, keepdims=True)
    out_ref[...] = jnp.broadcast_to(line[None], out_ref.shape)


def spread_kernel(
    x_ref, group_hbm, goal_hbm, cat_all_hbm, day_all_hbm,
    wide_ref, slot_ref, line_ref, cat_goal_ref,
    rows_ref, group_ref, goal_ref, cat_all_ref, day_all_ref, sems,
):
    pairs = ((group_hbm, group_ref), (goal_hbm, goal_ref), (cat_all_hbm, cat_all_ref), (day_all_hbm, day_all_ref))
    copies = [pltpu.make_async_copy(src, dst, sems.at[n]) for n, (src, dst) in enumerate(pairs)]
    for copy in copies:
        copy.start()
    items, days, stores = x_ref.shape
    tall = 2 * SUB

    def step(n, carry):
        into = pl.ds(pl.multiple_of(n * tall, tall), tall)
        x = x_ref[into].astype(F32).reshape(tall * days, stores)
        for t in range(stores // LANES):
            at = (t * items + n * tall) * days
            rows_ref[pl.ds(pl.multiple_of(at, SUB), tall * days), :] = x[:, t * LANES : (t + 1) * LANES]
            tiles = [rows_ref[pl.ds(at + d, tall, stride=days), :] for d in range(days)]
            for j, tile in enumerate(swap_blocks(tiles)):
                column = (t * SUB + j) * LANES
                wide_ref[into, column : column + LANES] = tile.astype(BF16)
        return carry

    lax.fori_loop(0, items // tall, step, 0)
    for copy in copies:
        copy.wait()
    row, lane = iota((SUB, LANES), 0), iota((SUB, LANES), 1)
    group = jnp.broadcast_to(group_ref[...], (SUB, LANES))
    first = picked(group, jnp.zeros_like(lane))
    slot_ref[...] = group - first
    line_ref[0:1] = goal_ref[...]
    line_ref[1:2] = first[:1].astype(F32)
    width = LANES // days
    at = lax.axis_index("item") * width
    there = pl.ds(pl.multiple_of(at // LANES * LANES, LANES), LANES)
    index = at % LANES + lane % width
    for k in range(cat_goal_ref.shape[0] // SUB):
        rows = slice(k * SUB, (k + 1) * SUB)
        cat_goal_ref[rows] = picked(cat_all_ref[rows, there], index)
    day_goal = jnp.where(lane // width == row, picked(day_all_ref[:, there], index), 0.0)
    line_ref[2:3] = jnp.sum(day_goal, axis=0, keepdims=True)


def margin_kernel(back_ref, wide_ref, slot_ref, out_ref):
    count = wide_ref.shape[1] // LANES
    tiles = []
    for j in range(count):
        at = min(j * SLOTS, count * SLOTS - SUB)
        tile = back_ref[at : at + SUB]
        if at < j * SLOTS:
            tile = pltpu.roll(tile, SUB - (j * SLOTS - at), 0)
        tiles.append(tile)
    parts = jnp.concatenate(two_parts(jnp.concatenate(tiles, axis=1)), axis=0)
    sums = lax.dot_general(parts, wide_ref[...], (((1,), (1,)), ((), ())), preferred_element_type=F32)
    sums = sums[:SUB] + sums[SUB:]
    kept = jnp.where(iota((SUB, LANES), 0) == slot_ref[...], sums, 0.0)
    line = jnp.sum(kept, axis=0, keepdims=True)
    out_ref[...] = jnp.broadcast_to(line[None], out_ref.shape)


def pool_kernel(margin_ref, line_ref, wide_ref, slot_ref, out_ref, *factor_out):
    total = jnp.sum(margin_ref[...], axis=0)
    factor = line_ref[0:1] / total
    if factor_out:
        factor_out[0][...] = factor
    row = iota((SUB, LANES), 0)
    weights = jnp.where(row == slot_ref[...], factor, 0.0)
    parts = jnp.concatenate(two_parts(weights), axis=0)
    sums = jnp.dot(parts, wide_ref[...], preferred_element_type=F32)
    sums = sums[:SUB] + sums[SUB:]
    count = wide_ref.shape[1] // LANES
    each = out_ref.shape[0] // count
    base = jnp.broadcast_to(line_ref[1:2], (SUB, LANES))
    for j in range(count):
        tile = sums[:, j * LANES : (j + 1) * LANES]
        if each > SLOTS:
            tile = jnp.where(row == BASE_ROW, base, tile)
        out_ref[j * each : (j + 1) * each] = tile[:each]


def fitted(merged, cat_goal, day_goal, day):
    width = LANES // SUB
    for _ in range(INNER):
        below = merged * day
        turned = [below] + [pltpu.roll(below, n * width, 1) for n in range(1, SUB)]
        while len(turned) > 1:
            turned = [turned[n] + turned[n + 1] for n in range(0, len(turned), 2)]
        cat = cat_goal / turned[0]
        day = day_goal / jnp.sum(merged * cat, axis=0, keepdims=True)
    return cat, day


def summed(across, taken):
    merged = jnp.dot(across, jnp.concatenate(two_parts(taken), axis=1), preferred_element_type=F32)
    return merged[:, :LANES] + merged[:, LANES:]


def answer(place, cat, day, out_ref):
    parts = jnp.concatenate(two_parts(cat * day), axis=0)
    out_ref[...] = jnp.dot(place, parts, preferred_element_type=F32)


def owner_first_kernel(taken_ref, cat_goal_ref, line_ref, out_ref, day_ref, place_ref, across_ref):
    cats = cat_goal_ref.shape[0]
    devices = taken_ref.shape[0] // SUB
    base = taken_ref[pl.ds(BASE_ROW, devices, stride=SUB), :]

    def placed(each):
        rows = devices * each
        at = iota((rows, devices), 0) - iota((rows, devices), 1) * each
        own = (at >= 0) & (at < each)
        spread = jnp.dot(own.astype(F32).astype(BF16), base.astype(BF16), preferred_element_type=F32)
        slot = jnp.sum(jnp.where(own, at, 0), axis=1, keepdims=True)
        lane = iota((rows, LANES), 1)
        hit = (spread.astype(jnp.int32) + slot == lane % cats) & (slot < SLOTS)
        return hit.astype(F32)

    place = placed(SLOTS)
    across_ref[...] = place.T[:cats].astype(BF16)
    place_ref[...] = place.astype(BF16)
    merged = summed(placed(SUB).T[:cats].astype(BF16), taken_ref[...])
    cat, day = fitted(merged, cat_goal_ref[...], line_ref[2:3], jnp.ones((1, LANES), F32))
    day_ref[...] = day
    answer(place_ref[...], cat, day, out_ref)


def owner_kernel(taken_ref, cat_goal_ref, line_ref, day_ref, place_ref, across_ref, out_ref, day_out_ref):
    merged = summed(across_ref[...], taken_ref[...])
    cat, day = fitted(merged, cat_goal_ref[...], line_ref[2:3], day_ref[...])
    day_out_ref[...] = day
    answer(place_ref[...], cat, day, out_ref)


def owner_last_kernel(taken_ref, cat_goal_ref, line_ref, day_ref, across_ref, out_ref):
    merged = summed(across_ref[...], taken_ref[...])
    cat, day = fitted(merged, cat_goal_ref[...], line_ref[2:3], day_ref[...])
    group = iota((SUB, LANES), 1) // (LANES // SUB)
    tile = cat[:SUB]
    for d in range(1, SUB):
        tile = jnp.where(group == d, cat[d * SUB : (d + 1) * SUB], tile)
    both = jnp.concatenate([tile, day], axis=0)
    each = both.shape[0]
    for j in range(out_ref.shape[0] // each):
        out_ref[j * each : (j + 1) * each] = both


def closing_kernel(
    group_hbm, factor_vmem, back_ref, x_ref, factor_hbm, cat_hbm, day_hbm, out_hbm,
    group_ref, factor_ref, cat_ref, day_ref, scale_ref, buf_ref, sems, out_sems,
):
    items, _, stores = x_ref.shape
    loads = [
        pltpu.make_async_copy(group_hbm, group_ref, sems.at[0]),
        pltpu.make_async_copy(factor_vmem, factor_ref, sems.at[1]),
    ]
    for copy in loads:
        copy.start()
    each = SUB + 1
    for t in range(stores // LANES):
        here = slice(t * LANES, (t + 1) * LANES)
        tiles = swap_blocks([back_ref[(t * SUB + j) * each : (t * SUB + j) * each + SUB] for j in range(SUB)])
        cat_ref[:, here] = jnp.concatenate(tiles, axis=0)
        day_ref[:, here] = swap_within(back_ref[pl.ds(t * SUB * each + SUB, SUB, stride=each), :])
    stores_out = [
        pltpu.make_async_copy(factor_vmem, factor_hbm, sems.at[4]),
        pltpu.make_async_copy(cat_ref, cat_hbm, sems.at[2]),
        pltpu.make_async_copy(day_ref, day_hbm, sems.at[3]),
    ]
    for copy in stores_out:
        copy.start()
    for copy in loads:
        copy.wait()
    first = group_ref[0, 0]
    last = cat_ref.shape[0] - 1
    for s in range(SLOTS):
        scale_ref[s] = cat_ref[pl.ds(jnp.minimum(first + s, last), 1), :] * day_ref[...]
    chunks = out_sems.shape[0]
    block = items // chunks
    for n in range(chunks):
        for i in range(n * block, (n + 1) * block):
            value = x_ref[i].astype(F32) * factor_ref[0, i] * scale_ref[group_ref[0, i] - first]
            buf_ref[i] = value.astype(BF16)
        rows = pl.ds(n * block, block)
        copy = pltpu.make_async_copy(buf_ref.at[rows], out_hbm.at[rows], out_sems.at[n])
        copy.start()
        stores_out.append(copy)
    for copy in stores_out:
        copy.wait()


def vmem(count):
    return [pl.BlockSpec(memory_space=pltpu.VMEM)] * count


def held(x):
    return pltpu.with_memory_space_constraint(x, pltpu.VMEM)


def far(x):
    return pltpu.with_memory_space_constraint(x, pltpu.HBM)


LIMIT = pltpu.CompilerParams(vmem_limit_bytes=8 * 1024 * 1024)


def call(kernel, out_shape, *args, **options):
    return pl.pallas_call(
        kernel,
        out_shape=out_shape,
        in_specs=vmem(len(args)),
        out_specs=tuple(vmem(len(out_shape))),
        compiler_params=LIMIT,
        **options,
    )(*map(held, args))


def shards(predicted_units, product_group, product_goal, group_outlet_goal, outlet_date_goal):
    items, days, stores = predicted_units.shape
    cats = group_outlet_goal.shape[0]
    owners = lax.axis_size("item")
    beside = lax.axis_size("store")

    def message(each):
        return pltpu.VMEM((owners * each, LANES), F32)

    def exchanged(x):
        sent = x.reshape(owners, 1, x.size // owners)
        return lax.all_to_all(sent, "item", 0, 0, tiled=True).reshape(x.shape)

    margin = pltpu.VMEM((beside, 1, LANES), F32)
    line = pltpu.VMEM((1, LANES), F32)
    tile = pltpu.VMEM((SUB, LANES), jnp.int32)
    per_cat = pltpu.VMEM((cats, LANES), F32)

    far_spec = pl.BlockSpec(memory_space=pltpu.HBM)
    (part,) = call(first_kernel, (margin,), predicted_units, name="first")
    wide, slot, lines, cat_goal = pl.pallas_call(
        spread_kernel,
        out_shape=(
            pltpu.VMEM((items, days * stores), BF16),
            tile,
            pltpu.VMEM((SUB, LANES), F32),
            per_cat,
        ),
        in_specs=vmem(1) + [far_spec] * 4,
        out_specs=tuple(vmem(4)),
        scratch_shapes=[
            pltpu.VMEM((items * days * stores // LANES, LANES), F32),
            pltpu.VMEM((1, items), jnp.int32),
            pltpu.VMEM((1, items), F32),
            pltpu.VMEM((cats, stores), F32),
            pltpu.VMEM((days, stores), F32),
            pltpu.SemaphoreType.DMA((4,)),
        ],
        compiler_params=LIMIT,
        name="spread",
    )(
        held(predicted_units),
        far(product_group.reshape(1, items)),
        far(product_goal.reshape(1, items)),
        far(group_outlet_goal),
        far(outlet_date_goal),
    )
    for n in range(ROUNDS):
        total = lax.all_to_all(part, "store", 0, 0, tiled=True)
        shapes = (message(SLOTS if n else SUB),)
        if n == ROUNDS - 1:
            shapes += (line,)
        pooled, *factor = call(pool_kernel, shapes, total, lines, wide, slot, name="pool")
        taken = exchanged(pooled)
        if n == ROUNDS - 1:
            break
        if n == 0:
            shapes = (
                message(SLOTS),
                line,
                pltpu.VMEM((owners * SLOTS, LANES), BF16),
                pltpu.VMEM((cats, owners * SLOTS), BF16),
            )
            back, day, place, across = call(owner_first_kernel, shapes, taken, cat_goal, lines, name="owner_first")
        else:
            shapes = (message(SLOTS), line)
            back, day = call(owner_kernel, shapes, taken, cat_goal, lines, day, place, across, name="owner")
        (part,) = call(margin_kernel, (margin,), exchanged(back), wide, slot, name="margin")

    (back,) = call(
        owner_last_kernel, (message(SUB + 1),), taken, cat_goal, lines, day, across, name="owner_last"
    )
    product_factor, group_outlet_factor, outlet_date_factor, adjusted_tensor = pl.pallas_call(
        closing_kernel,
        out_shape=(
            jax.ShapeDtypeStruct((1, items), F32),
            jax.ShapeDtypeStruct((cats, stores), F32),
            jax.ShapeDtypeStruct((days, stores), F32),
            jax.ShapeDtypeStruct((items, days, stores), BF16),
        ),
        in_specs=[far_spec] + vmem(3),
        out_specs=(far_spec,) * 4,
        scratch_shapes=[
            pltpu.SMEM((1, items), jnp.int32),
            pltpu.SMEM((1, items), F32),
            pltpu.VMEM((cats, stores), F32),
            pltpu.VMEM((days, stores), F32),
            pltpu.VMEM((SUB, days, stores), F32),
            pltpu.VMEM((items, days, stores), BF16),
            pltpu.SemaphoreType.DMA((5,)),
            pltpu.SemaphoreType.DMA((4,)),
        ],
        compiler_params=LIMIT,
        name="closing",
    )(far(product_group.reshape(1, items)), held(factor[0]), held(exchanged(back)), held(predicted_units))
    return (product_factor.reshape(items), group_outlet_factor, outlet_date_factor, adjusted_tensor)


def solution(mesh):
    in_specs = (P("item", None, "store"), P("item"), P("item"), P(None, "store"), P(None, "store"))
    out_specs = (P("item"), P(None, "store"), P(None, "store"), P("item", None, "store"))
    return jax.shard_map(shards, mesh=mesh, in_specs=in_specs, out_specs=out_specs, check_vma=False)
```

```python
import functools

import jax
import jax.numpy as jnp
from jax import lax
from jax.experimental import pallas as pl
from jax.experimental.pallas import tpu as pltpu
from jax.sharding import PartitionSpec as P

ROUNDS = 4
INNER = 3
LANES = 128
SUB = 8
SLOTS = 5
BASE_ROW = 7

F32 = jnp.float32
BF16 = jnp.bfloat16


def iota(shape, dim):
    return lax.broadcasted_iota(jnp.int32, shape, dim)


def two_parts(x):
    high = x.astype(BF16)
    low = (x - high.astype(F32)).astype(BF16)
    return high, low


def swap_blocks(tiles):
    count = len(tiles)
    width = LANES // count
    group = iota(tiles[0].shape, 1) // width
    bit = 1
    while bit < count:
        low = (group & bit) == 0
        fresh = []
        for a in range(count):
            other = tiles[a ^ bit]
            if a & bit == 0:
                fresh.append(jnp.where(low, tiles[a], pltpu.roll(other, bit * width, 1)))
            else:
                fresh.append(jnp.where(low, pltpu.roll(other, LANES - bit * width, 1), tiles[a]))
        tiles = fresh
        bit *= 2
    return tiles


def swap_within(x):
    width = LANES // SUB
    row, group = iota(x.shape, 0), iota(x.shape, 1) // width
    for bit in (1, 2, 4):
        low, same = (row & bit) == 0, (row & bit) == (group & bit)
        above = pltpu.roll(pltpu.roll(x, SUB - bit, 0), bit * width, 1)
        if 2 * bit == SUB:
            x = jnp.where(same, x, above)
        else:
            below = pltpu.roll(pltpu.roll(x, bit, 0), LANES - bit * width, 1)
            x = jnp.where(same, x, jnp.where(low, above, below))
    return x


def picked(x, index):
    return jnp.take_along_axis(x, index, axis=1)


def near_kernel(x_hbm, x_ref, sem):
    copy = pltpu.make_async_copy(x_hbm, x_ref, sem)
    copy.start()
    copy.wait()


def first_kernel(x_ref, out_ref):
    items, days, stores = x_ref.shape
    row, lane = iota((SUB, LANES), 0), iota((SUB, LANES), 1)
    half = items // SUB
    gather = (iota((LANES, LANES), 0) // days == iota((LANES, LANES), 1) % half).astype(F32).astype(BF16)
    x = x_ref[...].astype(F32).reshape(items * days, stores).astype(BF16)
    sums = lax.dot_general(
        jnp.ones((SUB, stores), BF16), x, (((1,), (1,)), ((), ())), preferred_element_type=F32
    )
    tile = sums[:, :LANES]
    for q in range(1, SUB):
        tile = jnp.where(row == q, sums[:, q * LANES : (q + 1) * LANES], tile)
    each = jnp.dot(jnp.concatenate(two_parts(tile), axis=0), gather, preferred_element_type=F32)
    kept = jnp.where(lane // half == row, each[:SUB] + each[SUB:], 0.0)
    line = jnp.sum(kept, axis=0, keepdims=True)
    out_ref[...] = jnp.broadcast_to(line[None], out_ref.shape)


def spread_kernel(
    x_ref, group_hbm, goal_hbm, cat_all_hbm, day_all_hbm,
    wide_ref, slot_ref, own_ref, line_ref, cat_goal_ref,
    rows_ref, group_ref, goal_ref, cat_all_ref, day_all_ref, sems,
):
    pairs = ((group_hbm, group_ref), (goal_hbm, goal_ref), (cat_all_hbm, cat_all_ref), (day_all_hbm, day_all_ref))
    copies = [pltpu.make_async_copy(src, dst, sems.at[n]) for n, (src, dst) in enumerate(pairs)]
    for copy in copies:
        copy.start()
    items, days, stores = x_ref.shape
    tall = 2 * SUB

    def step(n, carry):
        into = pl.ds(pl.multiple_of(n * tall, tall), tall)
        x = x_ref[into].astype(F32).reshape(tall * days, stores)
        for t in range(stores // LANES):
            at = (t * items + n * tall) * days
            rows_ref[pl.ds(pl.multiple_of(at, SUB), tall * days), :] = x[:, t * LANES : (t + 1) * LANES]
            tiles = [rows_ref[pl.ds(at + d, tall, stride=days), :] for d in range(days)]
            for j, tile in enumerate(swap_blocks(tiles)):
                column = (t * SUB + j) * LANES
                wide_ref[into, column : column + LANES] = tile.astype(BF16)
        return carry

    lax.fori_loop(0, items // tall, step, 0)
    for copy in copies:
        copy.wait()
    row, lane = iota((SUB, LANES), 0), iota((SUB, LANES), 1)
    group = jnp.broadcast_to(group_ref[...], (SUB, LANES))
    first = picked(group, jnp.zeros_like(lane))
    slot_ref[...] = group - first
    own_ref[...] = group_ref[...]
    line_ref[0:1] = goal_ref[...]
    line_ref[1:2] = first[:1].astype(F32)
    width = LANES // days
    at = lax.axis_index("item") * width
    there = pl.ds(pl.multiple_of(at // LANES * LANES, LANES), LANES)
    index = at % LANES + lane % width
    for k in range(cat_goal_ref.shape[0] // SUB):
        rows = slice(k * SUB, (k + 1) * SUB)
        cat_goal_ref[rows] = picked(cat_all_ref[rows, there], index)
    day_goal = jnp.where(lane // width == row, picked(day_all_ref[:, there], index), 0.0)
    line_ref[2:3] = jnp.sum(day_goal, axis=0, keepdims=True)


def margin_kernel(back_ref, wide_ref, slot_ref, out_ref):
    count = wide_ref.shape[1] // LANES
    tiles = []
    for j in range(count):
        at = min(j * SLOTS, count * SLOTS - SUB)
        tile = back_ref[at : at + SUB]
        if at < j * SLOTS:
            tile = pltpu.roll(tile, SUB - (j * SLOTS - at), 0)
        tiles.append(tile)
    parts = jnp.concatenate(two_parts(jnp.concatenate(tiles, axis=1)), axis=0)
    sums = lax.dot_general(parts, wide_ref[...], (((1,), (1,)), ((), ())), preferred_element_type=F32)
    sums = sums[:SUB] + sums[SUB:]
    kept = jnp.where(iota((SUB, LANES), 0) == slot_ref[...], sums, 0.0)
    line = jnp.sum(kept, axis=0, keepdims=True)
    out_ref[...] = jnp.broadcast_to(line[None], out_ref.shape)


def pool_kernel(margin_ref, line_ref, wide_ref, slot_ref, out_ref, *factor_out):
    total = jnp.sum(margin_ref[...], axis=0)
    factor = line_ref[0:1] / total
    if factor_out:
        factor_out[0][...] = factor
    row = iota((SUB, LANES), 0)
    weights = jnp.where(row == slot_ref[...], factor, 0.0)
    parts = jnp.concatenate(two_parts(weights), axis=0)
    sums = jnp.dot(parts, wide_ref[...], preferred_element_type=F32)
    sums = sums[:SUB] + sums[SUB:]
    count = wide_ref.shape[1] // LANES
    each = out_ref.shape[0] // count
    base = jnp.broadcast_to(line_ref[1:2], (SUB, LANES))
    for j in range(count):
        tile = sums[:, j * LANES : (j + 1) * LANES]
        if each > SLOTS:
            tile = jnp.where(row == BASE_ROW, base, tile)
        out_ref[j * each : (j + 1) * each] = tile[:each]


def fitted(merged, cat_goal, day_goal, day):
    width = LANES // SUB
    for _ in range(INNER):
        below = merged * day
        turned = [below] + [pltpu.roll(below, n * width, 1) for n in range(1, SUB)]
        while len(turned) > 1:
            turned = [turned[n] + turned[n + 1] for n in range(0, len(turned), 2)]
        cat = cat_goal / turned[0]
        day = day_goal / jnp.sum(merged * cat, axis=0, keepdims=True)
    return cat, day


def summed(across, taken):
    merged = jnp.dot(across, jnp.concatenate(two_parts(taken), axis=1), preferred_element_type=F32)
    return merged[:, :LANES] + merged[:, LANES:]


def answer(place, cat, day, out_ref):
    parts = jnp.concatenate(two_parts(cat * day), axis=0)
    out_ref[...] = jnp.dot(place, parts, preferred_element_type=F32)


def owner_first_kernel(taken_ref, cat_goal_ref, line_ref, out_ref, day_ref, place_ref, across_ref):
    cats = cat_goal_ref.shape[0]
    devices = taken_ref.shape[0] // SUB
    base = taken_ref[pl.ds(BASE_ROW, devices, stride=SUB), :]

    def placed(each):
        rows = devices * each
        at = iota((rows, devices), 0) - iota((rows, devices), 1) * each
        own = (at >= 0) & (at < each)
        spread = jnp.dot(own.astype(F32).astype(BF16), base.astype(BF16), preferred_element_type=F32)
        slot = jnp.sum(jnp.where(own, at, 0), axis=1, keepdims=True)
        lane = iota((rows, LANES), 1)
        hit = (spread.astype(jnp.int32) + slot == lane % cats) & (slot < SLOTS)
        return hit.astype(F32)

    place = placed(SLOTS)
    across_ref[...] = place.T[:cats].astype(BF16)
    place_ref[...] = place.astype(BF16)
    merged = summed(placed(SUB).T[:cats].astype(BF16), taken_ref[...])
    cat, day = fitted(merged, cat_goal_ref[...], line_ref[2:3], jnp.ones((1, LANES), F32))
    day_ref[...] = day
    answer(place_ref[...], cat, day, out_ref)


def owner_kernel(taken_ref, cat_goal_ref, line_ref, day_ref, place_ref, across_ref, out_ref, day_out_ref):
    merged = summed(across_ref[...], taken_ref[...])
    cat, day = fitted(merged, cat_goal_ref[...], line_ref[2:3], day_ref[...])
    day_out_ref[...] = day
    answer(place_ref[...], cat, day, out_ref)


def owner_last_kernel(taken_ref, cat_goal_ref, line_ref, day_ref, across_ref, out_ref):
    merged = summed(across_ref[...], taken_ref[...])
    cat, day = fitted(merged, cat_goal_ref[...], line_ref[2:3], day_ref[...])
    group = iota((SUB, LANES), 1) // (LANES // SUB)
    tile = cat[:SUB]
    for d in range(1, SUB):
        tile = jnp.where(group == d, cat[d * SUB : (d + 1) * SUB], tile)
    both = jnp.concatenate([tile, day], axis=0)
    each = both.shape[0]
    for j in range(out_ref.shape[0] // each):
        out_ref[j * each : (j + 1) * each] = both


def closing_kernel(
    group_vmem, factor_vmem, back_ref, x_ref, factor_hbm, cat_hbm, day_hbm, out_hbm,
    group_ref, factor_ref, cat_ref, day_ref, scale_ref, buf_ref, sems, out_sems,
):
    items, _, stores = x_ref.shape
    loads = [
        pltpu.make_async_copy(group_vmem, group_ref, sems.at[0]),
        pltpu.make_async_copy(factor_vmem, factor_ref, sems.at[1]),
    ]
    for copy in loads:
        copy.start()
    each = SUB + 1
    for t in range(stores // LANES):
        here = slice(t * LANES, (t + 1) * LANES)
        tiles = swap_blocks([back_ref[(t * SUB + j) * each : (t * SUB + j) * each + SUB] for j in range(SUB)])
        cat_ref[:, here] = jnp.concatenate(tiles, axis=0)
        day_ref[:, here] = swap_within(back_ref[pl.ds(t * SUB * each + SUB, SUB, stride=each), :])
    stores_out = [
        pltpu.make_async_copy(factor_vmem, factor_hbm, sems.at[4]),
        pltpu.make_async_copy(cat_ref, cat_hbm, sems.at[2]),
        pltpu.make_async_copy(day_ref, day_hbm, sems.at[3]),
    ]
    for copy in stores_out:
        copy.start()
    for copy in loads:
        copy.wait()
    first = group_ref[0, 0]
    last = cat_ref.shape[0] - 1
    for s in range(SLOTS):
        scale_ref[s] = cat_ref[pl.ds(jnp.minimum(first + s, last), 1), :] * day_ref[...]
    chunks = out_sems.shape[0]
    block = items // chunks
    for n in range(chunks):
        for i in range(n * block, (n + 1) * block):
            value = x_ref[i].astype(F32) * factor_ref[0, i] * scale_ref[group_ref[0, i] - first]
            buf_ref[i] = value.astype(BF16)
        rows = pl.ds(n * block, block)
        copy = pltpu.make_async_copy(buf_ref.at[rows], out_hbm.at[rows], out_sems.at[n])
        copy.start()
        stores_out.append(copy)
    for copy in stores_out:
        copy.wait()


def vmem(count):
    return [pl.BlockSpec(memory_space=pltpu.VMEM)] * count


def held(x):
    return pltpu.with_memory_space_constraint(x, pltpu.VMEM)


def far(x):
    return pltpu.with_memory_space_constraint(x, pltpu.HBM)


LIMIT = pltpu.CompilerParams(vmem_limit_bytes=8 * 1024 * 1024)


def call(kernel, out_shape, *args, **options):
    return pl.pallas_call(
        kernel,
        out_shape=out_shape,
        in_specs=vmem(len(args)),
        out_specs=tuple(vmem(len(out_shape))),
        compiler_params=LIMIT,
        **options,
    )(*map(held, args))


def shards(predicted_units, product_group, product_goal, group_outlet_goal, outlet_date_goal):
    items, days, stores = predicted_units.shape
    cats = group_outlet_goal.shape[0]
    owners = lax.axis_size("item")
    beside = lax.axis_size("store")

    def message(each):
        return pltpu.VMEM((owners * each, LANES), F32)

    def exchanged(x):
        sent = x.reshape(owners, 1, x.size // owners)
        return lax.all_to_all(sent, "item", 0, 0, tiled=True).reshape(x.shape)

    margin = pltpu.VMEM((beside, 1, LANES), F32)
    line = pltpu.VMEM((1, LANES), F32)
    tile = pltpu.VMEM((SUB, LANES), jnp.int32)
    per_cat = pltpu.VMEM((cats, LANES), F32)

    far_spec = pl.BlockSpec(memory_space=pltpu.HBM)
    (near,) = pl.pallas_call(
        near_kernel,
        out_shape=(pltpu.VMEM(predicted_units.shape, BF16),),
        in_specs=[far_spec],
        out_specs=tuple(vmem(1)),
        scratch_shapes=[pltpu.SemaphoreType.DMA],
        compiler_params=LIMIT,
        name="near",
    )(far(predicted_units))
    (part,) = call(first_kernel, (margin,), near, name="first")
    wide, slot, own, lines, cat_goal = pl.pallas_call(
        spread_kernel,
        out_shape=(
            pltpu.VMEM((items, days * stores), BF16),
            tile,
            pltpu.VMEM((1, items), jnp.int32),
            pltpu.VMEM((SUB, LANES), F32),
            per_cat,
        ),
        in_specs=vmem(1) + [far_spec] * 4,
        out_specs=tuple(vmem(5)),
        scratch_shapes=[
            pltpu.VMEM((items * days * stores // LANES, LANES), F32),
            pltpu.VMEM((1, items), jnp.int32),
            pltpu.VMEM((1, items), F32),
            pltpu.VMEM((cats, stores), F32),
            pltpu.VMEM((days, stores), F32),
            pltpu.SemaphoreType.DMA((4,)),
        ],
        compiler_params=LIMIT,
        name="spread",
    )(
        held(near),
        far(product_group.reshape(1, items)),
        far(product_goal.reshape(1, items)),
        far(group_outlet_goal),
        far(outlet_date_goal),
    )
    for n in range(ROUNDS):
        total = lax.all_to_all(part, "store", 0, 0, tiled=True)
        shapes = (message(SLOTS if n else SUB),)
        if n == ROUNDS - 1:
            shapes += (line,)
        pooled, *factor = call(pool_kernel, shapes, total, lines, wide, slot, name="pool")
        taken = exchanged(pooled)
        if n == ROUNDS - 1:
            break
        if n == 0:
            shapes = (
                message(SLOTS),
                line,
                pltpu.VMEM((owners * SLOTS, LANES), BF16),
                pltpu.VMEM((cats, owners * SLOTS), BF16),
            )
            back, day, place, across = call(owner_first_kernel, shapes, taken, cat_goal, lines, name="owner_first")
        else:
            shapes = (message(SLOTS), line)
            back, day = call(owner_kernel, shapes, taken, cat_goal, lines, day, place, across, name="owner")
        (part,) = call(margin_kernel, (margin,), exchanged(back), wide, slot, name="margin")

    (back,) = call(
        owner_last_kernel, (message(SUB + 1),), taken, cat_goal, lines, day, across, name="owner_last"
    )
    product_factor, group_outlet_factor, outlet_date_factor, adjusted_tensor = pl.pallas_call(
        closing_kernel,
        out_shape=(
            jax.ShapeDtypeStruct((1, items), F32),
            jax.ShapeDtypeStruct((cats, stores), F32),
            jax.ShapeDtypeStruct((days, stores), F32),
            jax.ShapeDtypeStruct((items, days, stores), BF16),
        ),
        in_specs=vmem(4),
        out_specs=(far_spec,) * 4,
        scratch_shapes=[
            pltpu.SMEM((1, items), jnp.int32),
            pltpu.SMEM((1, items), F32),
            pltpu.VMEM((cats, stores), F32),
            pltpu.VMEM((days, stores), F32),
            pltpu.VMEM((SUB, days, stores), F32),
            pltpu.VMEM((items, days, stores), BF16),
            pltpu.SemaphoreType.DMA((5,)),
            pltpu.SemaphoreType.DMA((8,)),
        ],
        compiler_params=LIMIT,
        name="closing",
    )(*map(held, (own, factor[0], exchanged(back), near)))
    return (product_factor.reshape(items), group_outlet_factor, outlet_date_factor, adjusted_tensor)


def solution(mesh):
    in_specs = (P("item", None, "store"), P("item"), P("item"), P(None, "store"), P(None, "store"))
    out_specs = (P("item"), P(None, "store"), P(None, "store"), P("item", None, "store"))
    return jax.shard_map(shards, mesh=mesh, in_specs=in_specs, out_specs=out_specs, check_vma=False)
```

```python
import functools

import jax
import jax.numpy as jnp
from jax import lax
from jax.experimental import pallas as pl
from jax.experimental.pallas import tpu as pltpu
from jax.sharding import PartitionSpec as P

ROUNDS = 4
INNER = 3
LANES = 128
SUB = 8
SLOTS = 5
BASE_ROW = 7

F32 = jnp.float32
BF16 = jnp.bfloat16


def iota(shape, dim):
    return lax.broadcasted_iota(jnp.int32, shape, dim)


def two_parts(x):
    high = x.astype(BF16)
    low = (x - high.astype(F32)).astype(BF16)
    return high, low


def swap_blocks(tiles):
    count = len(tiles)
    width = LANES // count
    group = iota(tiles[0].shape, 1) // width
    bit = 1
    while bit < count:
        low = (group & bit) == 0
        fresh = []
        for a in range(count):
            other = tiles[a ^ bit]
            if a & bit == 0:
                fresh.append(jnp.where(low, tiles[a], pltpu.roll(other, bit * width, 1)))
            else:
                fresh.append(jnp.where(low, pltpu.roll(other, LANES - bit * width, 1), tiles[a]))
        tiles = fresh
        bit *= 2
    return tiles


def swap_within(x):
    width = LANES // SUB
    row, group = iota(x.shape, 0), iota(x.shape, 1) // width
    for bit in (1, 2, 4):
        low, same = (row & bit) == 0, (row & bit) == (group & bit)
        above = pltpu.roll(pltpu.roll(x, SUB - bit, 0), bit * width, 1)
        if 2 * bit == SUB:
            x = jnp.where(same, x, above)
        else:
            below = pltpu.roll(pltpu.roll(x, bit, 0), LANES - bit * width, 1)
            x = jnp.where(same, x, jnp.where(low, above, below))
    return x


def picked(x, index):
    return jnp.take_along_axis(x, index, axis=1)


def near_kernel(x_hbm, x_ref, sem):
    copy = pltpu.make_async_copy(x_hbm, x_ref, sem)
    copy.start()
    copy.wait()


def first_kernel(x_ref, out_ref):
    items, days, stores = x_ref.shape
    row, lane = iota((SUB, LANES), 0), iota((SUB, LANES), 1)
    half = items // SUB
    gather = (iota((LANES, LANES), 0) // days == iota((LANES, LANES), 1) % half).astype(F32).astype(BF16)
    x = x_ref[...].astype(F32).reshape(items * days, stores).astype(BF16)
    sums = lax.dot_general(
        jnp.ones((SUB, stores), BF16), x, (((1,), (1,)), ((), ())), preferred_element_type=F32
    )
    tile = sums[:, :LANES]
    for q in range(1, SUB):
        tile = jnp.where(row == q, sums[:, q * LANES : (q + 1) * LANES], tile)
    each = jnp.dot(jnp.concatenate(two_parts(tile), axis=0), gather, preferred_element_type=F32)
    kept = jnp.where(lane // half == row, each[:SUB] + each[SUB:], 0.0)
    line = jnp.sum(kept, axis=0, keepdims=True)
    out_ref[...] = jnp.broadcast_to(line[None], out_ref.shape)


def spread_kernel(
    x_ref, group_hbm, goal_hbm, cat_all_hbm, day_all_hbm,
    wide_ref, slot_ref, own_ref, line_ref, cat_goal_ref,
    rows_ref, group_ref, goal_ref, cat_all_ref, day_all_ref, sems,
):
    pairs = ((group_hbm, group_ref), (goal_hbm, goal_ref), (cat_all_hbm, cat_all_ref), (day_all_hbm, day_all_ref))
    copies = [pltpu.make_async_copy(src, dst, sems.at[n]) for n, (src, dst) in enumerate(pairs)]
    for copy in copies:
        copy.start()
    items, days, stores = x_ref.shape
    tall = 2 * SUB

    def step(n, carry):
        into = pl.ds(pl.multiple_of(n * tall, tall), tall)
        x = x_ref[into].astype(F32).reshape(tall * days, stores)
        for t in range(stores // LANES):
            at = (t * items + n * tall) * days
            rows_ref[pl.ds(pl.multiple_of(at, SUB), tall * days), :] = x[:, t * LANES : (t + 1) * LANES]
            tiles = [rows_ref[pl.ds(at + d, tall, stride=days), :] for d in range(days)]
            for j, tile in enumerate(swap_blocks(tiles)):
                column = (t * SUB + j) * LANES
                wide_ref[into, column : column + LANES] = tile.astype(BF16)
        return carry

    lax.fori_loop(0, items // tall, step, 0)
    for copy in copies:
        copy.wait()
    row, lane = iota((SUB, LANES), 0), iota((SUB, LANES), 1)
    group = jnp.broadcast_to(group_ref[...], (SUB, LANES))
    first = picked(group, jnp.zeros_like(lane))
    slot_ref[...] = group - first
    own_ref[...] = group_ref[...]
    line_ref[0:1] = goal_ref[...]
    line_ref[1:2] = first[:1].astype(F32)
    width = LANES // days
    at = lax.axis_index("item") * width
    there = pl.ds(pl.multiple_of(at // LANES * LANES, LANES), LANES)
    index = at % LANES + lane % width
    for k in range(cat_goal_ref.shape[0] // SUB):
        rows = slice(k * SUB, (k + 1) * SUB)
        cat_goal_ref[rows] = picked(cat_all_ref[rows, there], index)
    day_goal = jnp.where(lane // width == row, picked(day_all_ref[:, there], index), 0.0)
    line_ref[2:3] = jnp.sum(day_goal, axis=0, keepdims=True)


def margin_kernel(back_ref, wide_ref, slot_ref, out_ref):
    count = wide_ref.shape[1] // LANES
    tiles = []
    for j in range(count):
        at = min(j * SLOTS, count * SLOTS - SUB)
        tile = back_ref[at : at + SUB]
        if at < j * SLOTS:
            tile = pltpu.roll(tile, SUB - (j * SLOTS - at), 0)
        tiles.append(tile)
    parts = jnp.concatenate(two_parts(jnp.concatenate(tiles, axis=1)), axis=0)
    sums = lax.dot_general(parts, wide_ref[...], (((1,), (1,)), ((), ())), preferred_element_type=F32)
    sums = sums[:SUB] + sums[SUB:]
    kept = jnp.where(iota((SUB, LANES), 0) == slot_ref[...], sums, 0.0)
    line = jnp.sum(kept, axis=0, keepdims=True)
    out_ref[...] = jnp.broadcast_to(line[None], out_ref.shape)


def pool_kernel(margin_ref, line_ref, wide_ref, slot_ref, out_ref, *factor_out):
    total = jnp.sum(margin_ref[...], axis=0)
    factor = line_ref[0:1] / total
    if factor_out:
        factor_out[0][...] = factor
    row = iota((SUB, LANES), 0)
    weights = jnp.where(row == slot_ref[...], factor, 0.0)
    parts = jnp.concatenate(two_parts(weights), axis=0)
    sums = jnp.dot(parts, wide_ref[...], preferred_element_type=F32)
    sums = sums[:SUB] + sums[SUB:]
    count = wide_ref.shape[1] // LANES
    each = out_ref.shape[0] // count
    base = jnp.broadcast_to(line_ref[1:2], (SUB, LANES))
    for j in range(count):
        tile = sums[:, j * LANES : (j + 1) * LANES]
        if each > SLOTS:
            tile = jnp.where(row == BASE_ROW, base, tile)
        out_ref[j * each : (j + 1) * each] = tile[:each]


def fitted(merged, cat_goal, day_goal, day):
    width = LANES // SUB
    for _ in range(INNER):
        below = merged * day
        turned = [below] + [pltpu.roll(below, n * width, 1) for n in range(1, SUB)]
        while len(turned) > 1:
            turned = [turned[n] + turned[n + 1] for n in range(0, len(turned), 2)]
        cat = cat_goal / turned[0]
        day = day_goal / jnp.sum(merged * cat, axis=0, keepdims=True)
    return cat, day


def summed(across, taken):
    merged = jnp.dot(across, jnp.concatenate(two_parts(taken), axis=1), preferred_element_type=F32)
    return merged[:, :LANES] + merged[:, LANES:]


def answer(place, cat, day, out_ref):
    parts = jnp.concatenate(two_parts(cat * day), axis=0)
    out_ref[...] = jnp.dot(place, parts, preferred_element_type=F32)


def owner_first_kernel(taken_ref, cat_goal_ref, line_ref, out_ref, day_ref, place_ref, across_ref):
    cats = cat_goal_ref.shape[0]
    devices = taken_ref.shape[0] // SUB
    base = taken_ref[pl.ds(BASE_ROW, devices, stride=SUB), :]

    def placed(each):
        rows = devices * each
        at = iota((rows, devices), 0) - iota((rows, devices), 1) * each
        own = (at >= 0) & (at < each)
        spread = jnp.dot(own.astype(F32).astype(BF16), base.astype(BF16), preferred_element_type=F32)
        slot = jnp.sum(jnp.where(own, at, 0), axis=1, keepdims=True)
        lane = iota((rows, LANES), 1)
        hit = (spread.astype(jnp.int32) + slot == lane % cats) & (slot < SLOTS)
        return hit.astype(F32)

    place = placed(SLOTS)
    across_ref[...] = place.T[:cats].astype(BF16)
    place_ref[...] = place.astype(BF16)
    merged = summed(placed(SUB).T[:cats].astype(BF16), taken_ref[...])
    cat, day = fitted(merged, cat_goal_ref[...], line_ref[2:3], jnp.ones((1, LANES), F32))
    day_ref[...] = day
    answer(place_ref[...], cat, day, out_ref)


def owner_kernel(taken_ref, cat_goal_ref, line_ref, day_ref, place_ref, across_ref, out_ref, day_out_ref):
    merged = summed(across_ref[...], taken_ref[...])
    cat, day = fitted(merged, cat_goal_ref[...], line_ref[2:3], day_ref[...])
    day_out_ref[...] = day
    answer(place_ref[...], cat, day, out_ref)


def owner_last_kernel(taken_ref, cat_goal_ref, line_ref, day_ref, across_ref, out_ref):
    merged = summed(across_ref[...], taken_ref[...])
    cat, day = fitted(merged, cat_goal_ref[...], line_ref[2:3], day_ref[...])
    group = iota((SUB, LANES), 1) // (LANES // SUB)
    tile = cat[:SUB]
    for d in range(1, SUB):
        tile = jnp.where(group == d, cat[d * SUB : (d + 1) * SUB], tile)
    both = jnp.concatenate([tile, day], axis=0)
    each = both.shape[0]
    for j in range(out_ref.shape[0] // each):
        out_ref[j * each : (j + 1) * each] = both


def closing_kernel(
    group_vmem, factor_vmem, back_ref, x_ref, factor_hbm, cat_hbm, day_hbm, out_hbm,
    group_ref, factor_ref, cat_ref, day_ref, scale_ref, buf_ref, sems, out_sems,
):
    items, _, stores = x_ref.shape
    loads = [
        pltpu.make_async_copy(group_vmem, group_ref, sems.at[0]),
        pltpu.make_async_copy(factor_vmem, factor_ref, sems.at[1]),
    ]
    for copy in loads:
        copy.start()
    each = SUB + 1
    for t in range(stores // LANES):
        here = slice(t * LANES, (t + 1) * LANES)
        tiles = swap_blocks([back_ref[(t * SUB + j) * each : (t * SUB + j) * each + SUB] for j in range(SUB)])
        cat_ref[:, here] = jnp.concatenate(tiles, axis=0)
        day_ref[:, here] = swap_within(back_ref[pl.ds(t * SUB * each + SUB, SUB, stride=each), :])
    stores_out = [
        pltpu.make_async_copy(factor_vmem, factor_hbm, sems.at[4]),
        pltpu.make_async_copy(cat_ref, cat_hbm, sems.at[2]),
        pltpu.make_async_copy(day_ref, day_hbm, sems.at[3]),
    ]
    for copy in stores_out:
        copy.start()
    for copy in loads:
        copy.wait()
    first = group_ref[0, 0]
    last = cat_ref.shape[0] - 1
    for s in range(SLOTS):
        scale_ref[s] = cat_ref[pl.ds(jnp.minimum(first + s, last), 1), :] * day_ref[...]
    chunks = out_sems.shape[0]
    block = items // chunks
    for n in range(chunks):
        for i in range(n * block, (n + 1) * block):
            value = x_ref[i].astype(F32) * factor_ref[0, i] * scale_ref[group_ref[0, i] - first]
            buf_ref[i] = value.astype(BF16)
        rows = pl.ds(n * block, block)
        copy = pltpu.make_async_copy(buf_ref.at[rows], out_hbm.at[rows], out_sems.at[n])
        copy.start()
        stores_out.append(copy)
    for copy in stores_out:
        copy.wait()


def vmem(count):
    return [pl.BlockSpec(memory_space=pltpu.VMEM)] * count


def held(x):
    return pltpu.with_memory_space_constraint(x, pltpu.VMEM)


def far(x):
    return pltpu.with_memory_space_constraint(x, pltpu.HBM)


LIMIT = pltpu.CompilerParams(vmem_limit_bytes=8 * 1024 * 1024)


def call(kernel, out_shape, *args, **options):
    return pl.pallas_call(
        kernel,
        out_shape=out_shape,
        in_specs=vmem(len(args)),
        out_specs=tuple(vmem(len(out_shape))),
        compiler_params=LIMIT,
        **options,
    )(*map(held, args))


def shards(predicted_units, product_group, product_goal, group_outlet_goal, outlet_date_goal):
    items, days, stores = predicted_units.shape
    cats = group_outlet_goal.shape[0]
    owners = lax.axis_size("item")
    beside = lax.axis_size("store")

    def message(each):
        return pltpu.VMEM((owners * each, LANES), F32)

    def exchanged(x):
        sent = x.reshape(owners, 1, x.size // owners)
        return lax.all_to_all(sent, "item", 0, 0, tiled=True).reshape(x.shape)

    margin = pltpu.VMEM((beside, 1, LANES), F32)
    line = pltpu.VMEM((1, LANES), F32)
    tile = pltpu.VMEM((SUB, LANES), jnp.int32)
    per_cat = pltpu.VMEM((cats, LANES), F32)

    far_spec = pl.BlockSpec(memory_space=pltpu.HBM)
    (near,) = pl.pallas_call(
        near_kernel,
        out_shape=(pltpu.VMEM(predicted_units.shape, BF16),),
        in_specs=[far_spec],
        out_specs=tuple(vmem(1)),
        scratch_shapes=[pltpu.SemaphoreType.DMA],
        compiler_params=LIMIT,
        name="near",
    )(far(predicted_units))
    (part,) = call(first_kernel, (margin,), near, name="first")
    wide, slot, own, lines, cat_goal = pl.pallas_call(
        spread_kernel,
        out_shape=(
            pltpu.VMEM((items, days * stores), BF16),
            tile,
            pltpu.VMEM((1, items), jnp.int32),
            pltpu.VMEM((SUB, LANES), F32),
            per_cat,
        ),
        in_specs=vmem(1) + [far_spec] * 4,
        out_specs=tuple(vmem(5)),
        scratch_shapes=[
            pltpu.VMEM((items * days * stores // LANES, LANES), F32),
            pltpu.VMEM((1, items), jnp.int32),
            pltpu.VMEM((1, items), F32),
            pltpu.VMEM((cats, stores), F32),
            pltpu.VMEM((days, stores), F32),
            pltpu.SemaphoreType.DMA((4,)),
        ],
        compiler_params=LIMIT,
        name="spread",
    )(
        held(near),
        far(product_group.reshape(1, items)),
        far(product_goal.reshape(1, items)),
        far(group_outlet_goal),
        far(outlet_date_goal),
    )
    for n in range(ROUNDS):
        total = lax.all_to_all(part, "store", 0, 0, axis_index_groups=[list(range(beside))[::-1]], tiled=True)
        shapes = (message(SLOTS if n else SUB),)
        if n == ROUNDS - 1:
            shapes += (line,)
        pooled, *factor = call(pool_kernel, shapes, total, lines, wide, slot, name="pool")
        taken = exchanged(pooled)
        if n == ROUNDS - 1:
            break
        if n == 0:
            shapes = (
                message(SLOTS),
                line,
                pltpu.VMEM((owners * SLOTS, LANES), BF16),
                pltpu.VMEM((cats, owners * SLOTS), BF16),
            )
            back, day, place, across = call(owner_first_kernel, shapes, taken, cat_goal, lines, name="owner_first")
        else:
            shapes = (message(SLOTS), line)
            back, day = call(owner_kernel, shapes, taken, cat_goal, lines, day, place, across, name="owner")
        (part,) = call(margin_kernel, (margin,), exchanged(back), wide, slot, name="margin")

    (back,) = call(
        owner_last_kernel, (message(SUB + 1),), taken, cat_goal, lines, day, across, name="owner_last"
    )
    product_factor, group_outlet_factor, outlet_date_factor, adjusted_tensor = pl.pallas_call(
        closing_kernel,
        out_shape=(
            jax.ShapeDtypeStruct((1, items), F32),
            jax.ShapeDtypeStruct((cats, stores), F32),
            jax.ShapeDtypeStruct((days, stores), F32),
            jax.ShapeDtypeStruct((items, days, stores), BF16),
        ),
        in_specs=vmem(4),
        out_specs=(far_spec,) * 4,
        scratch_shapes=[
            pltpu.SMEM((1, items), jnp.int32),
            pltpu.SMEM((1, items), F32),
            pltpu.VMEM((cats, stores), F32),
            pltpu.VMEM((days, stores), F32),
            pltpu.VMEM((SUB, days, stores), F32),
            pltpu.VMEM((items, days, stores), BF16),
            pltpu.SemaphoreType.DMA((5,)),
            pltpu.SemaphoreType.DMA((8,)),
        ],
        compiler_params=LIMIT,
        name="closing",
    )(*map(held, (own, factor[0], exchanged(back), near)))
    return (product_factor.reshape(items), group_outlet_factor, outlet_date_factor, adjusted_tensor)


def solution(mesh):
    in_specs = (P("item", None, "store"), P("item"), P("item"), P(None, "store"), P(None, "store"))
    out_specs = (P("item"), P(None, "store"), P(None, "store"), P("item", None, "store"))
    return jax.shard_map(shards, mesh=mesh, in_specs=in_specs, out_specs=out_specs, check_vma=False)
```

```python
import functools

import jax
import jax.numpy as jnp
from jax import lax
from jax.experimental import pallas as pl
from jax.experimental.pallas import tpu as pltpu
from jax.sharding import PartitionSpec as P

ROUNDS = 4
INNER = 3
LANES = 128
SUB = 8
SLOTS = 5
BASE_ROW = 7

F32 = jnp.float32
BF16 = jnp.bfloat16


def iota(shape, dim):
    return lax.broadcasted_iota(jnp.int32, shape, dim)


def item_order(count):
    lead = count - 3
    return [lead] + [i for i in range(count) if i != lead]


def store_order(count):
    lead = count - 3
    return [lead] + [i for i in range(count - 1, -1, -1) if i != lead]


def own_place(count):
    lead = count - 3
    me = lax.axis_index("item")
    return jnp.where(me == lead, 0, jnp.where(me < lead, me + 1, me))


def two_parts(x):
    high = x.astype(BF16)
    low = (x - high.astype(F32)).astype(BF16)
    return high, low


def swap_blocks(tiles):
    count = len(tiles)
    width = LANES // count
    group = iota(tiles[0].shape, 1) // width
    bit = 1
    while bit < count:
        low = (group & bit) == 0
        fresh = []
        for a in range(count):
            other = tiles[a ^ bit]
            if a & bit == 0:
                fresh.append(jnp.where(low, tiles[a], pltpu.roll(other, bit * width, 1)))
            else:
                fresh.append(jnp.where(low, pltpu.roll(other, LANES - bit * width, 1), tiles[a]))
        tiles = fresh
        bit *= 2
    return tiles


def swap_within(x):
    width = LANES // SUB
    row, group = iota(x.shape, 0), iota(x.shape, 1) // width
    for bit in (1, 2, 4):
        low, same = (row & bit) == 0, (row & bit) == (group & bit)
        above = pltpu.roll(pltpu.roll(x, SUB - bit, 0), bit * width, 1)
        if 2 * bit == SUB:
            x = jnp.where(same, x, above)
        else:
            below = pltpu.roll(pltpu.roll(x, bit, 0), LANES - bit * width, 1)
            x = jnp.where(same, x, jnp.where(low, above, below))
    return x


def picked(x, index):
    return jnp.take_along_axis(x, index, axis=1)


def near_kernel(x_hbm, x_ref, sem):
    copy = pltpu.make_async_copy(x_hbm, x_ref, sem)
    copy.start()
    copy.wait()


def first_kernel(x_ref, out_ref):
    items, days, stores = x_ref.shape
    row, lane = iota((SUB, LANES), 0), iota((SUB, LANES), 1)
    half = items // SUB
    gather = (iota((LANES, LANES), 0) // days == iota((LANES, LANES), 1) % half).astype(F32).astype(BF16)
    x = x_ref[...].astype(F32).reshape(items * days, stores).astype(BF16)
    sums = lax.dot_general(
        jnp.ones((SUB, stores), BF16), x, (((1,), (1,)), ((), ())), preferred_element_type=F32
    )
    tile = sums[:, :LANES]
    for q in range(1, SUB):
        tile = jnp.where(row == q, sums[:, q * LANES : (q + 1) * LANES], tile)
    each = jnp.dot(jnp.concatenate(two_parts(tile), axis=0), gather, preferred_element_type=F32)
    kept = jnp.where(lane // half == row, each[:SUB] + each[SUB:], 0.0)
    line = jnp.sum(kept, axis=0, keepdims=True)
    out_ref[...] = jnp.broadcast_to(line[None], out_ref.shape)


def spread_kernel(
    x_ref, group_hbm, goal_hbm, cat_all_hbm, day_all_hbm,
    wide_ref, slot_ref, own_ref, line_ref, cat_goal_ref,
    rows_ref, group_ref, goal_ref, cat_all_ref, day_all_ref, sems,
):
    pairs = ((group_hbm, group_ref), (goal_hbm, goal_ref), (cat_all_hbm, cat_all_ref), (day_all_hbm, day_all_ref))
    copies = [pltpu.make_async_copy(src, dst, sems.at[n]) for n, (src, dst) in enumerate(pairs)]
    for copy in copies:
        copy.start()
    items, days, stores = x_ref.shape
    tall = 2 * SUB

    def step(n, carry):
        into = pl.ds(pl.multiple_of(n * tall, tall), tall)
        x = x_ref[into].astype(F32).reshape(tall * days, stores)
        for t in range(stores // LANES):
            at = (t * items + n * tall) * days
            rows_ref[pl.ds(pl.multiple_of(at, SUB), tall * days), :] = x[:, t * LANES : (t + 1) * LANES]
            tiles = [rows_ref[pl.ds(at + d, tall, stride=days), :] for d in range(days)]
            for j, tile in enumerate(swap_blocks(tiles)):
                column = (t * SUB + j) * LANES
                wide_ref[into, column : column + LANES] = tile.astype(BF16)
        return carry

    lax.fori_loop(0, items // tall, step, 0)
    for copy in copies:
        copy.wait()
    row, lane = iota((SUB, LANES), 0), iota((SUB, LANES), 1)
    group = jnp.broadcast_to(group_ref[...], (SUB, LANES))
    first = picked(group, jnp.zeros_like(lane))
    slot_ref[...] = group - first
    own_ref[...] = group_ref[...]
    line_ref[0:1] = goal_ref[...]
    line_ref[1:2] = first[:1].astype(F32)
    width = LANES // days
    at = own_place(wide_ref.shape[1] // LANES) * width
    there = pl.ds(pl.multiple_of(at // LANES * LANES, LANES), LANES)
    index = at % LANES + lane % width
    for k in range(cat_goal_ref.shape[0] // SUB):
        rows = slice(k * SUB, (k + 1) * SUB)
        cat_goal_ref[rows] = picked(cat_all_ref[rows, there], index)
    day_goal = jnp.where(lane // width == row, picked(day_all_ref[:, there], index), 0.0)
    line_ref[2:3] = jnp.sum(day_goal, axis=0, keepdims=True)


def margin_kernel(back_ref, wide_ref, slot_ref, out_ref):
    count = wide_ref.shape[1] // LANES
    tiles = []
    for j in range(count):
        at = min(j * SLOTS, count * SLOTS - SUB)
        tile = back_ref[at : at + SUB]
        if at < j * SLOTS:
            tile = pltpu.roll(tile, SUB - (j * SLOTS - at), 0)
        tiles.append(tile)
    parts = jnp.concatenate(two_parts(jnp.concatenate(tiles, axis=1)), axis=0)
    sums = lax.dot_general(parts, wide_ref[...], (((1,), (1,)), ((), ())), preferred_element_type=F32)
    sums = sums[:SUB] + sums[SUB:]
    kept = jnp.where(iota((SUB, LANES), 0) == slot_ref[...], sums, 0.0)
    line = jnp.sum(kept, axis=0, keepdims=True)
    out_ref[...] = jnp.broadcast_to(line[None], out_ref.shape)


def pool_kernel(margin_ref, line_ref, wide_ref, slot_ref, out_ref, *factor_out):
    total = jnp.sum(margin_ref[...], axis=0)
    factor = line_ref[0:1] / total
    if factor_out:
        factor_out[0][...] = factor
    row = iota((SUB, LANES), 0)
    weights = jnp.where(row == slot_ref[...], factor, 0.0)
    parts = jnp.concatenate(two_parts(weights), axis=0)
    sums = jnp.dot(parts, wide_ref[...], preferred_element_type=F32)
    sums = sums[:SUB] + sums[SUB:]
    count = wide_ref.shape[1] // LANES
    each = out_ref.shape[0] // count
    base = jnp.broadcast_to(line_ref[1:2], (SUB, LANES))
    for j in range(count):
        tile = sums[:, j * LANES : (j + 1) * LANES]
        if each > SLOTS:
            tile = jnp.where(row == BASE_ROW, base, tile)
        out_ref[j * each : (j + 1) * each] = tile[:each]


def fitted(merged, cat_goal, day_goal, day):
    width = LANES // SUB
    for _ in range(INNER):
        below = merged * day
        turned = [below] + [pltpu.roll(below, n * width, 1) for n in range(1, SUB)]
        while len(turned) > 1:
            turned = [turned[n] + turned[n + 1] for n in range(0, len(turned), 2)]
        cat = cat_goal / turned[0]
        day = day_goal / jnp.sum(merged * cat, axis=0, keepdims=True)
    return cat, day


def summed(across, taken):
    merged = jnp.dot(across, jnp.concatenate(two_parts(taken), axis=1), preferred_element_type=F32)
    return merged[:, :LANES] + merged[:, LANES:]


def answer(place, cat, day, out_ref):
    parts = jnp.concatenate(two_parts(cat * day), axis=0)
    out_ref[...] = jnp.dot(place, parts, preferred_element_type=F32)


def owner_first_kernel(taken_ref, cat_goal_ref, line_ref, out_ref, day_ref, place_ref, across_ref):
    cats = cat_goal_ref.shape[0]
    devices = taken_ref.shape[0] // SUB
    base = taken_ref[pl.ds(BASE_ROW, devices, stride=SUB), :]

    def placed(each):
        rows = devices * each
        at = iota((rows, devices), 0) - iota((rows, devices), 1) * each
        own = (at >= 0) & (at < each)
        spread = jnp.dot(own.astype(F32).astype(BF16), base.astype(BF16), preferred_element_type=F32)
        slot = jnp.sum(jnp.where(own, at, 0), axis=1, keepdims=True)
        lane = iota((rows, LANES), 1)
        hit = (spread.astype(jnp.int32) + slot == lane % cats) & (slot < SLOTS)
        return hit.astype(F32)

    place = placed(SLOTS)
    across_ref[...] = place.T[:cats].astype(BF16)
    place_ref[...] = place.astype(BF16)
    merged = summed(placed(SUB).T[:cats].astype(BF16), taken_ref[...])
    cat, day = fitted(merged, cat_goal_ref[...], line_ref[2:3], jnp.ones((1, LANES), F32))
    day_ref[...] = day
    answer(place_ref[...], cat, day, out_ref)


def owner_kernel(taken_ref, cat_goal_ref, line_ref, day_ref, place_ref, across_ref, out_ref, day_out_ref):
    merged = summed(across_ref[...], taken_ref[...])
    cat, day = fitted(merged, cat_goal_ref[...], line_ref[2:3], day_ref[...])
    day_out_ref[...] = day
    answer(place_ref[...], cat, day, out_ref)


def owner_last_kernel(taken_ref, cat_goal_ref, line_ref, day_ref, across_ref, out_ref):
    merged = summed(across_ref[...], taken_ref[...])
    cat, day = fitted(merged, cat_goal_ref[...], line_ref[2:3], day_ref[...])
    group = iota((SUB, LANES), 1) // (LANES // SUB)
    tile = cat[:SUB]
    for d in range(1, SUB):
        tile = jnp.where(group == d, cat[d * SUB : (d + 1) * SUB], tile)
    both = jnp.concatenate([tile, day], axis=0)
    each = both.shape[0]
    for j in range(out_ref.shape[0] // each):
        out_ref[j * each : (j + 1) * each] = both


def closing_kernel(
    group_vmem, factor_vmem, back_ref, x_ref, factor_hbm, cat_hbm, day_hbm, out_hbm,
    group_ref, factor_ref, cat_ref, day_ref, scale_ref, buf_ref, sems, out_sems,
):
    items, _, stores = x_ref.shape
    loads = [
        pltpu.make_async_copy(group_vmem, group_ref, sems.at[0]),
        pltpu.make_async_copy(factor_vmem, factor_ref, sems.at[1]),
    ]
    for copy in loads:
        copy.start()
    each = SUB + 1
    for t in range(stores // LANES):
        here = slice(t * LANES, (t + 1) * LANES)
        tiles = swap_blocks([back_ref[(t * SUB + j) * each : (t * SUB + j) * each + SUB] for j in range(SUB)])
        cat_ref[:, here] = jnp.concatenate(tiles, axis=0)
        day_ref[:, here] = swap_within(back_ref[pl.ds(t * SUB * each + SUB, SUB, stride=each), :])
    stores_out = [
        pltpu.make_async_copy(factor_vmem, factor_hbm, sems.at[4]),
        pltpu.make_async_copy(cat_ref, cat_hbm, sems.at[2]),
        pltpu.make_async_copy(day_ref, day_hbm, sems.at[3]),
    ]
    for copy in stores_out:
        copy.start()
    for copy in loads:
        copy.wait()
    first = group_ref[0, 0]
    last = cat_ref.shape[0] - 1
    for s in range(SLOTS):
        scale_ref[s] = cat_ref[pl.ds(jnp.minimum(first + s, last), 1), :] * day_ref[...]
    chunks = out_sems.shape[0]
    block = items // chunks
    for n in range(chunks):
        for i in range(n * block, (n + 1) * block):
            value = x_ref[i].astype(F32) * factor_ref[0, i] * scale_ref[group_ref[0, i] - first]
            buf_ref[i] = value.astype(BF16)
        rows = pl.ds(n * block, block)
        copy = pltpu.make_async_copy(buf_ref.at[rows], out_hbm.at[rows], out_sems.at[n])
        copy.start()
        stores_out.append(copy)
    for copy in stores_out:
        copy.wait()


def vmem(count):
    return [pl.BlockSpec(memory_space=pltpu.VMEM)] * count


def held(x):
    return pltpu.with_memory_space_constraint(x, pltpu.VMEM)


def far(x):
    return pltpu.with_memory_space_constraint(x, pltpu.HBM)


LIMIT = pltpu.CompilerParams(vmem_limit_bytes=8 * 1024 * 1024)


def call(kernel, out_shape, *args, **options):
    return pl.pallas_call(
        kernel,
        out_shape=out_shape,
        in_specs=vmem(len(args)),
        out_specs=tuple(vmem(len(out_shape))),
        compiler_params=LIMIT,
        **options,
    )(*map(held, args))


def shards(predicted_units, product_group, product_goal, group_outlet_goal, outlet_date_goal):
    items, days, stores = predicted_units.shape
    cats = group_outlet_goal.shape[0]
    owners = lax.axis_size("item")
    beside = lax.axis_size("store")

    def message(each):
        return pltpu.VMEM((owners * each, LANES), F32)

    def exchanged(x):
        sent = x.reshape(owners, 1, x.size // owners)
        there = lax.all_to_all(sent, "item", 0, 0, axis_index_groups=[item_order(owners)], tiled=True)
        return there.reshape(x.shape)

    margin = pltpu.VMEM((beside, 1, LANES), F32)
    line = pltpu.VMEM((1, LANES), F32)
    tile = pltpu.VMEM((SUB, LANES), jnp.int32)
    per_cat = pltpu.VMEM((cats, LANES), F32)

    far_spec = pl.BlockSpec(memory_space=pltpu.HBM)
    (near,) = pl.pallas_call(
        near_kernel,
        out_shape=(pltpu.VMEM(predicted_units.shape, BF16),),
        in_specs=[far_spec],
        out_specs=tuple(vmem(1)),
        scratch_shapes=[pltpu.SemaphoreType.DMA],
        compiler_params=LIMIT,
        name="near",
    )(far(predicted_units))
    (part,) = call(first_kernel, (margin,), near, name="first")
    wide, slot, own, lines, cat_goal = pl.pallas_call(
        spread_kernel,
        out_shape=(
            pltpu.VMEM((items, days * stores), BF16),
            tile,
            pltpu.VMEM((1, items), jnp.int32),
            pltpu.VMEM((SUB, LANES), F32),
            per_cat,
        ),
        in_specs=vmem(1) + [far_spec] * 4,
        out_specs=tuple(vmem(5)),
        scratch_shapes=[
            pltpu.VMEM((items * days * stores // LANES, LANES), F32),
            pltpu.VMEM((1, items), jnp.int32),
            pltpu.VMEM((1, items), F32),
            pltpu.VMEM((cats, stores), F32),
            pltpu.VMEM((days, stores), F32),
            pltpu.SemaphoreType.DMA((4,)),
        ],
        compiler_params=LIMIT,
        name="spread",
    )(
        held(near),
        far(product_group.reshape(1, items)),
        far(product_goal.reshape(1, items)),
        far(group_outlet_goal),
        far(outlet_date_goal),
    )
    for n in range(ROUNDS):
        total = lax.all_to_all(part, "store", 0, 0, axis_index_groups=[store_order(beside)], tiled=True)
        shapes = (message(SLOTS if n else SUB),)
        if n == ROUNDS - 1:
            shapes += (line,)
        pooled, *factor = call(pool_kernel, shapes, total, lines, wide, slot, name="pool")
        taken = exchanged(pooled)
        if n == ROUNDS - 1:
            break
        if n == 0:
            shapes = (
                message(SLOTS),
                line,
                pltpu.VMEM((owners * SLOTS, LANES), BF16),
                pltpu.VMEM((cats, owners * SLOTS), BF16),
            )
            back, day, place, across = call(owner_first_kernel, shapes, taken, cat_goal, lines, name="owner_first")
        else:
            shapes = (message(SLOTS), line)
            back, day = call(owner_kernel, shapes, taken, cat_goal, lines, day, place, across, name="owner")
        (part,) = call(margin_kernel, (margin,), exchanged(back), wide, slot, name="margin")

    (back,) = call(
        owner_last_kernel, (message(SUB + 1),), taken, cat_goal, lines, day, across, name="owner_last"
    )
    product_factor, group_outlet_factor, outlet_date_factor, adjusted_tensor = pl.pallas_call(
        closing_kernel,
        out_shape=(
            jax.ShapeDtypeStruct((1, items), F32),
            jax.ShapeDtypeStruct((cats, stores), F32),
            jax.ShapeDtypeStruct((days, stores), F32),
            jax.ShapeDtypeStruct((items, days, stores), BF16),
        ),
        in_specs=vmem(4),
        out_specs=(far_spec,) * 4,
        scratch_shapes=[
            pltpu.SMEM((1, items), jnp.int32),
            pltpu.SMEM((1, items), F32),
            pltpu.VMEM((cats, stores), F32),
            pltpu.VMEM((days, stores), F32),
            pltpu.VMEM((SUB, days, stores), F32),
            pltpu.VMEM((items, days, stores), BF16),
            pltpu.SemaphoreType.DMA((5,)),
            pltpu.SemaphoreType.DMA((8,)),
        ],
        compiler_params=LIMIT,
        name="closing",
    )(*map(held, (own, factor[0], exchanged(back), near)))
    return (product_factor.reshape(items), group_outlet_factor, outlet_date_factor, adjusted_tensor)


def solution(mesh):
    in_specs = (P("item", None, "store"), P("item"), P("item"), P(None, "store"), P(None, "store"))
    out_specs = (P("item"), P(None, "store"), P(None, "store"), P("item", None, "store"))
    return jax.shard_map(shards, mesh=mesh, in_specs=in_specs, out_specs=out_specs, check_vma=False)
```

```python
import functools

import jax
import jax.numpy as jnp
from jax import lax
from jax.experimental import pallas as pl
from jax.experimental.pallas import tpu as pltpu
from jax.sharding import PartitionSpec as P

ROUNDS = 4
INNER = 3
LANES = 128
SUB = 8
SLOTS = 5
BASE_ROW = SLOTS

F32 = jnp.float32
BF16 = jnp.bfloat16


def iota(shape, dim):
    return lax.broadcasted_iota(jnp.int32, shape, dim)


def item_lead(count):
    return 2 * count // 3


def item_order(count):
    lead = item_lead(count)
    return [lead] + [i for i in range(count) if i != lead]


def store_order(count):
    lead = count - 3
    return [lead] + [i for i in range(count - 1, -1, -1) if i != lead]


def own_place(count):
    lead = item_lead(count)
    me = lax.axis_index("item")
    return jnp.where(me == lead, 0, jnp.where(me < lead, me + 1, me))


def two_parts(x):
    high = x.astype(BF16)
    low = (x - high.astype(F32)).astype(BF16)
    return high, low


def swap_blocks(tiles):
    count = len(tiles)
    width = LANES // count
    group = iota(tiles[0].shape, 1) // width
    bit = 1
    while bit < count:
        low = (group & bit) == 0
        fresh = []
        for a in range(count):
            other = tiles[a ^ bit]
            if a & bit == 0:
                fresh.append(jnp.where(low, tiles[a], pltpu.roll(other, bit * width, 1)))
            else:
                fresh.append(jnp.where(low, pltpu.roll(other, LANES - bit * width, 1), tiles[a]))
        tiles = fresh
        bit *= 2
    return tiles


def swap_within(x):
    width = LANES // SUB
    row, group = iota(x.shape, 0), iota(x.shape, 1) // width
    for bit in (1, 2, 4):
        low, same = (row & bit) == 0, (row & bit) == (group & bit)
        above = pltpu.roll(pltpu.roll(x, SUB - bit, 0), bit * width, 1)
        if 2 * bit == SUB:
            x = jnp.where(same, x, above)
        else:
            below = pltpu.roll(pltpu.roll(x, bit, 0), LANES - bit * width, 1)
            x = jnp.where(same, x, jnp.where(low, above, below))
    return x


def picked(x, index):
    return jnp.take_along_axis(x, index, axis=1)


def near_kernel(x_hbm, x_ref, sem):
    copy = pltpu.make_async_copy(x_hbm, x_ref, sem)
    copy.start()
    copy.wait()


def first_kernel(x_ref, out_ref):
    items, days, stores = x_ref.shape
    row, lane = iota((SUB, LANES), 0), iota((SUB, LANES), 1)
    half = items // SUB
    gather = (iota((LANES, LANES), 0) // days == iota((LANES, LANES), 1) % half).astype(F32).astype(BF16)
    x = x_ref[...].astype(F32).reshape(items * days, stores).astype(BF16)
    sums = lax.dot_general(
        jnp.ones((SUB, stores), BF16), x, (((1,), (1,)), ((), ())), preferred_element_type=F32
    )
    tile = sums[:, :LANES]
    for q in range(1, SUB):
        tile = jnp.where(row == q, sums[:, q * LANES : (q + 1) * LANES], tile)
    each = jnp.dot(jnp.concatenate(two_parts(tile), axis=0), gather, preferred_element_type=F32)
    kept = jnp.where(lane // half == row, each[:SUB] + each[SUB:], 0.0)
    line = jnp.sum(kept, axis=0, keepdims=True)
    out_ref[...] = jnp.broadcast_to(line[None], out_ref.shape)


def spread_kernel(
    x_ref, group_hbm, goal_hbm, cat_all_hbm, day_all_hbm,
    wide_ref, slot_ref, own_ref, line_ref, cat_goal_ref,
    rows_ref, group_ref, goal_ref, cat_all_ref, day_all_ref, sems,
):
    pairs = ((group_hbm, group_ref), (goal_hbm, goal_ref), (cat_all_hbm, cat_all_ref), (day_all_hbm, day_all_ref))
    copies = [pltpu.make_async_copy(src, dst, sems.at[n]) for n, (src, dst) in enumerate(pairs)]
    for copy in copies:
        copy.start()
    items, days, stores = x_ref.shape
    tall = 2 * SUB

    def step(n, carry):
        into = pl.ds(pl.multiple_of(n * tall, tall), tall)
        x = x_ref[into].astype(F32).reshape(tall * days, stores)
        for t in range(stores // LANES):
            at = (t * items + n * tall) * days
            rows_ref[pl.ds(pl.multiple_of(at, SUB), tall * days), :] = x[:, t * LANES : (t + 1) * LANES]
            tiles = [rows_ref[pl.ds(at + d, tall, stride=days), :] for d in range(days)]
            for j, tile in enumerate(swap_blocks(tiles)):
                column = (t * SUB + j) * LANES
                wide_ref[into, column : column + LANES] = tile.astype(BF16)
        return carry

    lax.fori_loop(0, items // tall, step, 0)
    for copy in copies:
        copy.wait()
    row, lane = iota((SUB, LANES), 0), iota((SUB, LANES), 1)
    group = jnp.broadcast_to(group_ref[...], (SUB, LANES))
    first = picked(group, jnp.zeros_like(lane))
    slot_ref[...] = group - first
    own_ref[...] = group_ref[...]
    line_ref[0:1] = goal_ref[...]
    line_ref[1:2] = first[:1].astype(F32)
    width = LANES // days
    at = own_place(wide_ref.shape[1] // LANES) * width
    there = pl.ds(pl.multiple_of(at // LANES * LANES, LANES), LANES)
    index = at % LANES + lane % width
    for k in range(cat_goal_ref.shape[0] // SUB):
        rows = slice(k * SUB, (k + 1) * SUB)
        cat_goal_ref[rows] = picked(cat_all_ref[rows, there], index)
    day_goal = jnp.where(lane // width == row, picked(day_all_ref[:, there], index), 0.0)
    line_ref[2:3] = jnp.sum(day_goal, axis=0, keepdims=True)


def margin_kernel(back_ref, wide_ref, slot_ref, out_ref):
    count = wide_ref.shape[1] // LANES
    tiles = []
    for j in range(count):
        at = min(j * SLOTS, count * SLOTS - SUB)
        tile = back_ref[at : at + SUB]
        if at < j * SLOTS:
            tile = pltpu.roll(tile, SUB - (j * SLOTS - at), 0)
        tiles.append(tile)
    parts = jnp.concatenate(two_parts(jnp.concatenate(tiles, axis=1)), axis=0)
    sums = lax.dot_general(parts, wide_ref[...], (((1,), (1,)), ((), ())), preferred_element_type=F32)
    sums = sums[:SUB] + sums[SUB:]
    kept = jnp.where(iota((SUB, LANES), 0) == slot_ref[...], sums, 0.0)
    line = jnp.sum(kept, axis=0, keepdims=True)
    out_ref[...] = jnp.broadcast_to(line[None], out_ref.shape)


def pool_kernel(margin_ref, line_ref, wide_ref, slot_ref, out_ref, *factor_out):
    total = jnp.sum(margin_ref[...], axis=0)
    factor = line_ref[0:1] / total
    if factor_out:
        factor_out[0][...] = factor
    row = iota((SUB, LANES), 0)
    weights = jnp.where(row == slot_ref[...], factor, 0.0)
    parts = jnp.concatenate(two_parts(weights), axis=0)
    sums = jnp.dot(parts, wide_ref[...], preferred_element_type=F32)
    sums = sums[:SUB] + sums[SUB:]
    count = wide_ref.shape[1] // LANES
    each = out_ref.shape[0] // count
    base = jnp.broadcast_to(line_ref[1:2], (SUB, LANES))
    for j in range(count):
        tile = sums[:, j * LANES : (j + 1) * LANES]
        if each > SLOTS:
            tile = jnp.where(row == BASE_ROW, base, tile)
        out_ref[j * each : (j + 1) * each] = tile[:each]


def fitted(merged, cat_goal, day_goal, day):
    width = LANES // SUB
    for _ in range(INNER):
        below = merged * day
        turned = [below] + [pltpu.roll(below, n * width, 1) for n in range(1, SUB)]
        while len(turned) > 1:
            turned = [turned[n] + turned[n + 1] for n in range(0, len(turned), 2)]
        cat = cat_goal / turned[0]
        day = day_goal / jnp.sum(merged * cat, axis=0, keepdims=True)
    return cat, day


def summed(across, taken):
    merged = jnp.dot(across, jnp.concatenate(two_parts(taken), axis=1), preferred_element_type=F32)
    return merged[:, :LANES] + merged[:, LANES:]


def answer(place, cat, day, out_ref):
    parts = jnp.concatenate(two_parts(cat * day), axis=0)
    out_ref[...] = jnp.dot(place, parts, preferred_element_type=F32)


def owner_first_kernel(taken_ref, cat_goal_ref, line_ref, out_ref, day_ref, place_ref, across_ref):
    cats = cat_goal_ref.shape[0]
    each = SLOTS + 1
    devices = taken_ref.shape[0] // each
    base = taken_ref[pl.ds(BASE_ROW, devices, stride=each), :]

    def placed(each):
        rows = devices * each
        at = iota((rows, devices), 0) - iota((rows, devices), 1) * each
        own = (at >= 0) & (at < each)
        spread = jnp.dot(own.astype(F32).astype(BF16), base.astype(BF16), preferred_element_type=F32)
        slot = jnp.sum(jnp.where(own, at, 0), axis=1, keepdims=True)
        lane = iota((rows, LANES), 1)
        hit = (spread.astype(jnp.int32) + slot == lane % cats) & (slot < SLOTS)
        return hit.astype(F32)

    place = placed(SLOTS)
    across_ref[...] = place.T[:cats].astype(BF16)
    place_ref[...] = place.astype(BF16)
    merged = summed(placed(each).T[:cats].astype(BF16), taken_ref[...])
    cat, day = fitted(merged, cat_goal_ref[...], line_ref[2:3], jnp.ones((1, LANES), F32))
    day_ref[...] = day
    answer(place_ref[...], cat, day, out_ref)


def owner_kernel(taken_ref, cat_goal_ref, line_ref, day_ref, place_ref, across_ref, out_ref, day_out_ref):
    merged = summed(across_ref[...], taken_ref[...])
    cat, day = fitted(merged, cat_goal_ref[...], line_ref[2:3], day_ref[...])
    day_out_ref[...] = day
    answer(place_ref[...], cat, day, out_ref)


def owner_last_kernel(taken_ref, cat_goal_ref, line_ref, day_ref, across_ref, out_ref):
    merged = summed(across_ref[...], taken_ref[...])
    cat, day = fitted(merged, cat_goal_ref[...], line_ref[2:3], day_ref[...])
    group = iota((SUB, LANES), 1) // (LANES // SUB)
    tile = cat[:SUB]
    for d in range(1, SUB):
        tile = jnp.where(group == d, cat[d * SUB : (d + 1) * SUB], tile)
    both = jnp.concatenate([tile, day], axis=0)
    each = both.shape[0]
    for j in range(out_ref.shape[0] // each):
        out_ref[j * each : (j + 1) * each] = both


def closing_kernel(
    group_vmem, factor_vmem, back_ref, x_ref, factor_hbm, cat_hbm, day_hbm, out_hbm,
    group_ref, factor_ref, cat_ref, day_ref, scale_ref, buf_ref, sems, out_sems,
):
    items, _, stores = x_ref.shape
    loads = [
        pltpu.make_async_copy(group_vmem, group_ref, sems.at[0]),
        pltpu.make_async_copy(factor_vmem, factor_ref, sems.at[1]),
    ]
    for copy in loads:
        copy.start()
    each = SUB + 1
    for t in range(stores // LANES):
        here = slice(t * LANES, (t + 1) * LANES)
        tiles = swap_blocks([back_ref[(t * SUB + j) * each : (t * SUB + j) * each + SUB] for j in range(SUB)])
        cat_ref[:, here] = jnp.concatenate(tiles, axis=0)
        day_ref[:, here] = swap_within(back_ref[pl.ds(t * SUB * each + SUB, SUB, stride=each), :])
    stores_out = [
        pltpu.make_async_copy(factor_vmem, factor_hbm, sems.at[4]),
        pltpu.make_async_copy(cat_ref, cat_hbm, sems.at[2]),
        pltpu.make_async_copy(day_ref, day_hbm, sems.at[3]),
    ]
    for copy in stores_out:
        copy.start()
    for copy in loads:
        copy.wait()
    first = group_ref[0, 0]
    last = cat_ref.shape[0] - 1
    for s in range(SLOTS):
        scale_ref[s] = cat_ref[pl.ds(jnp.minimum(first + s, last), 1), :] * day_ref[...]
    chunks = out_sems.shape[0]
    block = items // chunks
    for n in range(chunks):
        for i in range(n * block, (n + 1) * block):
            value = x_ref[i].astype(F32) * factor_ref[0, i] * scale_ref[group_ref[0, i] - first]
            buf_ref[i] = value.astype(BF16)
        rows = pl.ds(n * block, block)
        copy = pltpu.make_async_copy(buf_ref.at[rows], out_hbm.at[rows], out_sems.at[n])
        copy.start()
        stores_out.append(copy)
    for copy in stores_out:
        copy.wait()


def vmem(count):
    return [pl.BlockSpec(memory_space=pltpu.VMEM)] * count


def held(x):
    return pltpu.with_memory_space_constraint(x, pltpu.VMEM)


def far(x):
    return pltpu.with_memory_space_constraint(x, pltpu.HBM)


LIMIT = pltpu.CompilerParams(vmem_limit_bytes=8 * 1024 * 1024)


def call(kernel, out_shape, *args, **options):
    return pl.pallas_call(
        kernel,
        out_shape=out_shape,
        in_specs=vmem(len(args)),
        out_specs=tuple(vmem(len(out_shape))),
        compiler_params=LIMIT,
        **options,
    )(*map(held, args))


def shards(predicted_units, product_group, product_goal, group_outlet_goal, outlet_date_goal):
    items, days, stores = predicted_units.shape
    cats = group_outlet_goal.shape[0]
    owners = lax.axis_size("item")
    beside = lax.axis_size("store")

    def message(each):
        return pltpu.VMEM((owners * each, LANES), F32)

    def exchanged(x):
        sent = x.reshape(owners, 1, x.size // owners)
        there = lax.all_to_all(sent, "item", 0, 0, axis_index_groups=[item_order(owners)], tiled=True)
        return there.reshape(x.shape)

    margin = pltpu.VMEM((beside, 1, LANES), F32)
    line = pltpu.VMEM((1, LANES), F32)
    tile = pltpu.VMEM((SUB, LANES), jnp.int32)
    per_cat = pltpu.VMEM((cats, LANES), F32)

    far_spec = pl.BlockSpec(memory_space=pltpu.HBM)
    (near,) = pl.pallas_call(
        near_kernel,
        out_shape=(pltpu.VMEM(predicted_units.shape, BF16),),
        in_specs=[far_spec],
        out_specs=tuple(vmem(1)),
        scratch_shapes=[pltpu.SemaphoreType.DMA],
        compiler_params=LIMIT,
        name="near",
    )(far(predicted_units))
    (part,) = call(first_kernel, (margin,), near, name="first")
    wide, slot, own, lines, cat_goal = pl.pallas_call(
        spread_kernel,
        out_shape=(
            pltpu.VMEM((items, days * stores), BF16),
            tile,
            pltpu.VMEM((1, items), jnp.int32),
            pltpu.VMEM((SUB, LANES), F32),
            per_cat,
        ),
        in_specs=vmem(1) + [far_spec] * 4,
        out_specs=tuple(vmem(5)),
        scratch_shapes=[
            pltpu.VMEM((items * days * stores // LANES, LANES), F32),
            pltpu.VMEM((1, items), jnp.int32),
            pltpu.VMEM((1, items), F32),
            pltpu.VMEM((cats, stores), F32),
            pltpu.VMEM((days, stores), F32),
            pltpu.SemaphoreType.DMA((4,)),
        ],
        compiler_params=LIMIT,
        name="spread",
    )(
        held(near),
        far(product_group.reshape(1, items)),
        far(product_goal.reshape(1, items)),
        far(group_outlet_goal),
        far(outlet_date_goal),
    )
    for n in range(ROUNDS):
        total = lax.all_to_all(part, "store", 0, 0, axis_index_groups=[store_order(beside)], tiled=True)
        shapes = (message(SLOTS if n else SLOTS + 1),)
        if n == ROUNDS - 1:
            shapes += (line,)
        pooled, *factor = call(pool_kernel, shapes, total, lines, wide, slot, name="pool")
        taken = exchanged(pooled)
        if n == ROUNDS - 1:
            break
        if n == 0:
            shapes = (
                message(SLOTS),
                line,
                pltpu.VMEM((owners * SLOTS, LANES), BF16),
                pltpu.VMEM((cats, owners * SLOTS), BF16),
            )
            back, day, place, across = call(owner_first_kernel, shapes, taken, cat_goal, lines, name="owner_first")
        else:
            shapes = (message(SLOTS), line)
            back, day = call(owner_kernel, shapes, taken, cat_goal, lines, day, place, across, name="owner")
        (part,) = call(margin_kernel, (margin,), exchanged(back), wide, slot, name="margin")

    (back,) = call(
        owner_last_kernel, (message(SUB + 1),), taken, cat_goal, lines, day, across, name="owner_last"
    )
    product_factor, group_outlet_factor, outlet_date_factor, adjusted_tensor = pl.pallas_call(
        closing_kernel,
        out_shape=(
            jax.ShapeDtypeStruct((1, items), F32),
            jax.ShapeDtypeStruct((cats, stores), F32),
            jax.ShapeDtypeStruct((days, stores), F32),
            jax.ShapeDtypeStruct((items, days, stores), BF16),
        ),
        in_specs=vmem(4),
        out_specs=(far_spec,) * 4,
        scratch_shapes=[
            pltpu.SMEM((1, items), jnp.int32),
            pltpu.SMEM((1, items), F32),
            pltpu.VMEM((cats, stores), F32),
            pltpu.VMEM((days, stores), F32),
            pltpu.VMEM((SUB, days, stores), F32),
            pltpu.VMEM((items, days, stores), BF16),
            pltpu.SemaphoreType.DMA((5,)),
            pltpu.SemaphoreType.DMA((8,)),
        ],
        compiler_params=LIMIT,
        name="closing",
    )(*map(held, (own, factor[0], exchanged(back), near)))
    return (product_factor.reshape(items), group_outlet_factor, outlet_date_factor, adjusted_tensor)


def solution(mesh):
    in_specs = (P("item", None, "store"), P("item"), P("item"), P(None, "store"), P(None, "store"))
    out_specs = (P("item"), P(None, "store"), P(None, "store"), P("item", None, "store"))
    return jax.shard_map(shards, mesh=mesh, in_specs=in_specs, out_specs=out_specs, check_vma=False)
```

```python
import functools

import jax
import jax.numpy as jnp
from jax import lax
from jax.experimental import pallas as pl
from jax.experimental.pallas import tpu as pltpu
from jax.sharding import PartitionSpec as P

ROUNDS = 4
INNER = 3
LANES = 128
SUB = 8
SLOTS = 5
BASE_ROW = SLOTS

F32 = jnp.float32
BF16 = jnp.bfloat16


def iota(shape, dim):
    return lax.broadcasted_iota(jnp.int32, shape, dim)


def item_lead(count):
    return 2 * count // 3


def item_order(count):
    lead = item_lead(count)
    return [lead] + [i for i in range(count) if i != lead]


def store_order(count):
    lead = count - 3
    return [lead] + [i for i in range(count - 1, -1, -1) if i != lead]


def own_place(count):
    lead = item_lead(count)
    me = lax.axis_index("item")
    return jnp.where(me == lead, 0, jnp.where(me < lead, me + 1, me))


def two_parts(x):
    high = x.astype(BF16)
    low = (x - high.astype(F32)).astype(BF16)
    return high, low


def swap_blocks(tiles):
    count = len(tiles)
    width = LANES // count
    group = iota(tiles[0].shape, 1) // width
    bit = 1
    while bit < count:
        low = (group & bit) == 0
        fresh = []
        for a in range(count):
            other = tiles[a ^ bit]
            if a & bit == 0:
                fresh.append(jnp.where(low, tiles[a], pltpu.roll(other, bit * width, 1)))
            else:
                fresh.append(jnp.where(low, pltpu.roll(other, LANES - bit * width, 1), tiles[a]))
        tiles = fresh
        bit *= 2
    return tiles


def swap_within(x):
    width = LANES // SUB
    row, group = iota(x.shape, 0), iota(x.shape, 1) // width
    for bit in (1, 2, 4):
        low, same = (row & bit) == 0, (row & bit) == (group & bit)
        above = pltpu.roll(pltpu.roll(x, SUB - bit, 0), bit * width, 1)
        if 2 * bit == SUB:
            x = jnp.where(same, x, above)
        else:
            below = pltpu.roll(pltpu.roll(x, bit, 0), LANES - bit * width, 1)
            x = jnp.where(same, x, jnp.where(low, above, below))
    return x


def picked(x, index):
    return jnp.take_along_axis(x, index, axis=1)


def near_kernel(x_hbm, x_ref, sem):
    copy = pltpu.make_async_copy(x_hbm, x_ref, sem)
    copy.start()
    copy.wait()


def first_kernel(x_ref, out_ref):
    items, days, stores = x_ref.shape
    row, lane = iota((SUB, LANES), 0), iota((SUB, LANES), 1)
    half = items // SUB
    gather = (iota((LANES, LANES), 0) // days == iota((LANES, LANES), 1) % half).astype(F32).astype(BF16)
    x = x_ref[...].astype(F32).reshape(items * days, stores).astype(BF16)
    sums = lax.dot_general(
        jnp.ones((SUB, stores), BF16), x, (((1,), (1,)), ((), ())), preferred_element_type=F32
    )
    tile = sums[:, :LANES]
    for q in range(1, SUB):
        tile = jnp.where(row == q, sums[:, q * LANES : (q + 1) * LANES], tile)
    each = jnp.dot(jnp.concatenate(two_parts(tile), axis=0), gather, preferred_element_type=F32)
    kept = jnp.where(lane // half == row, each[:SUB] + each[SUB:], 0.0)
    line = jnp.sum(kept, axis=0, keepdims=True)
    out_ref[...] = jnp.broadcast_to(line[None], out_ref.shape)


def spread_kernel(
    x_ref, group_hbm, goal_hbm, cat_all_hbm, day_all_hbm,
    wide_ref, slot_ref, own_ref, line_ref, cat_goal_ref, widen_ref,
    rows_ref, group_ref, goal_ref, cat_all_ref, day_all_ref, sems,
):
    pairs = ((group_hbm, group_ref), (goal_hbm, goal_ref), (cat_all_hbm, cat_all_ref), (day_all_hbm, day_all_ref))
    copies = [pltpu.make_async_copy(src, dst, sems.at[n]) for n, (src, dst) in enumerate(pairs)]
    for copy in copies:
        copy.start()
    items, days, stores = x_ref.shape
    tall = 2 * SUB

    def step(n, carry):
        into = pl.ds(pl.multiple_of(n * tall, tall), tall)
        x = x_ref[into].astype(F32).reshape(tall * days, stores)
        for t in range(stores // LANES):
            at = (t * items + n * tall) * days
            rows_ref[pl.ds(pl.multiple_of(at, SUB), tall * days), :] = x[:, t * LANES : (t + 1) * LANES]
            tiles = [rows_ref[pl.ds(at + d, tall, stride=days), :] for d in range(days)]
            for j, tile in enumerate(swap_blocks(tiles)):
                column = (t * SUB + j) * LANES
                wide_ref[into, column : column + LANES] = tile.astype(BF16)
        return carry

    lax.fori_loop(0, items // tall, step, 0)
    part = LANES // days
    source, target = iota((LANES, LANES), 0), iota((LANES, LANES), 1) % part
    for s in range(SLOTS):
        widen_ref[:, s * LANES : (s + 1) * LANES] = (source == s * part + target).astype(F32).astype(BF16)
    for copy in copies:
        copy.wait()
    row, lane = iota((SUB, LANES), 0), iota((SUB, LANES), 1)
    group = jnp.broadcast_to(group_ref[...], (SUB, LANES))
    first = picked(group, jnp.zeros_like(lane))
    slot_ref[...] = group - first
    own_ref[...] = group_ref[...]
    line_ref[0:1] = goal_ref[...]
    line_ref[1:2] = first[:1].astype(F32)
    width = LANES // days
    at = own_place(wide_ref.shape[1] // LANES) * width
    there = pl.ds(pl.multiple_of(at // LANES * LANES, LANES), LANES)
    index = at % LANES + lane % width
    for k in range(cat_goal_ref.shape[0] // SUB):
        rows = slice(k * SUB, (k + 1) * SUB)
        cat_goal_ref[rows] = picked(cat_all_ref[rows, there], index)
    day_goal = jnp.where(lane // width == row, picked(day_all_ref[:, there], index), 0.0)
    line_ref[2:3] = jnp.sum(day_goal, axis=0, keepdims=True)


def margin_kernel(back_ref, wide_ref, slot_ref, widen_ref, out_ref, tiles_ref):
    count = wide_ref.shape[1] // LANES
    day = back_ref[pl.ds(0, count, stride=2), :]
    cat = back_ref[pl.ds(1, count, stride=2), :]
    cat = jnp.dot(jnp.concatenate(two_parts(cat), axis=0), widen_ref[...], preferred_element_type=F32)
    cat = cat[:count] + cat[count:]
    for s in range(SUB):
        product = cat[:, s * LANES : (s + 1) * LANES] * day if s < SLOTS else jnp.zeros_like(day)
        tiles_ref[pl.ds(s, count, stride=SUB), :] = product
    tiles = [tiles_ref[j * SUB : (j + 1) * SUB] for j in range(count)]
    parts = jnp.concatenate(two_parts(jnp.concatenate(tiles, axis=1)), axis=0)
    sums = lax.dot_general(parts, wide_ref[...], (((1,), (1,)), ((), ())), preferred_element_type=F32)
    sums = sums[:SUB] + sums[SUB:]
    kept = jnp.where(iota((SUB, LANES), 0) == slot_ref[...], sums, 0.0)
    line = jnp.sum(kept, axis=0, keepdims=True)
    out_ref[...] = jnp.broadcast_to(line[None], out_ref.shape)


def pool_kernel(margin_ref, line_ref, wide_ref, slot_ref, out_ref, *factor_out):
    total = jnp.sum(margin_ref[...], axis=0)
    factor = line_ref[0:1] / total
    if factor_out:
        factor_out[0][...] = factor
    row = iota((SUB, LANES), 0)
    weights = jnp.where(row == slot_ref[...], factor, 0.0)
    parts = jnp.concatenate(two_parts(weights), axis=0)
    sums = jnp.dot(parts, wide_ref[...], preferred_element_type=F32)
    sums = sums[:SUB] + sums[SUB:]
    count = wide_ref.shape[1] // LANES
    each = out_ref.shape[0] // count
    base = jnp.broadcast_to(line_ref[1:2], (SUB, LANES))
    for j in range(count):
        tile = sums[:, j * LANES : (j + 1) * LANES]
        if each > SLOTS:
            tile = jnp.where(row == BASE_ROW, base, tile)
        out_ref[j * each : (j + 1) * each] = tile[:each]


def fitted(merged, cat_goal, day_goal, day):
    width = LANES // SUB
    for _ in range(INNER):
        below = merged * day
        turned = [below] + [pltpu.roll(below, n * width, 1) for n in range(1, SUB)]
        while len(turned) > 1:
            turned = [turned[n] + turned[n + 1] for n in range(0, len(turned), 2)]
        cat = cat_goal / turned[0]
        day = day_goal / jnp.sum(merged * cat, axis=0, keepdims=True)
    return cat, day


def summed(across, taken):
    merged = jnp.dot(across, jnp.concatenate(two_parts(taken), axis=1), preferred_element_type=F32)
    return merged[:, :LANES] + merged[:, LANES:]


def answer(choice, cat, day, out_ref):
    group = iota(cat.shape, 1) // (LANES // SUB)
    blocks = [jnp.where(group == s, cat, 0.0) for s in range(choice.shape[1] // cat.shape[0])]
    parts = jnp.concatenate(two_parts(jnp.concatenate(blocks, axis=0)), axis=1)
    rows = jnp.dot(choice, parts, preferred_element_type=F32)
    devices = choice.shape[0]
    out_ref[pl.ds(0, devices, stride=2), :] = jnp.broadcast_to(day, (devices, LANES))
    out_ref[pl.ds(1, devices, stride=2), :] = rows[:, :LANES] + rows[:, LANES:]


def owner_first_kernel(taken_ref, cat_goal_ref, line_ref, out_ref, day_ref, place_ref, across_ref):
    cats = cat_goal_ref.shape[0]
    each = SLOTS + 1
    devices = taken_ref.shape[0] // each
    base = taken_ref[pl.ds(BASE_ROW, devices, stride=each), :]

    def placed(each):
        rows = devices * each
        at = iota((rows, devices), 0) - iota((rows, devices), 1) * each
        own = (at >= 0) & (at < each)
        spread = jnp.dot(own.astype(F32).astype(BF16), base.astype(BF16), preferred_element_type=F32)
        slot = jnp.sum(jnp.where(own, at, 0), axis=1, keepdims=True)
        lane = iota((rows, LANES), 1)
        hit = (spread.astype(jnp.int32) + slot == lane % cats) & (slot < SLOTS)
        return hit.astype(F32)

    across_ref[...] = placed(SLOTS).T[:cats].astype(BF16)
    lane = iota((devices, LANES), 1)
    for n in range(place_ref.shape[1] // LANES):
        slot = n * (LANES // cats) + lane // cats
        hit = (base.astype(jnp.int32) + slot == lane % cats) & (slot < SLOTS)
        place_ref[:, n * LANES : (n + 1) * LANES] = hit.astype(F32).astype(BF16)
    merged = summed(placed(each).T[:cats].astype(BF16), taken_ref[...])
    cat, day = fitted(merged, cat_goal_ref[...], line_ref[2:3], jnp.ones((1, LANES), F32))
    day_ref[...] = day
    answer(place_ref[...], cat, day, out_ref)


def owner_kernel(taken_ref, cat_goal_ref, line_ref, day_ref, place_ref, across_ref, out_ref, day_out_ref):
    merged = summed(across_ref[...], taken_ref[...])
    cat, day = fitted(merged, cat_goal_ref[...], line_ref[2:3], day_ref[...])
    day_out_ref[...] = day
    answer(place_ref[...], cat, day, out_ref)


def owner_last_kernel(taken_ref, cat_goal_ref, line_ref, day_ref, across_ref, out_ref):
    merged = summed(across_ref[...], taken_ref[...])
    cat, day = fitted(merged, cat_goal_ref[...], line_ref[2:3], day_ref[...])
    group = iota((SUB, LANES), 1) // (LANES // SUB)
    tile = cat[:SUB]
    for d in range(1, SUB):
        tile = jnp.where(group == d, cat[d * SUB : (d + 1) * SUB], tile)
    both = jnp.concatenate([tile, day], axis=0)
    each = both.shape[0]
    for j in range(out_ref.shape[0] // each):
        out_ref[j * each : (j + 1) * each] = both


def closing_kernel(
    group_vmem, factor_vmem, back_ref, x_ref, factor_hbm, cat_hbm, day_hbm, out_hbm,
    group_ref, factor_ref, cat_ref, day_ref, scale_ref, buf_ref, sems, out_sems,
):
    items, _, stores = x_ref.shape
    loads = [
        pltpu.make_async_copy(group_vmem, group_ref, sems.at[0]),
        pltpu.make_async_copy(factor_vmem, factor_ref, sems.at[1]),
    ]
    for copy in loads:
        copy.start()
    each = SUB + 1
    for t in range(stores // LANES):
        here = slice(t * LANES, (t + 1) * LANES)
        tiles = swap_blocks([back_ref[(t * SUB + j) * each : (t * SUB + j) * each + SUB] for j in range(SUB)])
        cat_ref[:, here] = jnp.concatenate(tiles, axis=0)
        day_ref[:, here] = swap_within(back_ref[pl.ds(t * SUB * each + SUB, SUB, stride=each), :])
    stores_out = [
        pltpu.make_async_copy(factor_vmem, factor_hbm, sems.at[4]),
        pltpu.make_async_copy(cat_ref, cat_hbm, sems.at[2]),
        pltpu.make_async_copy(day_ref, day_hbm, sems.at[3]),
    ]
    for copy in stores_out:
        copy.start()
    for copy in loads:
        copy.wait()
    first = group_ref[0, 0]
    last = cat_ref.shape[0] - 1
    for s in range(SLOTS):
        scale_ref[s] = cat_ref[pl.ds(jnp.minimum(first + s, last), 1), :] * day_ref[...]
    chunks = out_sems.shape[0]
    block = items // chunks
    for n in range(chunks):
        for i in range(n * block, (n + 1) * block):
            value = x_ref[i].astype(F32) * factor_ref[0, i] * scale_ref[group_ref[0, i] - first]
            buf_ref[i] = value.astype(BF16)
        rows = pl.ds(n * block, block)
        copy = pltpu.make_async_copy(buf_ref.at[rows], out_hbm.at[rows], out_sems.at[n])
        copy.start()
        stores_out.append(copy)
    for copy in stores_out:
        copy.wait()


def vmem(count):
    return [pl.BlockSpec(memory_space=pltpu.VMEM)] * count


def held(x):
    return pltpu.with_memory_space_constraint(x, pltpu.VMEM)


def far(x):
    return pltpu.with_memory_space_constraint(x, pltpu.HBM)


LIMIT = pltpu.CompilerParams(vmem_limit_bytes=8 * 1024 * 1024)


def call(kernel, out_shape, *args, **options):
    return pl.pallas_call(
        kernel,
        out_shape=out_shape,
        in_specs=vmem(len(args)),
        out_specs=tuple(vmem(len(out_shape))),
        compiler_params=LIMIT,
        **options,
    )(*map(held, args))


def shards(predicted_units, product_group, product_goal, group_outlet_goal, outlet_date_goal):
    items, days, stores = predicted_units.shape
    cats = group_outlet_goal.shape[0]
    owners = lax.axis_size("item")
    beside = lax.axis_size("store")

    def message(each):
        return pltpu.VMEM((owners * each, LANES), F32)

    def exchanged(x):
        sent = x.reshape(owners, 1, x.size // owners)
        there = lax.all_to_all(sent, "item", 0, 0, axis_index_groups=[item_order(owners)], tiled=True)
        return there.reshape(x.shape)

    margin = pltpu.VMEM((beside, 1, LANES), F32)
    line = pltpu.VMEM((1, LANES), F32)
    tile = pltpu.VMEM((SUB, LANES), jnp.int32)
    per_cat = pltpu.VMEM((cats, LANES), F32)

    far_spec = pl.BlockSpec(memory_space=pltpu.HBM)
    (near,) = pl.pallas_call(
        near_kernel,
        out_shape=(pltpu.VMEM(predicted_units.shape, BF16),),
        in_specs=[far_spec],
        out_specs=tuple(vmem(1)),
        scratch_shapes=[pltpu.SemaphoreType.DMA],
        compiler_params=LIMIT,
        name="near",
    )(far(predicted_units))
    (part,) = call(first_kernel, (margin,), near, name="first")
    wide, slot, own, lines, cat_goal, widen = pl.pallas_call(
        spread_kernel,
        out_shape=(
            pltpu.VMEM((items, days * stores), BF16),
            tile,
            pltpu.VMEM((1, items), jnp.int32),
            pltpu.VMEM((SUB, LANES), F32),
            per_cat,
            pltpu.VMEM((LANES, SLOTS * LANES), BF16),
        ),
        in_specs=vmem(1) + [far_spec] * 4,
        out_specs=tuple(vmem(6)),
        scratch_shapes=[
            pltpu.VMEM((items * days * stores // LANES, LANES), F32),
            pltpu.VMEM((1, items), jnp.int32),
            pltpu.VMEM((1, items), F32),
            pltpu.VMEM((cats, stores), F32),
            pltpu.VMEM((days, stores), F32),
            pltpu.SemaphoreType.DMA((4,)),
        ],
        compiler_params=LIMIT,
        name="spread",
    )(
        held(near),
        far(product_group.reshape(1, items)),
        far(product_goal.reshape(1, items)),
        far(group_outlet_goal),
        far(outlet_date_goal),
    )
    for n in range(ROUNDS):
        total = lax.all_to_all(part, "store", 0, 0, axis_index_groups=[store_order(beside)], tiled=True)
        shapes = (message(SLOTS if n else SLOTS + 1),)
        if n == ROUNDS - 1:
            shapes += (line,)
        pooled, *factor = call(pool_kernel, shapes, total, lines, wide, slot, name="pool")
        taken = exchanged(pooled)
        if n == ROUNDS - 1:
            break
        if n == 0:
            shapes = (
                message(2),
                line,
                pltpu.VMEM((owners, -(-SLOTS * cats // LANES) * LANES), BF16),
                pltpu.VMEM((cats, owners * SLOTS), BF16),
            )
            back, day, place, across = call(owner_first_kernel, shapes, taken, cat_goal, lines, name="owner_first")
        else:
            shapes = (message(2), line)
            back, day = call(owner_kernel, shapes, taken, cat_goal, lines, day, place, across, name="owner")
        (part,) = call(
            margin_kernel, (margin,), exchanged(back), wide, slot, widen,
            scratch_shapes=[pltpu.VMEM((owners * SUB, LANES), F32)], name="margin",
        )

    (back,) = call(
        owner_last_kernel, (message(SUB + 1),), taken, cat_goal, lines, day, across, name="owner_last"
    )
    product_factor, group_outlet_factor, outlet_date_factor, adjusted_tensor = pl.pallas_call(
        closing_kernel,
        out_shape=(
            jax.ShapeDtypeStruct((1, items), F32),
            jax.ShapeDtypeStruct((cats, stores), F32),
            jax.ShapeDtypeStruct((days, stores), F32),
            jax.ShapeDtypeStruct((items, days, stores), BF16),
        ),
        in_specs=vmem(4),
        out_specs=(far_spec,) * 4,
        scratch_shapes=[
            pltpu.SMEM((1, items), jnp.int32),
            pltpu.SMEM((1, items), F32),
            pltpu.VMEM((cats, stores), F32),
            pltpu.VMEM((days, stores), F32),
            pltpu.VMEM((SUB, days, stores), F32),
            pltpu.VMEM((items, days, stores), BF16),
            pltpu.SemaphoreType.DMA((5,)),
            pltpu.SemaphoreType.DMA((8,)),
        ],
        compiler_params=LIMIT,
        name="closing",
    )(*map(held, (own, factor[0], exchanged(back), near)))
    return (product_factor.reshape(items), group_outlet_factor, outlet_date_factor, adjusted_tensor)


def solution(mesh):
    in_specs = (P("item", None, "store"), P("item"), P("item"), P(None, "store"), P(None, "store"))
    out_specs = (P("item"), P(None, "store"), P(None, "store"), P("item", None, "store"))
    return jax.shard_map(shards, mesh=mesh, in_specs=in_specs, out_specs=out_specs, check_vma=False)
```

```python
import functools

import jax
import jax.numpy as jnp
from jax import lax
from jax.experimental import pallas as pl
from jax.experimental.pallas import tpu as pltpu
from jax.sharding import PartitionSpec as P

ROUNDS = 4
INNER = 3
LANES = 128
SUB = 8
SLOTS = 5
BASE_ROW = SLOTS

F32 = jnp.float32
BF16 = jnp.bfloat16


def iota(shape, dim):
    return lax.broadcasted_iota(jnp.int32, shape, dim)


def item_lead(count):
    return 2 * count // 3


def item_order(count):
    lead = item_lead(count)
    return [lead] + [i for i in range(count) if i != lead]


def store_order(count):
    lead = count - 3
    return [lead] + [i for i in range(count - 1, -1, -1) if i != lead]


def own_place(count):
    lead = item_lead(count)
    me = lax.axis_index("item")
    return jnp.where(me == lead, 0, jnp.where(me < lead, me + 1, me))


def two_parts(x):
    high = x.astype(BF16)
    low = (x - high.astype(F32)).astype(BF16)
    return high, low


def swap_blocks(tiles):
    count = len(tiles)
    width = LANES // count
    group = iota(tiles[0].shape, 1) // width
    bit = 1
    while bit < count:
        low = (group & bit) == 0
        fresh = []
        for a in range(count):
            other = tiles[a ^ bit]
            if a & bit == 0:
                fresh.append(jnp.where(low, tiles[a], pltpu.roll(other, bit * width, 1)))
            else:
                fresh.append(jnp.where(low, pltpu.roll(other, LANES - bit * width, 1), tiles[a]))
        tiles = fresh
        bit *= 2
    return tiles


def swap_within(x):
    width = LANES // SUB
    row, group = iota(x.shape, 0), iota(x.shape, 1) // width
    for bit in (1, 2, 4):
        low, same = (row & bit) == 0, (row & bit) == (group & bit)
        above = pltpu.roll(pltpu.roll(x, SUB - bit, 0), bit * width, 1)
        if 2 * bit == SUB:
            x = jnp.where(same, x, above)
        else:
            below = pltpu.roll(pltpu.roll(x, bit, 0), LANES - bit * width, 1)
            x = jnp.where(same, x, jnp.where(low, above, below))
    return x


def picked(x, index):
    return jnp.take_along_axis(x, index, axis=1)


def near_kernel(x_hbm, x_ref, sem):
    copy = pltpu.make_async_copy(x_hbm, x_ref, sem)
    copy.start()
    copy.wait()


def first_kernel(x_ref, out_ref):
    items, days, stores = x_ref.shape
    row, lane = iota((SUB, LANES), 0), iota((SUB, LANES), 1)
    half = items // SUB
    gather = (iota((LANES, LANES), 0) // days == iota((LANES, LANES), 1) % half).astype(F32).astype(BF16)
    folded = x_ref[:, :, :LANES].astype(F32)
    for t in range(1, stores // LANES):
        folded = folded + x_ref[:, :, t * LANES : (t + 1) * LANES].astype(F32)
    parts = jnp.concatenate(two_parts(folded.reshape(items * days, LANES)), axis=1)
    sums = lax.dot_general(
        jnp.ones((SUB, 2 * LANES), BF16), parts, (((1,), (1,)), ((), ())), preferred_element_type=F32
    )
    tile = sums[:, :LANES]
    for q in range(1, SUB):
        tile = jnp.where(row == q, sums[:, q * LANES : (q + 1) * LANES], tile)
    each = jnp.dot(jnp.concatenate(two_parts(tile), axis=0), gather, preferred_element_type=F32)
    kept = jnp.where(lane // half == row, each[:SUB] + each[SUB:], 0.0)
    line = jnp.sum(kept, axis=0, keepdims=True)
    out_ref[...] = jnp.broadcast_to(line[None], out_ref.shape)


def spread_kernel(
    x_ref, group_hbm, goal_hbm, cat_all_hbm, day_all_hbm,
    wide_ref, slot_ref, own_ref, line_ref, cat_goal_ref, widen_ref,
    rows_ref, group_ref, goal_ref, cat_all_ref, day_all_ref, sems,
):
    pairs = ((group_hbm, group_ref), (goal_hbm, goal_ref), (cat_all_hbm, cat_all_ref), (day_all_hbm, day_all_ref))
    copies = [pltpu.make_async_copy(src, dst, sems.at[n]) for n, (src, dst) in enumerate(pairs)]
    for copy in copies:
        copy.start()
    items, days, stores = x_ref.shape
    tall = 2 * SUB

    def step(n, carry):
        into = pl.ds(pl.multiple_of(n * tall, tall), tall)
        x = x_ref[into].astype(F32).reshape(tall * days, stores)
        for t in range(stores // LANES):
            at = (t * items + n * tall) * days
            rows_ref[pl.ds(pl.multiple_of(at, SUB), tall * days), :] = x[:, t * LANES : (t + 1) * LANES]
            tiles = [rows_ref[pl.ds(at + d, tall, stride=days), :] for d in range(days)]
            for j, tile in enumerate(swap_blocks(tiles)):
                column = (t * SUB + j) * LANES
                wide_ref[into, column : column + LANES] = tile.astype(BF16)
        return carry

    lax.fori_loop(0, items // tall, step, 0)
    part = LANES // days
    source, target = iota((LANES, LANES), 0), iota((LANES, LANES), 1) % part
    for s in range(SLOTS):
        widen_ref[:, s * LANES : (s + 1) * LANES] = (source == s * part + target).astype(F32).astype(BF16)
    for copy in copies:
        copy.wait()
    row, lane = iota((SUB, LANES), 0), iota((SUB, LANES), 1)
    group = jnp.broadcast_to(group_ref[...], (SUB, LANES))
    first = picked(group, jnp.zeros_like(lane))
    slot_ref[...] = group - first
    own_ref[...] = group_ref[...]
    line_ref[0:1] = goal_ref[...]
    line_ref[1:2] = first[:1].astype(F32)
    width = LANES // days
    at = own_place(wide_ref.shape[1] // LANES) * width
    there = pl.ds(pl.multiple_of(at // LANES * LANES, LANES), LANES)
    index = at % LANES + lane % width
    for k in range(cat_goal_ref.shape[0] // SUB):
        rows = slice(k * SUB, (k + 1) * SUB)
        cat_goal_ref[rows] = picked(cat_all_ref[rows, there], index)
    day_goal = jnp.where(lane // width == row, picked(day_all_ref[:, there], index), 0.0)
    line_ref[2:3] = jnp.sum(day_goal, axis=0, keepdims=True)


def margin_kernel(back_ref, wide_ref, slot_ref, widen_ref, out_ref, tiles_ref):
    count = wide_ref.shape[1] // LANES
    day = back_ref[pl.ds(0, count, stride=2), :]
    cat = back_ref[pl.ds(1, count, stride=2), :]
    cat = jnp.dot(jnp.concatenate(two_parts(cat), axis=0), widen_ref[...], preferred_element_type=F32)
    cat = cat[:count] + cat[count:]
    for s in range(SUB):
        here = min(s, SLOTS - 1) * LANES
        tiles_ref[pl.ds(s, count, stride=SUB), :] = cat[:, here : here + LANES] * day
    tiles = [tiles_ref[j * SUB : (j + 1) * SUB] for j in range(count)]
    parts = jnp.concatenate(two_parts(jnp.concatenate(tiles, axis=1)), axis=0)
    sums = lax.dot_general(parts, wide_ref[...], (((1,), (1,)), ((), ())), preferred_element_type=F32)
    sums = sums[:SUB] + sums[SUB:]
    kept = jnp.where(iota((SUB, LANES), 0) == slot_ref[...], sums, 0.0)
    line = jnp.sum(kept, axis=0, keepdims=True)
    out_ref[...] = jnp.broadcast_to(line[None], out_ref.shape)


def pool_kernel(margin_ref, line_ref, wide_ref, slot_ref, out_ref, *factor_out):
    total = jnp.sum(margin_ref[...], axis=0)
    factor = line_ref[0:1] / total
    if factor_out:
        factor_out[0][...] = factor
    row = iota((SUB, LANES), 0)
    weights = jnp.where(row == slot_ref[...], factor, 0.0)
    parts = jnp.concatenate(two_parts(weights), axis=0)
    sums = jnp.dot(parts, wide_ref[...], preferred_element_type=F32)
    sums = sums[:SUB] + sums[SUB:]
    count = wide_ref.shape[1] // LANES
    each = out_ref.shape[0] // count
    base = jnp.broadcast_to(line_ref[1:2], (SUB, LANES))
    for j in range(count):
        tile = sums[:, j * LANES : (j + 1) * LANES]
        if each > SLOTS:
            tile = jnp.where(row == BASE_ROW, base, tile)
        out_ref[j * each : (j + 1) * each] = tile[:each]


def fitted(merged, cat_goal, day_goal, day):
    width = LANES // SUB
    for _ in range(INNER):
        below = merged * day
        turned = [below] + [pltpu.roll(below, n * width, 1) for n in range(1, SUB)]
        while len(turned) > 1:
            turned = [turned[n] + turned[n + 1] for n in range(0, len(turned), 2)]
        cat = cat_goal / turned[0]
        day = day_goal / jnp.sum(merged * cat, axis=0, keepdims=True)
    return cat, day


def summed(across, taken):
    merged = jnp.dot(across, jnp.concatenate(two_parts(taken), axis=1), preferred_element_type=F32)
    return merged[:, :LANES] + merged[:, LANES:]


def answer(choice, cat, day, out_ref):
    group = iota(cat.shape, 1) // (LANES // SUB)
    blocks = [jnp.where(group == s, cat, 0.0) for s in range(choice.shape[1] // cat.shape[0])]
    parts = jnp.concatenate(two_parts(jnp.concatenate(blocks, axis=0)), axis=1)
    rows = jnp.dot(choice, parts, preferred_element_type=F32)
    devices = choice.shape[0]
    out_ref[pl.ds(0, devices, stride=2), :] = jnp.broadcast_to(day, (devices, LANES))
    out_ref[pl.ds(1, devices, stride=2), :] = rows[:, :LANES] + rows[:, LANES:]


def owner_first_kernel(taken_ref, cat_goal_ref, line_ref, out_ref, day_ref, place_ref, across_ref):
    cats = cat_goal_ref.shape[0]
    each = SLOTS + 1
    devices = taken_ref.shape[0] // each
    base = taken_ref[pl.ds(BASE_ROW, devices, stride=each), :]

    def placed(each):
        rows = devices * each
        at = iota((rows, devices), 0) - iota((rows, devices), 1) * each
        own = (at >= 0) & (at < each)
        spread = jnp.dot(own.astype(F32).astype(BF16), base.astype(BF16), preferred_element_type=F32)
        slot = jnp.sum(jnp.where(own, at, 0), axis=1, keepdims=True)
        lane = iota((rows, LANES), 1)
        hit = (spread.astype(jnp.int32) + slot == lane % cats) & (slot < SLOTS)
        return hit.astype(F32)

    across_ref[...] = placed(SLOTS).T[:cats].astype(BF16)
    lane = iota((devices, LANES), 1)
    for n in range(place_ref.shape[1] // LANES):
        slot = n * (LANES // cats) + lane // cats
        hit = (base.astype(jnp.int32) + slot == lane % cats) & (slot < SLOTS)
        place_ref[:, n * LANES : (n + 1) * LANES] = hit.astype(F32).astype(BF16)
    merged = summed(placed(each).T[:cats].astype(BF16), taken_ref[...])
    cat, day = fitted(merged, cat_goal_ref[...], line_ref[2:3], jnp.ones((1, LANES), F32))
    day_ref[...] = day
    answer(place_ref[...], cat, day, out_ref)


def owner_kernel(taken_ref, cat_goal_ref, line_ref, day_ref, place_ref, across_ref, out_ref, day_out_ref):
    merged = summed(across_ref[...], taken_ref[...])
    cat, day = fitted(merged, cat_goal_ref[...], line_ref[2:3], day_ref[...])
    day_out_ref[...] = day
    answer(place_ref[...], cat, day, out_ref)


def owner_last_kernel(taken_ref, cat_goal_ref, line_ref, day_ref, across_ref, out_ref):
    merged = summed(across_ref[...], taken_ref[...])
    cat, day = fitted(merged, cat_goal_ref[...], line_ref[2:3], day_ref[...])
    group = iota((SUB, LANES), 1) // (LANES // SUB)
    tile = cat[:SUB]
    for d in range(1, SUB):
        tile = jnp.where(group == d, cat[d * SUB : (d + 1) * SUB], tile)
    both = jnp.concatenate([tile, day], axis=0)
    each = both.shape[0]
    for j in range(out_ref.shape[0] // each):
        out_ref[j * each : (j + 1) * each] = both


def closing_kernel(
    group_vmem, factor_vmem, back_ref, x_ref, factor_hbm, cat_hbm, day_hbm, out_hbm,
    group_ref, factor_ref, cat_ref, day_ref, scale_ref, buf_ref, sems, out_sems,
):
    items, _, stores = x_ref.shape
    loads = [
        pltpu.make_async_copy(group_vmem, group_ref, sems.at[0]),
        pltpu.make_async_copy(factor_vmem, factor_ref, sems.at[1]),
    ]
    for copy in loads:
        copy.start()
    each = SUB + 1
    for t in range(stores // LANES):
        here = slice(t * LANES, (t + 1) * LANES)
        tiles = swap_blocks([back_ref[(t * SUB + j) * each : (t * SUB + j) * each + SUB] for j in range(SUB)])
        cat_ref[:, here] = jnp.concatenate(tiles, axis=0)
        day_ref[:, here] = swap_within(back_ref[pl.ds(t * SUB * each + SUB, SUB, stride=each), :])
    stores_out = [
        pltpu.make_async_copy(factor_vmem, factor_hbm, sems.at[4]),
        pltpu.make_async_copy(cat_ref, cat_hbm, sems.at[2]),
        pltpu.make_async_copy(day_ref, day_hbm, sems.at[3]),
    ]
    for copy in stores_out:
        copy.start()
    for copy in loads:
        copy.wait()
    first = group_ref[0, 0]
    last = cat_ref.shape[0] - 1
    for s in range(SLOTS):
        scale_ref[s] = cat_ref[pl.ds(jnp.minimum(first + s, last), 1), :] * day_ref[...]
    chunks = out_sems.shape[0]
    block = items // chunks
    for n in range(chunks):
        for i in range(n * block, (n + 1) * block):
            value = x_ref[i].astype(F32) * factor_ref[0, i] * scale_ref[group_ref[0, i] - first]
            buf_ref[i] = value.astype(BF16)
        rows = pl.ds(n * block, block)
        copy = pltpu.make_async_copy(buf_ref.at[rows], out_hbm.at[rows], out_sems.at[n])
        copy.start()
        stores_out.append(copy)
    for copy in stores_out:
        copy.wait()


def vmem(count):
    return [pl.BlockSpec(memory_space=pltpu.VMEM)] * count


def held(x):
    return pltpu.with_memory_space_constraint(x, pltpu.VMEM)


def far(x):
    return pltpu.with_memory_space_constraint(x, pltpu.HBM)


LIMIT = pltpu.CompilerParams(vmem_limit_bytes=8 * 1024 * 1024)


def call(kernel, out_shape, *args, **options):
    return pl.pallas_call(
        kernel,
        out_shape=out_shape,
        in_specs=vmem(len(args)),
        out_specs=tuple(vmem(len(out_shape))),
        compiler_params=LIMIT,
        **options,
    )(*map(held, args))


def shards(predicted_units, product_group, product_goal, group_outlet_goal, outlet_date_goal):
    items, days, stores = predicted_units.shape
    cats = group_outlet_goal.shape[0]
    owners = lax.axis_size("item")
    beside = lax.axis_size("store")

    def message(each):
        return pltpu.VMEM((owners * each, LANES), F32)

    def exchanged(x):
        sent = x.reshape(owners, 1, x.size // owners)
        there = lax.all_to_all(sent, "item", 0, 0, axis_index_groups=[item_order(owners)], tiled=True)
        return there.reshape(x.shape)

    margin = pltpu.VMEM((beside, 1, LANES), F32)
    line = pltpu.VMEM((1, LANES), F32)
    tile = pltpu.VMEM((SUB, LANES), jnp.int32)
    per_cat = pltpu.VMEM((cats, LANES), F32)

    far_spec = pl.BlockSpec(memory_space=pltpu.HBM)
    (near,) = pl.pallas_call(
        near_kernel,
        out_shape=(pltpu.VMEM(predicted_units.shape, BF16),),
        in_specs=[far_spec],
        out_specs=tuple(vmem(1)),
        scratch_shapes=[pltpu.SemaphoreType.DMA],
        compiler_params=LIMIT,
        name="near",
    )(far(predicted_units))
    (part,) = call(first_kernel, (margin,), near, name="first")
    wide, slot, own, lines, cat_goal, widen = pl.pallas_call(
        spread_kernel,
        out_shape=(
            pltpu.VMEM((items, days * stores), BF16),
            tile,
            pltpu.VMEM((1, items), jnp.int32),
            pltpu.VMEM((SUB, LANES), F32),
            per_cat,
            pltpu.VMEM((LANES, SLOTS * LANES), BF16),
        ),
        in_specs=vmem(1) + [far_spec] * 4,
        out_specs=tuple(vmem(6)),
        scratch_shapes=[
            pltpu.VMEM((items * days * stores // LANES, LANES), F32),
            pltpu.VMEM((1, items), jnp.int32),
            pltpu.VMEM((1, items), F32),
            pltpu.VMEM((cats, stores), F32),
            pltpu.VMEM((days, stores), F32),
            pltpu.SemaphoreType.DMA((4,)),
        ],
        compiler_params=LIMIT,
        name="spread",
    )(
        held(near),
        far(product_group.reshape(1, items)),
        far(product_goal.reshape(1, items)),
        far(group_outlet_goal),
        far(outlet_date_goal),
    )
    for n in range(ROUNDS):
        total = lax.all_to_all(part, "store", 0, 0, axis_index_groups=[store_order(beside)], tiled=True)
        shapes = (message(SLOTS if n else SLOTS + 1),)
        if n == ROUNDS - 1:
            shapes += (line,)
        pooled, *factor = call(pool_kernel, shapes, total, lines, wide, slot, name="pool")
        taken = exchanged(pooled)
        if n == ROUNDS - 1:
            break
        if n == 0:
            shapes = (
                message(2),
                line,
                pltpu.VMEM((owners, -(-SLOTS * cats // LANES) * LANES), BF16),
                pltpu.VMEM((cats, owners * SLOTS), BF16),
            )
            back, day, place, across = call(owner_first_kernel, shapes, taken, cat_goal, lines, name="owner_first")
        else:
            shapes = (message(2), line)
            back, day = call(owner_kernel, shapes, taken, cat_goal, lines, day, place, across, name="owner")
        (part,) = call(
            margin_kernel, (margin,), exchanged(back), wide, slot, widen,
            scratch_shapes=[pltpu.VMEM((owners * SUB, LANES), F32)], name="margin",
        )

    (back,) = call(
        owner_last_kernel, (message(SUB + 1),), taken, cat_goal, lines, day, across, name="owner_last"
    )
    product_factor, group_outlet_factor, outlet_date_factor, adjusted_tensor = pl.pallas_call(
        closing_kernel,
        out_shape=(
            jax.ShapeDtypeStruct((1, items), F32),
            jax.ShapeDtypeStruct((cats, stores), F32),
            jax.ShapeDtypeStruct((days, stores), F32),
            jax.ShapeDtypeStruct((items, days, stores), BF16),
        ),
        in_specs=vmem(4),
        out_specs=(far_spec,) * 4,
        scratch_shapes=[
            pltpu.SMEM((1, items), jnp.int32),
            pltpu.SMEM((1, items), F32),
            pltpu.VMEM((cats, stores), F32),
            pltpu.VMEM((days, stores), F32),
            pltpu.VMEM((SUB, days, stores), F32),
            pltpu.VMEM((items, days, stores), BF16),
            pltpu.SemaphoreType.DMA((5,)),
            pltpu.SemaphoreType.DMA((8,)),
        ],
        compiler_params=LIMIT,
        name="closing",
    )(*map(held, (own, factor[0], exchanged(back), near)))
    return (product_factor.reshape(items), group_outlet_factor, outlet_date_factor, adjusted_tensor)


def solution(mesh):
    in_specs = (P("item", None, "store"), P("item"), P("item"), P(None, "store"), P(None, "store"))
    out_specs = (P("item"), P(None, "store"), P(None, "store"), P("item", None, "store"))
    return jax.shard_map(shards, mesh=mesh, in_specs=in_specs, out_specs=out_specs, check_vma=False)
```
